32 devices in a mesh: grp: 2 (over x), site: 16 (over z, y, core).
Axes of the slice: x: 2, y: 2, z: 4, core: 2. Of those that a mesh axis runs over, the one named last changes fastest.
Arguments:
- vectors: float32 [4, 3, 16, 288, 256], P('grp', None, 'site'), parts along dimension 0, may hold values from -6 to 6
- links: float32 [6, 2, 3, 3, 16, 288], P('grp', None, None, None, 'site'), parts along dimension 0, may hold values from -1 to 1, as said below
- momenta: int32 [4, 3], replicated, may hold values from -2 to 2
- directions: int32 [256], replicated, may hold values from 0 to 2
Outputs:
- meson: float32 [256, 8, 2, 256], P('site', 'grp'), parts along dimension 1
The draws below stay inside these ranges and needn't reach their ends.
There are 2 independent parts, one for each index of `grp`. The reference program is written for one: setup_inputs(seed, part) draws one part's arguments, and reference() takes and returns one part's arrays. A program takes and returns all parts, laid end to end along the dimension named above; an argument that names none is the same for every part. Nothing has to cross between parts.
Inputs may be any that keep to these rules, and one draw needn't show every extreme that they name: Each links[k, :, :, :, t, s] holds the real and imaginary parts of a unitary 3 x 3 matrix.
All inputs are finite; a program needn't handle non-finite values.
Results may differ from the reference program's by a relative error of at most 0.0001.
Values sent between devices are 32-bit elements; how exact they have to be, the bound alone decides.
No kernel may reach another device: no remote copies, remote signals or barrier semaphores. Data moves between devices by JAX's collectives and lax.ppermute only.
A program may use at most 128 MiB of HBM per device.

```python
import math
import jax
import jax.numpy as jnp
from jax import lax

NEV = 256
NMOM = 4
TLX = 12
TLY = 12
LZ = 2
NTX = 4
LX = 48
LY = 48
N_SITE = 16


def draw_links(key, part):
    shape = (3, 2, 3, 3, NTX * NTX, LZ * TLX * TLY)
    raw = jax.random.normal(key, shape, jnp.float32)
    columns = []
    for colour in range(3):
        v_real = raw[:, 0, :, colour]
        v_imag = raw[:, 1, :, colour]
        for q_real, q_imag in columns:
            p_real = jnp.sum(q_real * v_real + q_imag * v_imag, axis=1, keepdims=True)
            p_imag = jnp.sum(q_real * v_imag - q_imag * v_real, axis=1, keepdims=True)
            v_real = v_real - (p_real * q_real - p_imag * q_imag)
            v_imag = v_imag - (p_real * q_imag + p_imag * q_real)
        length = jnp.sqrt(jnp.sum(v_real * v_real + v_imag * v_imag, axis=1, keepdims=True))
        length = jnp.maximum(length, 0.001)
        columns.append((v_real / length, v_imag / length))
    real_part = jnp.stack([c[0] for c in columns], axis=2)
    imag_part = jnp.stack([c[1] for c in columns], axis=2)
    return jnp.stack([real_part, imag_part], axis=1).astype(jnp.float32)


def plant(drawn, stream_key, least, largest):
    shape = drawn.shape
    index_at = [jax.random.randint(jax.random.fold_in(stream_key, axis), (), 0, shape[axis]) for axis in range(len(shape))]
    drawn = drawn.at[tuple(index_at)].set(least)
    longest = shape.index(max(shape))
    index_at[longest] = (index_at[longest] + 1) % shape[longest]
    return drawn.at[tuple(index_at)].set(largest)


def block_levels(own_key, dims, pieces, smallest, top_value):
    factor_of, own = 1.0, jax.random.fold_in(own_key, 6)
    for dim, parts in pieces:
        heights = jnp.exp(jax.random.uniform(jax.random.fold_in(own, dim), (parts,), jnp.float32, smallest / len(pieces), top_value / len(pieces)))
        factor_of = factor_of * jnp.repeat(heights, dims[dim] // parts).reshape([-1 if axis == dim else 1 for axis in range(len(dims))])
    return factor_of


def bell_draw(own_key, extent, scale, most, pieces=(), kind=jnp.bfloat16):
    result = jax.random.normal(own_key, extent, jnp.float32) * scale
    if len(pieces) > 0:
        result = block_levels(own_key, extent, pieces, -0.22, 0.18) * result
    return jnp.clip(result, min=-most, max=most).astype(kind)


def setup_inputs(seed: int = 0, part: int = 0) -> dict:
    key_of = jax.random.split(jax.random.key(seed), 5)
    own_keys = jax.random.split(jax.random.fold_in(key_of[4], part), 5)
    vectors = bell_draw(own_keys[0], (2, 3, N_SITE, LZ * TLX * TLY, NEV), 1.0, 6.0, ((2, 16),), jnp.float32)
    links = draw_links(jax.random.fold_in(jax.random.fold_in(key_of[4], part), 71), part)
    momenta = plant(jax.random.randint(key_of[2], (NMOM, 3), -2, 3), jax.random.fold_in(key_of[2], 1), -2, 2).astype(jnp.int32)
    directions = plant(jax.random.randint(key_of[3], (NEV,), 0, 3), jax.random.fold_in(key_of[3], 1), 0, 2).astype(jnp.int32)
    return {"vectors": vectors, "links": links, "momenta": momenta, "directions": directions}


kappa = 0.08

def to_lattice(arr, tiles, planes, tile_x, tile_y, trailing):
    count = arr.ndim - 2 - trailing
    lead = arr.shape[:count]
    trail = arr.shape[count + 2:]
    grid = arr.reshape(lead + (tiles, tiles, planes, tile_x, tile_y) + trail)
    order = tuple(range(count)) + (count + 2, count, count + 3, count + 1, count + 4)
    order = order + tuple(range(count + 5, count + 5 + trailing))
    grid = jnp.transpose(grid, order)
    return grid.reshape(lead + (planes, tiles * tile_x, tiles * tile_y) + trail)

def mat_apply(link_k, field):
    real_part = 0.0
    imag_part = 0.0
    for colour in range(3):
        u_real = link_k[0, :, colour][..., None]
        u_imag = link_k[1, :, colour][..., None]
        f_real = field[0, colour][None]
        f_imag = field[1, colour][None]
        real_part = real_part + u_real * f_real - u_imag * f_imag
        imag_part = imag_part + u_real * f_imag + u_imag * f_real
    return jnp.stack([real_part, imag_part])

def adj_apply(link_k, field):
    real_part = 0.0
    imag_part = 0.0
    for colour in range(3):
        u_real = link_k[0, colour][..., None]
        u_imag = link_k[1, colour][..., None]
        f_real = field[0, colour][None]
        f_imag = field[1, colour][None]
        real_part = real_part + u_real * f_real + u_imag * f_imag
        imag_part = imag_part + u_real * f_imag - u_imag * f_real
    return jnp.stack([real_part, imag_part])

def next_y(field):
    rolled = jnp.roll(field, -1, -2)
    edge = jnp.roll(field[..., 0, :], -TLX, -2)
    return jnp.concatenate([rolled[..., :-1, :], edge[..., None, :]], axis=-2)

def prev_y(field):
    rolled = jnp.roll(field, 1, -2)
    edge = jnp.roll(field[..., -1, :], TLX, -2)
    return jnp.concatenate([edge[..., None, :], rolled[..., 1:, :]], axis=-2)

def hop_terms(field, links, sign):
    terms = []
    forward = mat_apply(links[0], jnp.roll(field, -1, -3))
    backward = jnp.roll(adj_apply(links[0], field), 1, -3)
    terms.append(forward + sign * backward)
    forward = mat_apply(links[1], next_y(field))
    backward = prev_y(adj_apply(links[1], field))
    terms.append(forward + sign * backward)
    forward = mat_apply(links[2], jnp.roll(field, -1, -4))
    backward = jnp.roll(adj_apply(links[2], field), 1, -4)
    terms.append(forward + sign * backward)
    return terms

def smear_step(field, links):
    terms = hop_terms(field, links, 1.0)
    return field + kappa * (terms[0] + terms[1] + terms[2] - 6.0 * field)

def displace(field, links, masks):
    terms = hop_terms(field, links, -1.0)
    total = 0.0
    for which in range(3):
        total = total + masks[which][None, None, None, None, None, :] * terms[which]
    return total

def meson_fields(left_field, shifted, momenta, xs, ys, zs, lx, ly, planes, scale):
    nev = left_field.shape[-1]
    flat_v = left_field.reshape((2, 3, -1, nev))
    flat_s = shifted.reshape((2, 3, -1, nev))
    blocks = []
    for moment in range(momenta.shape[0]):
        frac = (momenta[moment, 0] * xs % lx).astype(jnp.float32) / lx
        frac = frac + (momenta[moment, 1] * ys % ly).astype(jnp.float32) / ly
        frac = frac + (momenta[moment, 2] * zs % planes).astype(jnp.float32) / planes
        theta = (2.0 * math.pi * frac).reshape(-1)
        cosine = jnp.cos(theta)[:, None]
        sine = jnp.sin(theta)[:, None]
        a_real = cosine * flat_v[0] - sine * flat_v[1]
        a_imag = -(sine * flat_v[0] + cosine * flat_v[1])
        left = jnp.stack([a_real, a_imag])
        prods = jnp.einsum('acsn,bcsm->anbm', left, flat_s, precision=lax.Precision.HIGHEST)
        re_block = prods[0, :, 0] - prods[1, :, 1]
        im_block = prods[0, :, 1] + prods[1, :, 0]
        blocks.append(jnp.stack([re_block, im_block], axis=1))
    return jnp.stack(blocks, axis=1) * scale

def reference(vectors, links, momenta, directions):
    masks = (directions[None, :] == jnp.arange(3, dtype=jnp.int32)[:, None]).astype(jnp.float32)
    field = to_lattice(vectors, NTX, LZ, TLX, TLY, 1)
    lattice_links = to_lattice(links, NTX, LZ, TLX, TLY, 0)
    once = smear_step(field, lattice_links)
    twice = smear_step(once, lattice_links)
    shifted = displace(twice, lattice_links, masks)
    zs = jnp.arange(LZ, dtype=jnp.int32)[:, None, None]
    xs = jnp.arange(LX, dtype=jnp.int32)[None, :, None]
    ys = jnp.arange(LY, dtype=jnp.int32)[None, None, :]
    scale = 1.0 / math.sqrt(3.0 * LX * LY * LZ)
    return meson_fields(field, shifted, momenta, xs, ys, zs, LX, LY, LZ, scale)
```

```python
import functools
import math

import jax
import jax.numpy as jnp
import numpy as np
from jax import lax
from jax.experimental import pallas as pl
from jax.experimental.pallas import tpu as pltpu
from jax.sharding import PartitionSpec as P

TLX = 12
TLY = 12
LZ = 2
KAPPA = 0.08

LAYER = LZ * TLY
SITES = TLX * LAYER
XROWS = 3 * LAYER
MAIN = TLX * XROWS
PADDED = (TLX + 2) * XROWS
EDGE = 4 * XROWS
HEAD = MAIN // 128 * 128
TAIL = MAIN - HEAD + EDGE
LANES = 128
CX, CY, CZ = 0, 18, 36
CYF, CYB, CZS, CZD = 54, 72, 90, 108
VMEM_LIMIT = 60 * 2**20


def call(kernel, outs, scratch=(), flops=0, moved=0, **kwargs):
    return pl.pallas_call(
        kernel,
        out_shape=outs,
        scratch_shapes=list(scratch),
        compiler_params=pltpu.CompilerParams(vmem_limit_bytes=VMEM_LIMIT),
        cost_estimate=pl.CostEstimate(flops=flops, bytes_accessed=moved, transcendentals=0),
        **kwargs,
    )


def f32(*shape):
    return jax.ShapeDtypeStruct(shape, jnp.float32)


def bf16(*shape):
    return jax.ShapeDtypeStruct(shape, jnp.bfloat16)


def spread(table, column, lanes=LANES):
    return jnp.broadcast_to(table[:, column : column + 1], (table.shape[0], lanes))


def matvec(table, first, field, adjoint=False, acc=None, minus=False):
    out = [[None] * 3, [None] * 3] if acc is None else [list(acc[0]), list(acc[1])]
    lanes = field[0][0].shape[-1]

    def put(part, row, value, negative):
        if negative != minus:
            out[part][row] = -value if out[part][row] is None else out[part][row] - value
        else:
            out[part][row] = value if out[part][row] is None else out[part][row] + value

    for row in range(3):
        for col in range(3):
            at = first + (3 * col + row if adjoint else 3 * row + col)
            real = spread(table, at, lanes)
            imag = spread(table, at + 9, lanes)
            put(0, row, real * field[0][col], False)
            put(0, row, imag * field[1][col], not adjoint)
            put(1, row, real * field[1][col], False)
            put(1, row, imag * field[0][col], adjoint)
    return out


def layer_rows(ref, part, half, first, size=LAYER):
    return ref[part, half, first : first + size, :]


def grid2(load):
    return [[load(part, colour) for colour in range(3)] for part in range(2)]


def y_rows(colour, z, y):
    return pl.ds(XROWS + colour * LAYER + z * TLY + y, TLX, stride=XROWS)


def send_layers(f_ref, wc_ref, xlo_ref, xhi_ref, ylo_ref, yhi_ref):
    last = TLX * XROWS
    for half in range(f_ref.shape[1]):
        for part in range(2):
            xlo_ref[part, half] = f_ref[part, half, XROWS : 2 * XROWS, :]
            for colour in range(3):
                for z in range(LZ):
                    to = colour * LAYER + z * TLX
                    ylo_ref[part, half, to : to + TLX, :] = f_ref[part, half, y_rows(colour, z, 0), :]
        table = wc_ref[TLX * LAYER : (TLX + 1) * LAYER, :]
        hop = matvec(table, CX, grid2(lambda p, c: layer_rows(f_ref, p, half, last + c * LAYER)), adjoint=True)
        for part in range(2):
            for colour in range(3):
                xhi_ref[part, half, colour * LAYER : (colour + 1) * LAYER, :] = hop[part][colour]
        for z in range(LZ):
            table = wc_ref[pl.ds(LAYER + z * TLY + TLY - 1, TLX, stride=LAYER), :]
            hop = matvec(table, CY, grid2(lambda p, c: f_ref[p, half, y_rows(c, z, TLY - 1), :]), adjoint=True)
            for part in range(2):
                for colour in range(3):
                    to = colour * LAYER + z * TLX
                    yhi_ref[part, half, to : to + TLX, :] = hop[part][colour]


def clear_ends(ref):
    for part in range(2):
        for half in range(ref.shape[1]):
            ref[part, half, 0:XROWS, :] = jnp.zeros((XROWS, LANES), jnp.float32)
            ref[part, half, PADDED - XROWS : PADDED, :] = jnp.zeros((XROWS, LANES), jnp.float32)


def pack_kernel(v_ref, l_ref, fr_ref, wc_ref, xlo_ref, xhi_ref, ylo_ref, yhi_ref, la, lb, ta, tb):
    la[...] = jnp.zeros_like(la)
    lb[...] = jnp.zeros_like(lb)
    plane = SITES // LZ
    la[0:54, 0:SITES] = l_ref[...]
    la[CYF : CYF + 18, 0:SITES] = l_ref[CY : CY + 18, :]
    la[CYB : CYB + 18, 0:SITES] = l_ref[CY : CY + 18, :]
    la[CZS : CZS + 18, 0:SITES] = l_ref[CZ : CZ + 18, :]
    la[CZD : CZD + 18, 0:SITES] = l_ref[CZ : CZ + 18, :]
    for part in range(2):
        for row in range(3):
            for col in range(3):
                k = 9 * part + 3 * row + col
                kt = CZ + 9 * part + 3 * col + row
                value = l_ref[kt : kt + 1, :]
                sign = 1.0 if part == 0 else -1.0
                lb[CZS + k : CZS + k + 1, 0:SITES] = sign * value
                lb[CZD + k : CZD + k + 1, 0:SITES] = -sign * value
    ta[...] = jnp.transpose(la[...])
    tb[...] = jnp.transpose(lb[...])
    raw = ta[0:SITES, :]
    other = jnp.concatenate([tb[plane:SITES, :], tb[0:plane, :]], axis=0)
    y = lax.broadcasted_iota(jnp.int32, (SITES, LANES), 0) % TLY
    column = lax.broadcasted_iota(jnp.int32, (SITES, LANES), 1)
    back = pltpu.roll(raw, 1, 0)
    is_yf = (column >= CYF) & (column < CYB)
    is_yb = (column >= CYB) & (column < CZS)
    table = jnp.where(is_yb, back, raw)
    gone = (is_yf & (y == TLY - 1)) | (is_yb & (y == 0))
    ta[0:SITES, :] = jnp.where(gone, 0.0, table) + other
    wc_ref[0:LAYER, :] = jnp.zeros((LAYER, LANES), jnp.float32)
    clear_ends(fr_ref)
    for x in range(TLX):
        for z in range(LZ):
            src = z * plane + x * TLY
            dst = (x + 1) * LAYER + z * TLY
            wc_ref[dst : dst + TLY, :] = ta[src : src + TLY, :]
            for half in range(fr_ref.shape[1]):
                for part in range(2):
                    for colour in range(3):
                        dst = (x + 1) * XROWS + colour * LAYER + z * TLY
                        fr_ref[part, half, dst : dst + TLY, :] = v_ref[
                            3 * part + colour, src : src + TLY, half * LANES : (half + 1) * LANES
                        ]
    send_layers(fr_ref, wc_ref, xlo_ref, xhi_ref, ylo_ref, yhi_ref)


def roll_layer(f_ref, half, base, rolled):
    for part in range(2):
        for colour in range(3):
            rows = f_ref[part, half, pl.ds(base + colour * LAYER, LAYER), :]
            at = colour * LAYER
            rolled[0, half, part, at : at + LAYER, :] = pltpu.roll(rows, LAYER - 1, 0)
            rolled[1, half, part, at : at + LAYER, :] = pltpu.roll(rows, 1, 0)
            rolled[2, half, part, at : at + LAYER, :] = pltpu.roll(rows, TLY, 0)


def layer_hops(f_ref, wc_ref, rolled, half, x, tile, z_column):
    base = pl.multiple_of((x + 1) * XROWS, 8)
    table = wc_ref[pl.ds(pl.multiple_of((x + 1) * LAYER, 8) + 8 * tile, 8), :]
    below = wc_ref[pl.ds(pl.multiple_of(x * LAYER, 8) + 8 * tile, 8), :]

    def straight(shift):
        return lambda p, c: f_ref[p, half, pl.ds(base + shift + c * LAYER + 8 * tile, 8), :]

    def turned(which):
        return lambda p, c: rolled[which, half, p, c * LAYER + 8 * tile : c * LAYER + 8 * tile + 8, :]

    return (
        (table, CX, straight(XROWS), False, 0),
        (below, CX, straight(-XROWS), True, 0),
        (table, CYF, turned(0), False, 1),
        (table, CYB, turned(1), True, 1),
        (table, z_column, turned(2), False, 2),
    ), straight(0)


def smear_kernel(f_ref, wc_ref, out_ref, rolled):
    clear_ends(out_ref)

    def layer(x, carry):
        base = pl.multiple_of((x + 1) * XROWS, 8)
        for half in range(f_ref.shape[1]):
            roll_layer(f_ref, half, base, rolled)
        for tile in range(LAYER // 8):
            for half in range(f_ref.shape[1]):
                hops, here = layer_hops(f_ref, wc_ref, rolled, half, x, tile, CZS)
                acc = None
                for weights, column, load, adjoint, _ in hops:
                    acc = matvec(weights, column, grid2(load), adjoint, acc)
                for part in range(2):
                    for colour in range(3):
                        value = (1.0 - 6.0 * KAPPA) * here(part, colour) + KAPPA * acc[part][colour]
                        out_ref[part, half, pl.ds(base + colour * LAYER + 8 * tile, 8), :] = value
        return carry

    lax.fori_loop(0, TLX, layer, 0)


def cross(once_ref, wc_ref, rxlo, rxhi, rylo, ryhi, save=None):
    last = TLX * XROWS
    for half in range(once_ref.shape[1]):
        table = wc_ref[TLX * LAYER : (TLX + 1) * LAYER, :]
        hop_x = matvec(table, CX, grid2(lambda p, c: layer_rows(rxhi, p, half, c * LAYER)))
        hop_y = []
        for z in range(LZ):
            table = wc_ref[pl.ds(LAYER + z * TLY + TLY - 1, TLX, stride=LAYER), :]
            hop_y.append(matvec(table, CY, grid2(lambda p, c: layer_rows(ryhi, p, half, c * LAYER + z * TLX, TLX))))
        for part in range(2):
            for colour in range(3):
                at = colour * LAYER
                low = layer_rows(rxlo, part, half, at)
                once_ref[part, half, XROWS + at : XROWS + at + LAYER, :] += KAPPA * low
                once_ref[part, half, last + at : last + at + LAYER, :] += KAPPA * hop_x[part][colour]
                if save is not None:
                    save[part, half, at : at + LAYER, :] = low
                    save[part, half, XROWS + at : XROWS + at + LAYER, :] = hop_x[part][colour]
                for z in range(LZ):
                    low = layer_rows(rylo, part, half, at + z * TLX, TLX)
                    rows = y_rows(colour, z, 0)
                    once_ref[part, half, rows, :] = once_ref[part, half, rows, :] + KAPPA * low
                    rows = y_rows(colour, z, TLY - 1)
                    once_ref[part, half, rows, :] = once_ref[part, half, rows, :] + KAPPA * hop_y[z][part][colour]
                    if save is not None:
                        to = 2 * XROWS + at + z * TLX
                        save[part, half, to : to + TLX, :] = low
                        save[part, half, to + XROWS : to + XROWS + TLX, :] = hop_y[z][part][colour]


def edge_kernel(part_ref, wc_ref, rxlo, rxhi, rylo, ryhi, once_ref, save, xlo_ref, xhi_ref, ylo_ref, yhi_ref):
    once_ref[...] = part_ref[...]
    cross(once_ref, wc_ref, rxlo, rxhi, rylo, ryhi, save)
    send_layers(once_ref, wc_ref, xlo_ref, xhi_ref, ylo_ref, yhi_ref)


def split(value):
    high = value.astype(jnp.bfloat16)
    return high, (value - high.astype(jnp.float32)).astype(jnp.bfloat16)


def phased(real, imag, half, lane, at, size, cos_ref, sin_ref, ah_ref, al_ref):
    real, imag = jnp.transpose(real), jnp.transpose(imag)
    halves = ah_ref.shape[0] // cos_ref.shape[0] // LANES
    for m in range(cos_ref.shape[0]):
        cosine = jnp.broadcast_to(cos_ref[m : m + 1, lane : lane + LANES], (LANES, LANES))
        sine = jnp.broadcast_to(sin_ref[m : m + 1, lane : lane + LANES], (LANES, LANES))
        row = (m * halves + half) * LANES
        high, low = split(cosine * real - sine * imag)
        ah_ref[row : row + LANES, at : at + LANES] = high
        al_ref[row : row + LANES, at : at + LANES] = low
        high, low = split(sine * real + cosine * imag)
        ah_ref[row : row + LANES, size + at : size + at + LANES] = high
        al_ref[row : row + LANES, size + at : size + at + LANES] = low


def head_kernel(fr_ref, cos_ref, sin_ref, ah_ref, al_ref):
    for half in range(fr_ref.shape[1]):
        for at in range(0, HEAD, LANES):
            real, imag = (fr_ref[p, half, XROWS + at : XROWS + at + LANES, :] for p in range(2))
            phased(real, imag, half, at, at, HEAD, cos_ref, sin_ref, ah_ref, al_ref)


def tail_kernel(fr_ref, save, cos_ref, sin_ref, ah_ref, al_ref, rows):
    for half in range(fr_ref.shape[1]):
        for part in range(2):
            rows[part, 0 : MAIN - HEAD, :] = fr_ref[part, half, XROWS + HEAD : XROWS + MAIN, :]
            rows[part, MAIN - HEAD : TAIL, :] = save[part, half]
        for at in range(0, TAIL, LANES):
            real, imag = (rows[p, at : at + LANES, :] for p in range(2))
            phased(real, imag, half, HEAD + at, at, TAIL, cos_ref, sin_ref, ah_ref, al_ref)


def displace_kernel(part_ref, wc_ref, rxlo, rxhi, rylo, ryhi, mask_ref, sh_ref, sl_ref, th_ref, tl_ref, twice, shift, rolled):
    twice[...] = part_ref[...]
    cross(twice, wc_ref, rxlo, rxhi, rylo, ryhi)
    halves = range(twice.shape[1])

    def layer(x, carry):
        into = pl.multiple_of(x * XROWS, 8)
        for half in halves:
            roll_layer(twice, half, pl.multiple_of((x + 1) * XROWS, 8), rolled)
        for tile in range(LAYER // 8):
            for half in halves:
                hops, _ = layer_hops(twice, wc_ref, rolled, half, x, tile, CZD)
                total = None
                for which in range(3):
                    acc = None
                    for weights, column, load, adjoint, direction in hops:
                        if direction == which:
                            acc = matvec(weights, column, grid2(load), adjoint, acc, adjoint)
                    lanes = slice(half * LANES, (half + 1) * LANES)
                    mask = jnp.broadcast_to(mask_ref[which : which + 1, lanes], (8, LANES))
                    acc = [[mask * a for a in row] for row in acc]
                    total = acc if total is None else [[t + a for t, a in zip(*rows)] for rows in zip(total, acc)]
                for part in range(2):
                    for colour in range(3):
                        shift[part, half, pl.ds(into + colour * LAYER + 8 * tile, 8), :] = total[part][colour]
        return carry

    lax.fori_loop(0, TLX, layer, 0)
    last = TLX * XROWS
    for half in halves:
        lanes = slice(half * LANES, (half + 1) * LANES)
        mask_x = jnp.broadcast_to(mask_ref[0:1, lanes], (XROWS, LANES))
        mask_y = jnp.broadcast_to(mask_ref[1:2, lanes], (TLX, LANES))
        for part in range(2):
            shift[part, half, MAIN : MAIN + XROWS, :] = mask_x * twice[part, half, XROWS : 2 * XROWS, :]
            shift[part, half, MAIN + XROWS : MAIN + 2 * XROWS, :] = -mask_x * twice[part, half, last : last + XROWS, :]
            for colour in range(3):
                for z in range(LZ):
                    to = MAIN + 2 * XROWS + colour * LAYER + z * TLX
                    shift[part, half, to : to + TLX, :] = mask_y * twice[part, half, y_rows(colour, z, 0), :]
                    to += XROWS
                    shift[part, half, to : to + TLX, :] = -mask_y * twice[part, half, y_rows(colour, z, TLY - 1), :]
    width = len(halves) * LANES
    for high_ref, low_ref, first, size in ((sh_ref, sl_ref, 0, HEAD), (th_ref, tl_ref, HEAD, TAIL)):
        for half in halves:
            real = slice(half * LANES, (half + 1) * LANES)
            imag = slice(width + half * LANES, width + (half + 1) * LANES)
            for row in range(0, size, 128):
                top = slice(row, row + 128)
                bottom = slice(size + row, size + row + 128)
                high, low = split(shift[0, half, first + row : first + row + 128, :])
                high_ref[top, real] = high
                low_ref[top, real] = low
                high_ref[bottom, imag] = -high
                low_ref[bottom, imag] = -low
                high, low = split(shift[1, half, first + row : first + row + 128, :])
                high_ref[bottom, real] = high
                low_ref[bottom, real] = low
                high_ref[top, imag] = high
                low_ref[top, imag] = low


def dot(a, b):
    return jnp.dot(a, b, preferred_element_type=jnp.float32)


def meson_kernel(ah, al, bh, bl, sh, sl, th, tl, out_ref):
    total = dot(ah[...], sh[...]) + dot(ah[...], sl[...]) + dot(al[...], sh[...])
    out_ref[...] = total + dot(bh[...], th[...]) + dot(bh[...], tl[...]) + dot(bl[...], th[...])


def phases(momenta, position, devices, tiles):
    site = np.arange(SITES)
    x, zy = site // LAYER, site % LAYER
    own = [np.repeat(a.reshape(TLX, 1, LAYER), 3, 1).reshape(-1) for a in (x, zy % TLY, zy // TLY)]
    edge = np.arange(LAYER)
    full = np.full(LAYER, 0)
    edges = (
        (full + TLX - 1, edge % TLY, edge // TLY),
        (full, edge % TLY, edge // TLY),
        (edge % TLX, full + TLY - 1, edge // TLX),
        (edge % TLX, full, edge // TLX),
    )
    steps = (-tiles, tiles, -1, 1)
    xs, ys, zs, move = own[0], own[1], own[2], np.zeros(MAIN, np.int64)
    for step, (ex, ey, ez) in zip(steps, edges):
        xs = np.concatenate([xs] + [ex] * 3)
        ys = np.concatenate([ys] + [ey] * 3)
        zs = np.concatenate([zs] + [ez] * 3)
        move = np.concatenate([move, np.full(XROWS, step)])
    tile = (position + jnp.asarray(move, jnp.int32) + devices) % devices
    lx, ly = TLX * tiles, TLY * tiles
    sx = (tile // tiles) * TLX + jnp.asarray(xs, jnp.int32)
    sy = (tile % tiles) * TLY + jnp.asarray(ys, jnp.int32)
    sz = jnp.asarray(zs, jnp.int32)
    frac = (momenta[:, 0:1] * sx % lx).astype(jnp.float32) / lx
    frac = frac + (momenta[:, 1:2] * sy % ly).astype(jnp.float32) / ly
    frac = frac + (momenta[:, 2:3] * sz % LZ).astype(jnp.float32) / LZ
    theta = 2.0 * math.pi * frac
    return jnp.cos(theta), jnp.sin(theta)


def send(block, devices, distance):
    return lax.ppermute(block, "site", [(i, (i + distance) % devices) for i in range(devices)])


def halo(sends, devices, tiles):
    xlo, xhi, ylo, yhi = sends
    return (
        send(xhi, devices, tiles),
        send(xlo, devices, -tiles),
        send(yhi, devices, 1),
        send(ylo, devices, -1),
    )


def stages(devices):
    found, stride = [], 1
    while stride < devices:
        left = devices // stride
        size = 2 if stride < 4 else 4 if left % 4 == 0 else 2
        found.append((stride, size))
        stride *= size
    return found


def scatter_sum(block, position, devices):
    shape = block.shape[1:]
    for stride, size in stages(devices):
        left = block.shape[0] // size
        block = block.reshape((left, size) + shape)
        mine = (position // stride) % size
        total = lax.dynamic_index_in_dim(block, mine, 1, keepdims=False)
        for step in range(1, size):
            other = (mine + step) % size
            out = lax.dynamic_index_in_dim(block, other, 1, keepdims=False)
            route = []
            for i in range(devices):
                digit = (i // stride) % size
                route.append((i, i + ((digit + step) % size - digit) * stride))
            total = total + lax.ppermute(out, "site", route)
        block = total
    return block[0]


def on_device(vectors, links, momenta, directions):
    devices = lax.axis_size("site")
    tiles = math.isqrt(devices)
    position = lax.axis_index("site")
    nev = vectors.shape[-1]
    moments = momenta.shape[0]
    field = vectors.reshape(6, SITES, nev)
    table = links.reshape(54, SITES)
    halves = nev // LANES
    layer = f32(2, halves, XROWS, LANES)
    padded = f32(2, halves, PADDED, LANES)
    fr, wc, *sends = call(
        pack_kernel,
        (padded, f32((TLX + 1) * LAYER, LANES), layer, layer, layer, layer),
        [pltpu.VMEM((128, 384), jnp.float32)] * 2 + [pltpu.VMEM((384, 128), jnp.float32)] * 2,
    )(field, table)
    received = halo(sends, devices, tiles)
    rolled = pltpu.VMEM((3, halves, 2, XROWS, LANES), jnp.float32)
    flops = 2 * 180 * 2 * SITES * nev
    once = call(smear_kernel, padded, [rolled], flops, 3 << 20)(fr, wc)
    cosine, sine = phases(momenta, position, devices, tiles)
    head = bf16(moments * nev, 2 * HEAD)
    tail = bf16(moments * nev, 2 * TAIL)
    ah, al = call(head_kernel, (head, head), flops=flops, moved=8 << 20)(fr, cosine, sine)
    once, save, *sends = call(edge_kernel, (padded, f32(2, halves, EDGE, LANES), layer, layer, layer, layer))(
        once, wc, *received
    )
    received = halo(sends, devices, tiles)
    twice = call(smear_kernel, padded, [rolled], flops, 3 << 20)(once, wc)
    rows = pltpu.VMEM((2, TAIL, LANES), jnp.float32)
    bh, bl = call(tail_kernel, (tail, tail), [rows], flops=flops, moved=4 << 20)(fr, save, cosine, sine)
    scale = 1.0 / math.sqrt(3.0 * TLX * tiles * TLY * tiles * LZ)
    which = jnp.arange(3, dtype=jnp.int32)[:, None]
    masks = jnp.where(directions[None, :] == which, jnp.float32(scale), jnp.float32(0.0))
    sh, sl, th, tl = call(
        displace_kernel,
        (bf16(2 * HEAD, 2 * nev), bf16(2 * HEAD, 2 * nev), bf16(2 * TAIL, 2 * nev), bf16(2 * TAIL, 2 * nev)),
        [
            pltpu.VMEM((2, halves, PADDED, LANES), jnp.float32),
            pltpu.VMEM((2, halves, HEAD + TAIL, LANES), jnp.float32),
            rolled,
        ],
    )(twice, wc, *received, masks)
    whole = lambda a: pl.BlockSpec(a.shape, lambda m: (0, 0))
    partial = pl.pallas_call(
        meson_kernel,
        out_shape=f32(nev, moments * 2 * nev),
        grid=(moments,),
        in_specs=[pl.BlockSpec((nev, 2 * HEAD), lambda m: (m, 0))] * 2
        + [pl.BlockSpec((nev, 2 * TAIL), lambda m: (m, 0))] * 2
        + [whole(sh), whole(sl), whole(th), whole(tl)],
        out_specs=pl.BlockSpec((nev, 2 * nev), lambda m: (0, m)),
        compiler_params=pltpu.CompilerParams(vmem_limit_bytes=VMEM_LIMIT),
    )(ah, al, bh, bl, sh, sl, th, tl)
    total = scatter_sum(partial.reshape(devices, nev // devices, moments * 2 * nev), position, devices)
    return total.reshape(nev // devices, moments, 2, nev)


def solution(mesh):
    placed = (
        P("grp", None, "site", None, None),
        P("grp", None, None, None, "site", None),
        P(),
        P(),
    )
    return jax.shard_map(
        on_device,
        mesh=mesh,
        in_specs=placed,
        out_specs=P("site", "grp", None, None),
        check_vma=False,
    )
```

```python
import functools
import math

import jax
import jax.numpy as jnp
import numpy as np
from jax import lax
from jax.experimental import pallas as pl
from jax.experimental.pallas import tpu as pltpu
from jax.sharding import PartitionSpec as P

TLX = 12
TLY = 12
LZ = 2
KAPPA = 0.08

LAYER = LZ * TLY
SITES = TLX * LAYER
XROWS = 3 * LAYER
MAIN = TLX * XROWS
PADDED = (TLX + 2) * XROWS
EDGE = 4 * XROWS
HEAD = MAIN // 128 * 128
TAIL = MAIN - HEAD + EDGE
LANES = 128
BX, BYF, BYB, BZS, BZD, WIDE = 0, 18, 36, 54, 72, 90
CX, CY, CZ = 0, 18, 36
CYF, CYB, CZS, CZD = 54, 72, 90, 108
VMEM_LIMIT = 12 * 2**20


def call(kernel, outs, scratch=(), flops=0, moved=0, inputs=1, **kwargs):
    on_chip = pl.BlockSpec(memory_space=pltpu.VMEM)
    return pl.pallas_call(
        kernel,
        out_shape=outs,
        in_specs=[on_chip] * inputs,
        out_specs=jax.tree.map(lambda _: on_chip, outs),
        scratch_shapes=list(scratch),
        compiler_params=pltpu.CompilerParams(vmem_limit_bytes=VMEM_LIMIT),
        cost_estimate=pl.CostEstimate(flops=flops, bytes_accessed=moved, transcendentals=0),
        **kwargs,
    )


def f32(*shape):
    return jax.ShapeDtypeStruct(shape, jnp.float32)


def bf16(*shape):
    return jax.ShapeDtypeStruct(shape, jnp.bfloat16)


def spread(table, column, lanes=LANES):
    return jnp.broadcast_to(table[:, column : column + 1], (table.shape[0], lanes))


def matvec(table, first, field, adjoint=False, acc=None, minus=False):
    out = [[None] * 3, [None] * 3] if acc is None else [list(acc[0]), list(acc[1])]
    lanes = field[0][0].shape[-1]

    def put(part, row, value, negative):
        if negative != minus:
            out[part][row] = -value if out[part][row] is None else out[part][row] - value
        else:
            out[part][row] = value if out[part][row] is None else out[part][row] + value

    for row in range(3):
        for col in range(3):
            at = first + (3 * col + row if adjoint else 3 * row + col)
            real = spread(table, at, lanes)
            imag = spread(table, at + 9, lanes)
            put(0, row, real * field[0][col], False)
            put(0, row, imag * field[1][col], not adjoint)
            put(1, row, real * field[1][col], False)
            put(1, row, imag * field[0][col], adjoint)
    return out


def layer_rows(ref, part, half, first, size=LAYER):
    return ref[part, half, first : first + size, :]


def grid2(load):
    return [[load(part, colour) for colour in range(3)] for part in range(2)]


def y_rows(colour, z, y):
    return pl.ds(XROWS + colour * LAYER + z * TLY + y, TLX, stride=XROWS)


def send_layers(f_ref, wc_ref, xlo_ref, xhi_ref, ylo_ref, yhi_ref):
    last = TLX * XROWS
    for half in range(f_ref.shape[1]):
        for part in range(2):
            xlo_ref[part, half] = f_ref[part, half, XROWS : 2 * XROWS, :]
            for colour in range(3):
                for z in range(LZ):
                    to = colour * LAYER + z * TLX
                    ylo_ref[part, half, to : to + TLX, :] = f_ref[part, half, y_rows(colour, z, 0), :]
        table = wc_ref[TLX * LAYER : (TLX + 1) * LAYER, :]
        hop = matvec(table, CX, grid2(lambda p, c: layer_rows(f_ref, p, half, last + c * LAYER)), adjoint=True)
        for part in range(2):
            for colour in range(3):
                xhi_ref[part, half, colour * LAYER : (colour + 1) * LAYER, :] = hop[part][colour]
        for z in range(LZ):
            table = wc_ref[pl.ds(LAYER + z * TLY + TLY - 1, TLX, stride=LAYER), :]
            hop = matvec(table, CY, grid2(lambda p, c: f_ref[p, half, y_rows(c, z, TLY - 1), :]), adjoint=True)
            for part in range(2):
                for colour in range(3):
                    to = colour * LAYER + z * TLX
                    yhi_ref[part, half, to : to + TLX, :] = hop[part][colour]


def clear_ends(ref):
    for part in range(2):
        for half in range(ref.shape[1]):
            ref[part, half, 0:XROWS, :] = jnp.zeros((XROWS, LANES), jnp.float32)
            ref[part, half, PADDED - XROWS : PADDED, :] = jnp.zeros((XROWS, LANES), jnp.float32)


def pack_kernel(v_ref, l_ref, fr_ref, wc_ref, xlo_ref, xhi_ref, ylo_ref, yhi_ref, la, lb, ta, tb):
    la[...] = jnp.zeros_like(la)
    lb[...] = jnp.zeros_like(lb)
    plane = SITES // LZ
    la[0:54, 0:SITES] = l_ref[...]
    la[CYF : CYF + 18, 0:SITES] = l_ref[CY : CY + 18, :]
    la[CYB : CYB + 18, 0:SITES] = l_ref[CY : CY + 18, :]
    la[CZS : CZS + 18, 0:SITES] = l_ref[CZ : CZ + 18, :]
    la[CZD : CZD + 18, 0:SITES] = l_ref[CZ : CZ + 18, :]
    for part in range(2):
        for row in range(3):
            for col in range(3):
                k = 9 * part + 3 * row + col
                kt = CZ + 9 * part + 3 * col + row
                value = l_ref[kt : kt + 1, :]
                sign = 1.0 if part == 0 else -1.0
                lb[CZS + k : CZS + k + 1, 0:SITES] = sign * value
                lb[CZD + k : CZD + k + 1, 0:SITES] = -sign * value
    ta[...] = jnp.transpose(la[...])
    tb[...] = jnp.transpose(lb[...])
    raw = ta[0:SITES, :]
    other = jnp.concatenate([tb[plane:SITES, :], tb[0:plane, :]], axis=0)
    y = lax.broadcasted_iota(jnp.int32, (SITES, LANES), 0) % TLY
    column = lax.broadcasted_iota(jnp.int32, (SITES, LANES), 1)
    back = pltpu.roll(raw, 1, 0)
    is_yf = (column >= CYF) & (column < CYB)
    is_yb = (column >= CYB) & (column < CZS)
    table = jnp.where(is_yb, back, raw)
    gone = (is_yf & (y == TLY - 1)) | (is_yb & (y == 0))
    ta[0:SITES, :] = jnp.where(gone, 0.0, table) + other
    wc_ref[0:LAYER, :] = jnp.zeros((LAYER, LANES), jnp.float32)
    clear_ends(fr_ref)
    for x in range(TLX):
        for z in range(LZ):
            src = z * plane + x * TLY
            dst = (x + 1) * LAYER + z * TLY
            wc_ref[dst : dst + TLY, :] = ta[src : src + TLY, :]
            for half in range(fr_ref.shape[1]):
                for part in range(2):
                    for colour in range(3):
                        dst = (x + 1) * XROWS + colour * LAYER + z * TLY
                        fr_ref[part, half, dst : dst + TLY, :] = v_ref[
                            3 * part + colour, src : src + TLY, half * LANES : (half + 1) * LANES
                        ]
    send_layers(fr_ref, wc_ref, xlo_ref, xhi_ref, ylo_ref, yhi_ref)


def roll_layer(f_ref, half, base, rolled):
    for part in range(2):
        for colour in range(3):
            rows = f_ref[part, half, pl.ds(base + colour * LAYER, LAYER), :]
            at = colour * LAYER
            rolled[0, half, part, at : at + LAYER, :] = pltpu.roll(rows, LAYER - 1, 0)
            rolled[1, half, part, at : at + LAYER, :] = pltpu.roll(rows, 1, 0)
            rolled[2, half, part, at : at + LAYER, :] = pltpu.roll(rows, TLY, 0)


def layer_hops(f_ref, wb_ref, rolled, x, tile, z_column):
    step = 8 * tile
    base = (x + 1) * XROWS

    def table(column):
        return wb_ref[x + 1, column, pl.ds(pl.multiple_of(step, 8), 8), :]

    def below(column):
        return wb_ref[x, column, pl.ds(pl.multiple_of(step, 8), 8), :]

    def straight(shift):
        return lambda p, c, half: f_ref[p, half, pl.ds(pl.multiple_of(base + shift + c * LAYER + step, 8), 8), :]

    def turned(which):
        return lambda p, c, half: rolled[which, half, p, pl.ds(pl.multiple_of(c * LAYER + step, 8), 8), :]

    return (
        (table, BX, straight(XROWS), False, 0),
        (below, BX, straight(-XROWS), True, 0),
        (table, BYF, turned(0), False, 1),
        (table, BYB, turned(1), True, 1),
        (table, z_column, turned(2), False, 2),
    ), straight(0)


def hop_all(weights, column, load, adjoint, halves, acc, minus=False):
    for col in range(3):
        field = [[load(p, col, half) for half in halves] for p in range(2)]
        for row in range(3):
            at = column + (3 * col + row if adjoint else 3 * row + col)
            real = weights(at)
            imag = weights(at + 9)
            for half in halves:
                terms = (
                    (0, real * field[0][half], False),
                    (0, imag * field[1][half], not adjoint),
                    (1, real * field[1][half], False),
                    (1, imag * field[0][half], adjoint),
                )
                for part, value, negative in terms:
                    before = acc[part][row][half]
                    if before is None:
                        acc[part][row][half] = -value if negative != minus else value
                    else:
                        acc[part][row][half] = before - value if negative != minus else before + value
    return acc


def spread_kernel(wc_ref, wb_ref):
    def layer(x, carry):
        table = wc_ref[pl.ds(pl.multiple_of(x * LAYER, 8), LAYER), :]
        for column in range(WIDE):
            source = column if column < 18 else column + CYF - 18
            wb_ref[x, column] = spread(table, source)
        return carry

    lax.fori_loop(0, TLX + 1, layer, 0)


def empty_acc(halves):
    return [[[None for _ in halves] for _ in range(3)] for _ in range(2)]


def smear_kernel(f_ref, wb_ref, out_ref, rolled):
    clear_ends(out_ref)
    halves = range(f_ref.shape[1])

    def layer(x, carry):
        base = pl.multiple_of((x + 1) * XROWS, 8)
        for half in halves:
            roll_layer(f_ref, half, base, rolled)

        def tiles(tile, carry):
            hops, here = layer_hops(f_ref, wb_ref, rolled, x, tile, BZS)
            acc = empty_acc(halves)
            for weights, column, load, adjoint, _ in hops:
                hop_all(weights, column, load, adjoint, halves, acc)
            for part in range(2):
                for colour in range(3):
                    for half in halves:
                        value = (1.0 - 6.0 * KAPPA) * here(part, colour, half) + KAPPA * acc[part][colour][half]
                        out_ref[part, half, pl.ds(base + colour * LAYER + 8 * tile, 8), :] = value
            return carry

        return lax.fori_loop(0, LAYER // 8, tiles, carry, unroll=True)

    lax.fori_loop(0, TLX, layer, 0)


def cross(once_ref, wc_ref, rxlo, rxhi, rylo, ryhi, save=None):
    last = TLX * XROWS
    for half in range(once_ref.shape[1]):
        table = wc_ref[TLX * LAYER : (TLX + 1) * LAYER, :]
        hop_x = matvec(table, CX, grid2(lambda p, c: layer_rows(rxhi, p, half, c * LAYER)))
        hop_y = []
        for z in range(LZ):
            table = wc_ref[pl.ds(LAYER + z * TLY + TLY - 1, TLX, stride=LAYER), :]
            hop_y.append(matvec(table, CY, grid2(lambda p, c: layer_rows(ryhi, p, half, c * LAYER + z * TLX, TLX))))
        for part in range(2):
            for colour in range(3):
                at = colour * LAYER
                low = layer_rows(rxlo, part, half, at)
                once_ref[part, half, XROWS + at : XROWS + at + LAYER, :] += KAPPA * low
                once_ref[part, half, last + at : last + at + LAYER, :] += KAPPA * hop_x[part][colour]
                if save is not None:
                    save[part, half, at : at + LAYER, :] = low
                    save[part, half, XROWS + at : XROWS + at + LAYER, :] = hop_x[part][colour]
                for z in range(LZ):
                    low = layer_rows(rylo, part, half, at + z * TLX, TLX)
                    rows = y_rows(colour, z, 0)
                    once_ref[part, half, rows, :] = once_ref[part, half, rows, :] + KAPPA * low
                    rows = y_rows(colour, z, TLY - 1)
                    once_ref[part, half, rows, :] = once_ref[part, half, rows, :] + KAPPA * hop_y[z][part][colour]
                    if save is not None:
                        to = 2 * XROWS + at + z * TLX
                        save[part, half, to : to + TLX, :] = low
                        save[part, half, to + XROWS : to + XROWS + TLX, :] = hop_y[z][part][colour]


def edge_kernel(part_ref, wc_ref, rxlo, rxhi, rylo, ryhi, once_ref, save, xlo_ref, xhi_ref, ylo_ref, yhi_ref):
    once_ref[...] = part_ref[...]
    cross(once_ref, wc_ref, rxlo, rxhi, rylo, ryhi, save)
    send_layers(once_ref, wc_ref, xlo_ref, xhi_ref, ylo_ref, yhi_ref)


def split(value):
    high = value.astype(jnp.bfloat16)
    return high, (value - high.astype(jnp.float32)).astype(jnp.bfloat16)


def phased(real, imag, half, lane, at, size, cos_ref, sin_ref, ah_ref, al_ref):
    real, imag = jnp.transpose(real), jnp.transpose(imag)
    halves = ah_ref.shape[0] // cos_ref.shape[0] // LANES
    for m in range(cos_ref.shape[0]):
        cosine = jnp.broadcast_to(cos_ref[m : m + 1, lane : lane + LANES], (LANES, LANES))
        sine = jnp.broadcast_to(sin_ref[m : m + 1, lane : lane + LANES], (LANES, LANES))
        row = (m * halves + half) * LANES
        high, low = split(cosine * real - sine * imag)
        ah_ref[row : row + LANES, at : at + LANES] = high
        al_ref[row : row + LANES, at : at + LANES] = low
        high, low = split(sine * real + cosine * imag)
        ah_ref[row : row + LANES, size + at : size + at + LANES] = high
        al_ref[row : row + LANES, size + at : size + at + LANES] = low


def head_kernel(fr_ref, cos_ref, sin_ref, ah_ref, al_ref):
    for half in range(fr_ref.shape[1]):
        for at in range(0, HEAD, LANES):
            real, imag = (fr_ref[p, half, XROWS + at : XROWS + at + LANES, :] for p in range(2))
            phased(real, imag, half, at, at, HEAD, cos_ref, sin_ref, ah_ref, al_ref)


def tail_kernel(fr_ref, save, cos_ref, sin_ref, ah_ref, al_ref, rows):
    for half in range(fr_ref.shape[1]):
        for part in range(2):
            rows[part, 0 : MAIN - HEAD, :] = fr_ref[part, half, XROWS + HEAD : XROWS + MAIN, :]
            rows[part, MAIN - HEAD : TAIL, :] = save[part, half]
        for at in range(0, TAIL, LANES):
            real, imag = (rows[p, at : at + LANES, :] for p in range(2))
            phased(real, imag, half, HEAD + at, at, TAIL, cos_ref, sin_ref, ah_ref, al_ref)


def displace_kernel(part_ref, wc_ref, wb_ref, rxlo, rxhi, rylo, ryhi, mask_ref, sh_ref, sl_ref, th_ref, tl_ref, twice, shift, rolled):
    twice[...] = part_ref[...]
    cross(twice, wc_ref, rxlo, rxhi, rylo, ryhi)
    halves = range(twice.shape[1])

    def layer(x, carry):
        into = pl.multiple_of(x * XROWS, 8)
        for half in halves:
            roll_layer(twice, half, pl.multiple_of((x + 1) * XROWS, 8), rolled)

        def tiles(tile, carry):
            hops, _ = layer_hops(twice, wb_ref, rolled, x, tile, BZD)
            total = empty_acc(halves)
            for which in range(3):
                acc = empty_acc(halves)
                for weights, column, load, adjoint, direction in hops:
                    if direction == which:
                        hop_all(weights, column, load, adjoint, halves, acc, adjoint)
                for half in halves:
                    lanes = slice(half * LANES, (half + 1) * LANES)
                    mask = jnp.broadcast_to(mask_ref[which : which + 1, lanes], (8, LANES))
                    for part in range(2):
                        for row in range(3):
                            value = mask * acc[part][row][half]
                            before = total[part][row][half]
                            total[part][row][half] = value if before is None else before + value
            for part in range(2):
                for colour in range(3):
                    for half in halves:
                        at = pl.ds(pl.multiple_of(into + colour * LAYER + 8 * tile, 8), 8)
                        shift[part, half, at, :] = total[part][colour][half]
            return carry

        return lax.fori_loop(0, LAYER // 8, tiles, carry, unroll=True)

    lax.fori_loop(0, TLX, layer, 0)
    last = TLX * XROWS
    for half in halves:
        lanes = slice(half * LANES, (half + 1) * LANES)
        mask_x = jnp.broadcast_to(mask_ref[0:1, lanes], (XROWS, LANES))
        mask_y = jnp.broadcast_to(mask_ref[1:2, lanes], (TLX, LANES))
        for part in range(2):
            shift[part, half, MAIN : MAIN + XROWS, :] = mask_x * twice[part, half, XROWS : 2 * XROWS, :]
            shift[part, half, MAIN + XROWS : MAIN + 2 * XROWS, :] = -mask_x * twice[part, half, last : last + XROWS, :]
            for colour in range(3):
                for z in range(LZ):
                    to = MAIN + 2 * XROWS + colour * LAYER + z * TLX
                    shift[part, half, to : to + TLX, :] = mask_y * twice[part, half, y_rows(colour, z, 0), :]
                    to += XROWS
                    shift[part, half, to : to + TLX, :] = -mask_y * twice[part, half, y_rows(colour, z, TLY - 1), :]
    width = len(halves) * LANES
    for high_ref, low_ref, first, size in ((sh_ref, sl_ref, 0, HEAD), (th_ref, tl_ref, HEAD, TAIL)):
        for half in halves:
            real = slice(half * LANES, (half + 1) * LANES)
            imag = slice(width + half * LANES, width + (half + 1) * LANES)
            for row in range(0, size, 128):
                top = slice(row, row + 128)
                bottom = slice(size + row, size + row + 128)
                high, low = split(shift[0, half, first + row : first + row + 128, :])
                high_ref[top, real] = high
                low_ref[top, real] = low
                high_ref[bottom, imag] = -high
                low_ref[bottom, imag] = -low
                high, low = split(shift[1, half, first + row : first + row + 128, :])
                high_ref[bottom, real] = high
                low_ref[bottom, real] = low
                high_ref[top, imag] = high
                low_ref[top, imag] = low


def dot(a, b):
    return jnp.dot(a, b, preferred_element_type=jnp.float32)


def meson_kernel(ah, al, bh, bl, sh, sl, th, tl, out_ref):
    total = dot(ah[...], sh[...]) + dot(ah[...], sl[...]) + dot(al[...], sh[...])
    out_ref[...] = total + dot(bh[...], th[...]) + dot(bh[...], tl[...]) + dot(bl[...], th[...])


def phases(momenta, position, devices, tiles):
    site = np.arange(SITES)
    x, zy = site // LAYER, site % LAYER
    own = [np.repeat(a.reshape(TLX, 1, LAYER), 3, 1).reshape(-1) for a in (x, zy % TLY, zy // TLY)]
    edge = np.arange(LAYER)
    full = np.full(LAYER, 0)
    edges = (
        (full + TLX - 1, edge % TLY, edge // TLY),
        (full, edge % TLY, edge // TLY),
        (edge % TLX, full + TLY - 1, edge // TLX),
        (edge % TLX, full, edge // TLX),
    )
    steps = (-tiles, tiles, -1, 1)
    xs, ys, zs, move = own[0], own[1], own[2], np.zeros(MAIN, np.int64)
    for step, (ex, ey, ez) in zip(steps, edges):
        xs = np.concatenate([xs] + [ex] * 3)
        ys = np.concatenate([ys] + [ey] * 3)
        zs = np.concatenate([zs] + [ez] * 3)
        move = np.concatenate([move, np.full(XROWS, step)])
    tile = (position + jnp.asarray(move, jnp.int32) + devices) % devices
    lx, ly = TLX * tiles, TLY * tiles
    sx = (tile // tiles) * TLX + jnp.asarray(xs, jnp.int32)
    sy = (tile % tiles) * TLY + jnp.asarray(ys, jnp.int32)
    sz = jnp.asarray(zs, jnp.int32)
    frac = (momenta[:, 0:1] * sx % lx).astype(jnp.float32) / lx
    frac = frac + (momenta[:, 1:2] * sy % ly).astype(jnp.float32) / ly
    frac = frac + (momenta[:, 2:3] * sz % LZ).astype(jnp.float32) / LZ
    theta = 2.0 * math.pi * frac
    return jnp.cos(theta), jnp.sin(theta)


def send(block, devices, distance):
    return lax.ppermute(block, "site", [(i, (i + distance) % devices) for i in range(devices)])


def halo(sends, devices, tiles):
    xlo, xhi, ylo, yhi = sends
    return (
        send(xhi, devices, tiles),
        send(xlo, devices, -tiles),
        send(yhi, devices, 1),
        send(ylo, devices, -1),
    )


def stages(devices):
    found, stride = [], 1
    while stride < devices:
        left = devices // stride
        size = 2 if stride < 4 else 4 if left % 4 == 0 else 2
        found.append((stride, size))
        stride *= size
    return found


def scatter_sum(block, position, devices):
    shape = block.shape[1:]
    for stride, size in stages(devices):
        left = block.shape[0] // size
        block = block.reshape((left, size) + shape)
        mine = (position // stride) % size
        total = lax.dynamic_index_in_dim(block, mine, 1, keepdims=False)
        for step in range(1, size):
            other = (mine + step) % size
            out = lax.dynamic_index_in_dim(block, other, 1, keepdims=False)
            route = []
            for i in range(devices):
                digit = (i // stride) % size
                route.append((i, i + ((digit + step) % size - digit) * stride))
            total = total + lax.ppermute(out, "site", route)
        block = total
    return block[0]


def on_device(vectors, links, momenta, directions):
    devices = lax.axis_size("site")
    tiles = math.isqrt(devices)
    position = lax.axis_index("site")
    nev = vectors.shape[-1]
    moments = momenta.shape[0]
    field = vectors.reshape(6, SITES, nev)
    table = links.reshape(54, SITES)
    halves = nev // LANES
    layer = f32(2, halves, XROWS, LANES)
    padded = f32(2, halves, PADDED, LANES)
    fr, wc, *sends = call(
        pack_kernel,
        (padded, f32((TLX + 1) * LAYER, LANES), layer, layer, layer, layer),
        [pltpu.VMEM((128, 384), jnp.float32)] * 2 + [pltpu.VMEM((384, 128), jnp.float32)] * 2,
        inputs=2,
    )(field, table)
    received = halo(sends, devices, tiles)
    flops = 2 * 180 * 2 * SITES * nev
    wb = call(spread_kernel, f32(TLX + 1, WIDE, LAYER, LANES), (), flops >> 4, 1 << 20)(wc)
    rolled = pltpu.VMEM((3, halves, 2, XROWS, LANES), jnp.float32)
    once = call(smear_kernel, padded, [rolled], flops, 3 << 20, 2)(fr, wb)
    cosine, sine = phases(momenta, position, devices, tiles)
    head = bf16(moments * nev, 2 * HEAD)
    tail = bf16(moments * nev, 2 * TAIL)
    ah, al = call(head_kernel, (head, head), (), flops, 8 << 20, 3)(fr, cosine, sine)
    once, save, *sends = call(edge_kernel, (padded, f32(2, halves, EDGE, LANES), layer, layer, layer, layer), inputs=6)(
        once, wc, *received
    )
    received = halo(sends, devices, tiles)
    twice = call(smear_kernel, padded, [rolled], flops, 3 << 20, 2)(once, wb)
    rows = pltpu.VMEM((2, TAIL, LANES), jnp.float32)
    bh, bl = call(tail_kernel, (tail, tail), [rows], flops, 4 << 20, 4)(fr, save, cosine, sine)
    scale = 1.0 / math.sqrt(3.0 * TLX * tiles * TLY * tiles * LZ)
    which = jnp.arange(3, dtype=jnp.int32)[:, None]
    masks = jnp.where(directions[None, :] == which, jnp.float32(scale), jnp.float32(0.0))
    sh, sl, th, tl = call(
        displace_kernel,
        (bf16(2 * HEAD, 2 * nev), bf16(2 * HEAD, 2 * nev), bf16(2 * TAIL, 2 * nev), bf16(2 * TAIL, 2 * nev)),
        [
            pltpu.VMEM((2, halves, PADDED, LANES), jnp.float32),
            pltpu.VMEM((2, halves, HEAD + TAIL, LANES), jnp.float32),
            rolled,
        ],
        inputs=8,
    )(twice, wc, wb, *received, masks)
    whole = lambda a: pl.BlockSpec(a.shape, lambda m: (0, 0))
    partial = pl.pallas_call(
        meson_kernel,
        out_shape=f32(nev, moments * 2 * nev),
        grid=(moments,),
        in_specs=[pl.BlockSpec((nev, 2 * HEAD), lambda m: (m, 0))] * 2
        + [pl.BlockSpec((nev, 2 * TAIL), lambda m: (m, 0))] * 2
        + [whole(sh), whole(sl), whole(th), whole(tl)],
        out_specs=pl.BlockSpec((nev, 2 * nev), lambda m: (0, m)),
        compiler_params=pltpu.CompilerParams(vmem_limit_bytes=VMEM_LIMIT),
    )(ah, al, bh, bl, sh, sl, th, tl)
    total = scatter_sum(partial.reshape(devices, nev // devices, moments * 2 * nev), position, devices)
    return total.reshape(nev // devices, moments, 2, nev)


def solution(mesh):
    placed = (
        P("grp", None, "site", None, None),
        P("grp", None, None, None, "site", None),
        P(),
        P(),
    )
    return jax.shard_map(
        on_device,
        mesh=mesh,
        in_specs=placed,
        out_specs=P("site", "grp", None, None),
        check_vma=False,
    )
```

```python
import functools
import math

import jax
import jax.numpy as jnp
import numpy as np
from jax import lax
from jax.experimental import pallas as pl
from jax.experimental.pallas import tpu as pltpu
from jax.sharding import PartitionSpec as P

TLX = 12
TLY = 12
LZ = 2
KAPPA = 0.08

LAYER = LZ * TLY
SITES = TLX * LAYER
XROWS = 3 * LAYER
MAIN = TLX * XROWS
PADDED = (TLX + 2) * XROWS
EDGE = 4 * XROWS
HEAD = MAIN // 128 * 128
TAIL = MAIN - HEAD + EDGE
LANES = 128
BX, BYF, BYB, BZS, BZD, WIDE = 0, 18, 36, 54, 72, 90
CX, CY, CZ = 0, 18, 36
CYF, CYB, CZS, CZD = 54, 72, 90, 108
VMEM_LIMIT = 12 * 2**20


def call(kernel, outs, scratch=(), flops=0, moved=0, inputs=1, scalars=0, off_chip=0, **kwargs):
    on_chip = pl.BlockSpec(memory_space=pltpu.VMEM)
    first = [pl.BlockSpec(memory_space=pltpu.SMEM)] * scalars + [pl.BlockSpec(memory_space=pltpu.HBM)] * off_chip
    return pl.pallas_call(
        kernel,
        out_shape=outs,
        in_specs=first + [on_chip] * inputs,
        out_specs=jax.tree.map(lambda _: on_chip, outs),
        scratch_shapes=list(scratch),
        compiler_params=pltpu.CompilerParams(vmem_limit_bytes=VMEM_LIMIT),
        cost_estimate=pl.CostEstimate(flops=flops, bytes_accessed=moved, transcendentals=0),
        **kwargs,
    )


def f32(*shape):
    return jax.ShapeDtypeStruct(shape, jnp.float32)


def bf16(*shape):
    return jax.ShapeDtypeStruct(shape, jnp.bfloat16)


def spread(table, column, lanes=LANES):
    return jnp.broadcast_to(table[:, column : column + 1], (table.shape[0], lanes))


def matvec(table, first, field, adjoint=False, acc=None, minus=False):
    out = [[None] * 3, [None] * 3] if acc is None else [list(acc[0]), list(acc[1])]
    lanes = field[0][0].shape[-1]

    def put(part, row, value, negative):
        if negative != minus:
            out[part][row] = -value if out[part][row] is None else out[part][row] - value
        else:
            out[part][row] = value if out[part][row] is None else out[part][row] + value

    for row in range(3):
        for col in range(3):
            at = first + (3 * col + row if adjoint else 3 * row + col)
            real = spread(table, at, lanes)
            imag = spread(table, at + 9, lanes)
            put(0, row, real * field[0][col], False)
            put(0, row, imag * field[1][col], not adjoint)
            put(1, row, real * field[1][col], False)
            put(1, row, imag * field[0][col], adjoint)
    return out


def layer_rows(ref, part, half, first, size=LAYER):
    return ref[part, half, first : first + size, :]


def grid2(load):
    return [[load(part, colour) for colour in range(3)] for part in range(2)]


def y_rows(colour, z, y):
    return pl.ds(XROWS + colour * LAYER + z * TLY + y, TLX, stride=XROWS)


def send_layers(f_ref, wc_ref, xlo_ref, xhi_ref, ylo_ref, yhi_ref):
    last = TLX * XROWS
    for half in range(f_ref.shape[1]):
        for part in range(2):
            xlo_ref[part, half] = f_ref[part, half, XROWS : 2 * XROWS, :]
            for colour in range(3):
                for z in range(LZ):
                    to = colour * LAYER + z * TLX
                    ylo_ref[part, half, to : to + TLX, :] = f_ref[part, half, y_rows(colour, z, 0), :]
        table = wc_ref[TLX * LAYER : (TLX + 1) * LAYER, :]
        hop = matvec(table, CX, grid2(lambda p, c: layer_rows(f_ref, p, half, last + c * LAYER)), adjoint=True)
        for part in range(2):
            for colour in range(3):
                xhi_ref[part, half, colour * LAYER : (colour + 1) * LAYER, :] = hop[part][colour]
        for z in range(LZ):
            table = wc_ref[pl.ds(LAYER + z * TLY + TLY - 1, TLX, stride=LAYER), :]
            hop = matvec(table, CY, grid2(lambda p, c: f_ref[p, half, y_rows(c, z, TLY - 1), :]), adjoint=True)
            for part in range(2):
                for colour in range(3):
                    to = colour * LAYER + z * TLX
                    yhi_ref[part, half, to : to + TLX, :] = hop[part][colour]


def clear_ends(ref):
    for part in range(2):
        for half in range(ref.shape[1]):
            ref[part, half, 0:XROWS, :] = jnp.zeros((XROWS, LANES), jnp.float32)
            ref[part, half, PADDED - XROWS : PADDED, :] = jnp.zeros((XROWS, LANES), jnp.float32)


def pack_kernel(v_ref, l_ref, fr_ref, wc_ref, xlo_ref, xhi_ref, ylo_ref, yhi_ref, la, lb, ta, tb):
    la[...] = jnp.zeros_like(la)
    lb[...] = jnp.zeros_like(lb)
    plane = SITES // LZ
    la[0:54, 0:SITES] = l_ref[...]
    la[CYF : CYF + 18, 0:SITES] = l_ref[CY : CY + 18, :]
    la[CYB : CYB + 18, 0:SITES] = l_ref[CY : CY + 18, :]
    la[CZS : CZS + 18, 0:SITES] = l_ref[CZ : CZ + 18, :]
    la[CZD : CZD + 18, 0:SITES] = l_ref[CZ : CZ + 18, :]
    for part in range(2):
        for row in range(3):
            for col in range(3):
                k = 9 * part + 3 * row + col
                kt = CZ + 9 * part + 3 * col + row
                value = l_ref[kt : kt + 1, :]
                sign = 1.0 if part == 0 else -1.0
                lb[CZS + k : CZS + k + 1, 0:SITES] = sign * value
                lb[CZD + k : CZD + k + 1, 0:SITES] = -sign * value
    ta[...] = jnp.transpose(la[...])
    tb[...] = jnp.transpose(lb[...])
    raw = ta[0:SITES, :]
    other = jnp.concatenate([tb[plane:SITES, :], tb[0:plane, :]], axis=0)
    y = lax.broadcasted_iota(jnp.int32, (SITES, LANES), 0) % TLY
    column = lax.broadcasted_iota(jnp.int32, (SITES, LANES), 1)
    back = pltpu.roll(raw, 1, 0)
    is_yf = (column >= CYF) & (column < CYB)
    is_yb = (column >= CYB) & (column < CZS)
    table = jnp.where(is_yb, back, raw)
    gone = (is_yf & (y == TLY - 1)) | (is_yb & (y == 0))
    ta[0:SITES, :] = jnp.where(gone, 0.0, table) + other
    wc_ref[0:LAYER, :] = jnp.zeros((LAYER, LANES), jnp.float32)
    clear_ends(fr_ref)
    for x in range(TLX):
        for z in range(LZ):
            src = z * plane + x * TLY
            dst = (x + 1) * LAYER + z * TLY
            wc_ref[dst : dst + TLY, :] = ta[src : src + TLY, :]
            for half in range(fr_ref.shape[1]):
                for part in range(2):
                    for colour in range(3):
                        dst = (x + 1) * XROWS + colour * LAYER + z * TLY
                        fr_ref[part, half, dst : dst + TLY, :] = v_ref[
                            3 * part + colour, src : src + TLY, half * LANES : (half + 1) * LANES
                        ]
    send_layers(fr_ref, wc_ref, xlo_ref, xhi_ref, ylo_ref, yhi_ref)


def roll_layer(f_ref, half, base, rolled):
    for part in range(2):
        for colour in range(3):
            rows = f_ref[part, half, pl.ds(base + colour * LAYER, LAYER), :]
            at = colour * LAYER
            rolled[0, half, part, at : at + LAYER, :] = pltpu.roll(rows, LAYER - 1, 0)
            rolled[1, half, part, at : at + LAYER, :] = pltpu.roll(rows, 1, 0)
            rolled[2, half, part, at : at + LAYER, :] = pltpu.roll(rows, TLY, 0)


def layer_hops(f_ref, wb_ref, rolled, x, tile, z_column):
    step = 8 * tile
    base = (x + 1) * XROWS

    def table(column):
        return wb_ref[x + 1, column, pl.ds(pl.multiple_of(step, 8), 8), :]

    def below(column):
        return wb_ref[x, column, pl.ds(pl.multiple_of(step, 8), 8), :]

    def straight(shift):
        return lambda p, c, half: f_ref[p, half, pl.ds(pl.multiple_of(base + shift + c * LAYER + step, 8), 8), :]

    def turned(which):
        return lambda p, c, half: rolled[which, half, p, pl.ds(pl.multiple_of(c * LAYER + step, 8), 8), :]

    return (
        (table, BX, straight(XROWS), False, 0),
        (below, BX, straight(-XROWS), True, 0),
        (table, BYF, turned(0), False, 1),
        (table, BYB, turned(1), True, 1),
        (table, z_column, turned(2), False, 2),
    ), straight(0)


def hop_all(weights, column, load, adjoint, halves, acc, minus=False):
    for col in range(3):
        field = [[load(p, col, half) for half in halves] for p in range(2)]
        for row in range(3):
            at = column + (3 * col + row if adjoint else 3 * row + col)
            real = weights(at)
            imag = weights(at + 9)
            for half in halves:
                terms = (
                    (0, real * field[0][half], False),
                    (0, imag * field[1][half], not adjoint),
                    (1, real * field[1][half], False),
                    (1, imag * field[0][half], adjoint),
                )
                for part, value, negative in terms:
                    before = acc[part][row][half]
                    if before is None:
                        acc[part][row][half] = -value if negative != minus else value
                    else:
                        acc[part][row][half] = before - value if negative != minus else before + value
    return acc


def hop_column(weights, col, field, adjoint, acc, minus):
    for row in range(3):
        at = 3 * col + row if adjoint else 3 * row + col
        real, imag = weights(at), weights(at + 9)
        terms = (
            (0, real * field[0], False),
            (0, imag * field[1], not adjoint),
            (1, real * field[1], False),
            (1, imag * field[0], adjoint),
        )
        for part, value, negative in terms:
            before = acc[part][row][0]
            if before is None:
                acc[part][row][0] = -value if negative != minus else value
            else:
                acc[part][row][0] = before - value if negative != minus else before + value


def spread_kernel(wc_ref, wb_ref):
    rest = wc_ref[...]
    terms = []
    for _ in range(2):
        terms.append(rest.astype(jnp.bfloat16))
        rest = rest - terms[-1].astype(jnp.float32)
    terms = jnp.concatenate(terms, axis=1)
    row = lax.broadcasted_iota(jnp.int32, (LANES, 2 * LANES), 0)
    right = lax.broadcasted_iota(jnp.int32, (LANES, 2 * LANES), 1) // LANES
    for column in range(0, WIDE, 2):
        source = column if column < 18 else column + CYF - 18
        ones = jnp.where(row == source + right, 1.0, 0.0).astype(jnp.bfloat16)
        copies = dot(terms, jnp.concatenate([ones] * 2, axis=0))
        for k in range(2):
            wb_ref[:, column + k] = copies[:, k * LANES : (k + 1) * LANES].reshape(TLX + 1, LAYER, LANES)


def empty_acc(halves):
    return [[[None for _ in halves] for _ in range(3)] for _ in range(2)]


def smear_kernel(f_ref, wb_ref, out_ref, rolled):
    clear_ends(out_ref)
    halves = range(f_ref.shape[1])

    def layer(x, carry):
        base = pl.multiple_of((x + 1) * XROWS, 8)
        for half in halves:
            roll_layer(f_ref, half, base, rolled)

        def tiles(tile, carry):
            hops, here = layer_hops(f_ref, wb_ref, rolled, x, tile, BZS)
            acc = empty_acc(halves)
            for weights, column, load, adjoint, _ in hops:
                hop_all(weights, column, load, adjoint, halves, acc)
            for part in range(2):
                for colour in range(3):
                    for half in halves:
                        value = (1.0 - 6.0 * KAPPA) * here(part, colour, half) + KAPPA * acc[part][colour][half]
                        out_ref[part, half, pl.ds(base + colour * LAYER + 8 * tile, 8), :] = value
            return carry

        return lax.fori_loop(0, LAYER // 8, tiles, carry, unroll=True)

    lax.fori_loop(0, TLX, layer, 0)


def cross(once_ref, wc_ref, rxlo, rxhi, rylo, ryhi, save=None):
    last = TLX * XROWS
    for half in range(once_ref.shape[1]):
        table = wc_ref[TLX * LAYER : (TLX + 1) * LAYER, :]
        hop_x = matvec(table, CX, grid2(lambda p, c: layer_rows(rxhi, p, half, c * LAYER)))
        hop_y = []
        for z in range(LZ):
            table = wc_ref[pl.ds(LAYER + z * TLY + TLY - 1, TLX, stride=LAYER), :]
            hop_y.append(matvec(table, CY, grid2(lambda p, c: layer_rows(ryhi, p, half, c * LAYER + z * TLX, TLX))))
        for part in range(2):
            for colour in range(3):
                at = colour * LAYER
                low = layer_rows(rxlo, part, half, at)
                once_ref[part, half, XROWS + at : XROWS + at + LAYER, :] += KAPPA * low
                once_ref[part, half, last + at : last + at + LAYER, :] += KAPPA * hop_x[part][colour]
                if save is not None:
                    save[part, half, at : at + LAYER, :] = low
                    save[part, half, XROWS + at : XROWS + at + LAYER, :] = hop_x[part][colour]
                for z in range(LZ):
                    low = layer_rows(rylo, part, half, at + z * TLX, TLX)
                    rows = y_rows(colour, z, 0)
                    once_ref[part, half, rows, :] = once_ref[part, half, rows, :] + KAPPA * low
                    rows = y_rows(colour, z, TLY - 1)
                    once_ref[part, half, rows, :] = once_ref[part, half, rows, :] + KAPPA * hop_y[z][part][colour]
                    if save is not None:
                        to = 2 * XROWS + at + z * TLX
                        save[part, half, to : to + TLX, :] = low
                        save[part, half, to + XROWS : to + XROWS + TLX, :] = hop_y[z][part][colour]


def edge_kernel(part_ref, wc_ref, rxlo, rxhi, rylo, ryhi, once_ref, save, xlo_ref, xhi_ref, ylo_ref, yhi_ref):
    once_ref[...] = part_ref[...]
    cross(once_ref, wc_ref, rxlo, rxhi, rylo, ryhi, save)
    send_layers(once_ref, wc_ref, xlo_ref, xhi_ref, ylo_ref, yhi_ref)


def split(value):
    high = value.astype(jnp.bfloat16)
    return high, (value - high.astype(jnp.float32)).astype(jnp.bfloat16)


def phased(real, imag, half, lane, at, size, cos_ref, sin_ref, ah_ref, al_ref):
    real, imag = jnp.transpose(real), jnp.transpose(imag)
    halves = ah_ref.shape[0] // cos_ref.shape[0] // LANES
    for m in range(cos_ref.shape[0]):
        cosine = jnp.broadcast_to(cos_ref[m : m + 1, lane : lane + LANES], (LANES, LANES))
        sine = jnp.broadcast_to(sin_ref[m : m + 1, lane : lane + LANES], (LANES, LANES))
        row = (m * halves + half) * LANES
        high, low = split(cosine * real - sine * imag)
        ah_ref[row : row + LANES, at : at + LANES] = high
        al_ref[row : row + LANES, at : at + LANES] = low
        high, low = split(sine * real + cosine * imag)
        ah_ref[row : row + LANES, size + at : size + at + LANES] = high
        al_ref[row : row + LANES, size + at : size + at + LANES] = low


def head_kernel(fr_ref, cos_ref, sin_ref, ah_ref, al_ref):
    for half in range(fr_ref.shape[1]):
        for at in range(0, HEAD, LANES):
            real, imag = (fr_ref[p, half, XROWS + at : XROWS + at + LANES, :] for p in range(2))
            phased(real, imag, half, at, at, HEAD, cos_ref, sin_ref, ah_ref, al_ref)


def tail_kernel(fr_ref, save, cos_ref, sin_ref, ah_ref, al_ref, rows):
    for half in range(fr_ref.shape[1]):
        for part in range(2):
            rows[part, 0 : MAIN - HEAD, :] = fr_ref[part, half, XROWS + HEAD : XROWS + MAIN, :]
            rows[part, MAIN - HEAD : TAIL, :] = save[part, half]
        for at in range(0, TAIL, LANES):
            real, imag = (rows[p, at : at + LANES, :] for p in range(2))
            phased(real, imag, half, HEAD + at, at, TAIL, cos_ref, sin_ref, ah_ref, al_ref)


def displace_kernel(part_ref, wc_ref, wb_ref, rxlo, rxhi, rylo, ryhi, dir_ref, sh_ref, sl_ref, th_ref, tl_ref, twice, shift, rolled, *, scale):
    twice[...] = part_ref[...]
    cross(twice, wc_ref, rxlo, rxhi, rylo, ryhi)
    halves = range(twice.shape[1])

    def along(which, half, rows=8):
        return jnp.broadcast_to(dir_ref[0:1, half * LANES : (half + 1) * LANES], (rows, LANES)) == which

    def layer(x, carry):
        into = pl.multiple_of(x * XROWS, 8)
        for half in halves:
            roll_layer(twice, half, pl.multiple_of((x + 1) * XROWS, 8), rolled)
        for tile in range(LAYER // 8):
            hops, _ = layer_hops(twice, wb_ref, rolled, x, tile, BZD)
            (ahead_x, bx, load_xf, _, _), (below, _, load_xb, _, _) = hops[0], hops[1]
            (table, byf, load_yf, _, _), (_, byb, load_yb, _, _), (_, bz, load_z, _, _) = hops[2:]
            for half in halves:
                is_x, is_y = along(0, half), along(1, half)
                acc = empty_acc([0])
                for col in range(3):
                    ahead = [
                        jnp.where(is_x, load_xf(p, col, half), jnp.where(is_y, load_yf(p, col, half), load_z(p, col, half)))
                        for p in range(2)
                    ]
                    behind = [
                        jnp.where(is_x, load_xb(p, col, half), jnp.where(is_y, load_yb(p, col, half), 0.0))
                        for p in range(2)
                    ]

                    def forward(at):
                        return jnp.where(is_x, ahead_x(bx + at), jnp.where(is_y, table(byf + at), table(bz + at)))

                    def backward(at):
                        return jnp.where(is_x, below(bx + at), table(byb + at))

                    hop_column(forward, col, ahead, False, acc, False)
                    hop_column(backward, col, behind, True, acc, True)
                for part in range(2):
                    for colour in range(3):
                        at = pl.ds(pl.multiple_of(into + colour * LAYER + 8 * tile, 8), 8)
                        shift[part, half, at, :] = scale * acc[part][colour][0]
        return carry

    lax.fori_loop(0, TLX, layer, 0)
    last = TLX * XROWS
    for half in halves:
        mask_x = jnp.where(along(0, half, XROWS), scale, 0.0)
        mask_y = jnp.where(along(1, half, TLX), scale, 0.0)
        for part in range(2):
            shift[part, half, MAIN : MAIN + XROWS, :] = mask_x * twice[part, half, XROWS : 2 * XROWS, :]
            shift[part, half, MAIN + XROWS : MAIN + 2 * XROWS, :] = -mask_x * twice[part, half, last : last + XROWS, :]
            for colour in range(3):
                for z in range(LZ):
                    to = MAIN + 2 * XROWS + colour * LAYER + z * TLX
                    shift[part, half, to : to + TLX, :] = mask_y * twice[part, half, y_rows(colour, z, 0), :]
                    to += XROWS
                    shift[part, half, to : to + TLX, :] = -mask_y * twice[part, half, y_rows(colour, z, TLY - 1), :]
    width = len(halves) * LANES
    for high_ref, low_ref, first, size in ((sh_ref, sl_ref, 0, HEAD), (th_ref, tl_ref, HEAD, TAIL)):
        for half in halves:
            real = slice(half * LANES, (half + 1) * LANES)
            imag = slice(width + half * LANES, width + (half + 1) * LANES)
            for row in range(0, size, 128):
                top = slice(row, row + 128)
                bottom = slice(size + row, size + row + 128)
                high, low = split(shift[0, half, first + row : first + row + 128, :])
                high_ref[top, real] = high
                low_ref[top, real] = low
                high_ref[bottom, imag] = -high
                low_ref[bottom, imag] = -low
                high, low = split(shift[1, half, first + row : first + row + 128, :])
                high_ref[bottom, real] = high
                low_ref[bottom, real] = low
                high_ref[top, imag] = high
                low_ref[top, imag] = low


def dot(a, b):
    return jnp.dot(a, b, preferred_element_type=jnp.float32)


def meson_kernel(ah, al, bh, bl, sh, sl, th, tl, out_ref):
    total = dot(ah[...], sh[...]) + dot(ah[...], sl[...]) + dot(al[...], sh[...])
    out_ref[...] = total + dot(bh[...], th[...]) + dot(bh[...], tl[...]) + dot(bl[...], th[...])


def product(blocks, moments, refs):
    ah, al, bh, bl, sh, sl, th, tl = refs
    nev = ah.shape[0] // moments
    size = blocks[1]

    def rows(ref):
        picked = [ref[pl.ds(pl.multiple_of(m * nev + b, size), size), :] for m in range(moments) for b in blocks[0]]
        return jnp.concatenate(picked, axis=0)

    ahv, alv, bhv, blv = rows(ah), rows(al), rows(bh), rows(bl)
    total = dot(ahv, sh[...]) + dot(ahv, sl[...]) + dot(alv, sh[...])
    return total + dot(bhv, th[...]) + dot(bhv, tl[...]) + dot(blv, th[...])


def put(out_ref, value, count, moments, added=None):
    size, width = out_ref.shape[1], value.shape[-1]
    for m in range(moments):
        for k in range(count):
            block = value[(m * count + k) * size : (m * count + k + 1) * size]
            lanes = slice(m * width, (m + 1) * width)
            if added is not None:
                block = block + added(k, lanes)
            out_ref[k, :, lanes] = block


def owners(groups, size, cores, turns):
    position = lax.axis_index("site")
    core, y, z = position % 2, position // 2 % 2, position // 4
    core = (core + cores) % 2
    return [((z + g) % groups * 4 + (y + turn) % 2 * 2 + core) * size for g in range(groups) for turn in turns]


def piece_kernel(*refs, moments, groups, cores, turns):
    out_ref = refs[-1]
    size = out_ref.shape[1]
    blocks = owners(groups, size, cores, turns)
    put(out_ref, product((blocks, size), moments, refs[:-1]), len(blocks), moments)


def merge_kernel(mine, theirs, *outs, picks):
    for out_ref, pairs in zip(outs, picks):
        for k, (a, b) in enumerate(pairs):
            out_ref[k] = mine[a] + theirs[b]


def phases(momenta, position, devices, tiles):
    site = np.arange(SITES)
    x, zy = site // LAYER, site % LAYER
    own = [np.repeat(a.reshape(TLX, 1, LAYER), 3, 1).reshape(-1) for a in (x, zy % TLY, zy // TLY)]
    edge = np.arange(LAYER)
    full = np.full(LAYER, 0)
    edges = (
        (full + TLX - 1, edge % TLY, edge // TLY),
        (full, edge % TLY, edge // TLY),
        (edge % TLX, full + TLY - 1, edge // TLX),
        (edge % TLX, full, edge // TLX),
    )
    steps = (-tiles, tiles, -1, 1)
    xs, ys, zs, move = own[0], own[1], own[2], np.zeros(MAIN, np.int64)
    for step, (ex, ey, ez) in zip(steps, edges):
        xs = np.concatenate([xs] + [ex] * 3)
        ys = np.concatenate([ys] + [ey] * 3)
        zs = np.concatenate([zs] + [ez] * 3)
        move = np.concatenate([move, np.full(XROWS, step)])
    tile = (position + jnp.asarray(move, jnp.int32) + devices) % devices
    lx, ly = TLX * tiles, TLY * tiles
    sx = (tile // tiles) * TLX + jnp.asarray(xs, jnp.int32)
    sy = (tile % tiles) * TLY + jnp.asarray(ys, jnp.int32)
    sz = jnp.asarray(zs, jnp.int32)
    frac = (momenta[:, 0:1] * sx % lx).astype(jnp.float32) / lx
    frac = frac + (momenta[:, 1:2] * sy % ly).astype(jnp.float32) / ly
    frac = frac + (momenta[:, 2:3] * sz % LZ).astype(jnp.float32) / LZ
    theta = 2.0 * math.pi * frac
    return jnp.cos(theta), jnp.sin(theta)


def send(block, devices, distance):
    return lax.ppermute(block, "site", [(i, (i + distance) % devices) for i in range(devices)])


def halo(sends, devices, tiles):
    xlo, xhi, ylo, yhi = sends
    return (
        send(xhi, devices, tiles),
        send(xlo, devices, -tiles),
        send(yhi, devices, 1),
        send(ylo, devices, -1),
    )


def stages(devices):
    found, stride = [], 1
    while stride < devices:
        left = devices // stride
        size = 2 if stride < 4 else 4 if left % 4 == 0 else 2
        found.append((stride, size))
        stride *= size
    return found


def scatter_sum(block, position, devices):
    shape = block.shape[1:]
    for stride, size in stages(devices):
        left = block.shape[0] // size
        block = block.reshape((left, size) + shape)
        mine = (position // stride) % size
        total = lax.dynamic_index_in_dim(block, mine, 1, keepdims=False)
        for step in range(1, size):
            other = (mine + step) % size
            out = lax.dynamic_index_in_dim(block, other, 1, keepdims=False)
            route = []
            for i in range(devices):
                digit = (i // stride) % size
                route.append((i, i + ((digit + step) % size - digit) * stride))
            total = total + lax.ppermute(out, "site", route)
        block = total
    return block[0]


def on_device(vectors, links, momenta, directions):
    devices = lax.axis_size("site")
    tiles = math.isqrt(devices)
    position = lax.axis_index("site")
    nev = vectors.shape[-1]
    moments = momenta.shape[0]
    field = vectors.reshape(6, SITES, nev)
    table = links.reshape(54, SITES)
    halves = nev // LANES
    layer = f32(2, halves, XROWS, LANES)
    padded = f32(2, halves, PADDED, LANES)
    fr, wc, *sends = call(
        pack_kernel,
        (padded, f32((TLX + 1) * LAYER, LANES), layer, layer, layer, layer),
        [pltpu.VMEM((128, 384), jnp.float32)] * 2 + [pltpu.VMEM((384, 128), jnp.float32)] * 2,
        inputs=2,
    )(field, table)
    received = halo(sends, devices, tiles)
    flops = 2 * 180 * 2 * SITES * nev
    wb = call(spread_kernel, f32(TLX + 1, WIDE, LAYER, LANES), (), flops >> 4, 1 << 20)(wc)
    rolled = pltpu.VMEM((3, halves, 2, XROWS, LANES), jnp.float32)
    once = call(smear_kernel, padded, [rolled], flops, 3 << 20, 2)(fr, wb)
    cosine, sine = phases(momenta, position, devices, tiles)
    head = bf16(moments * nev, 2 * HEAD)
    tail = bf16(moments * nev, 2 * TAIL)
    ah, al = call(head_kernel, (head, head), (), flops, 8 << 20, 3)(fr, cosine, sine)
    once, save, *sends = call(edge_kernel, (padded, f32(2, halves, EDGE, LANES), layer, layer, layer, layer), inputs=6)(
        once, wc, *received
    )
    received = halo(sends, devices, tiles)
    twice = call(smear_kernel, padded, [rolled], flops, 3 << 20, 2)(once, wb)
    rows = pltpu.VMEM((2, TAIL, LANES), jnp.float32)
    bh, bl = call(tail_kernel, (tail, tail), [rows], flops, 4 << 20, 4)(fr, save, cosine, sine)
    scale = 1.0 / math.sqrt(3.0 * TLX * tiles * TLY * tiles * LZ)
    operands = call(
        functools.partial(displace_kernel, scale=scale),
        (bf16(2 * HEAD, 2 * nev), bf16(2 * HEAD, 2 * nev), bf16(2 * TAIL, 2 * nev), bf16(2 * TAIL, 2 * nev)),
        [
            pltpu.VMEM((2, halves, PADDED, LANES), jnp.float32),
            pltpu.VMEM((2, halves, HEAD + TAIL, LANES), jnp.float32),
            rolled,
        ],
        inputs=8,
    )(twice, wc, wb, *received, directions[None, :])
    operands = (ah, al, bh, bl) + tuple(operands)
    size, columns = nev // devices, moments * 2 * nev
    if size % 16 == 0 and devices % 8 == 0:
        total = pieces(operands, position, devices, moments, size, columns)
    else:
        total = whole_product(operands, position, devices, moments, nev)
    return total.reshape(size, moments, 2, nev)


def whole_product(operands, position, devices, moments, nev):
    whole = lambda a: pl.BlockSpec(a.shape, lambda m: (0, 0))
    partial = pl.pallas_call(
        meson_kernel,
        out_shape=f32(nev, moments * 2 * nev),
        grid=(moments,),
        in_specs=[pl.BlockSpec((nev, a.shape[1]), lambda m: (m, 0)) for a in operands[:4]]
        + [whole(a) for a in operands[4:]],
        out_specs=pl.BlockSpec((nev, 2 * nev), lambda m: (0, m)),
        compiler_params=pltpu.CompilerParams(vmem_limit_bytes=40 * 2**20),
    )(*operands)
    return scatter_sum(partial.reshape(devices, nev // devices, moments * 2 * nev), position, devices)


def pieces(operands, position, devices, moments, size, columns):
    groups = devices // 4
    shared = dict(moments=moments, groups=groups)
    cost = dict(flops=2 * 3 * size * groups * moments * 4 * (HEAD + TAIL) * 256, moved=1 << 20)
    block = lambda count: f32(count, size, columns)
    out = call(
        functools.partial(piece_kernel, cores=1, turns=(0, 1), **shared), block(2 * groups), (), inputs=8, **cost
    )(*operands)
    swapped = lax.ppermute(out, "site", [(i, i ^ 1) for i in range(devices)])
    far = call(
        functools.partial(piece_kernel, cores=0, turns=(1,), **shared), block(groups), (), inputs=8, **cost
    )(*operands)
    early = list(range(1, groups // 2 + 1))
    late = list(range(groups // 2 + 1, groups)) + [0]
    first, second = call(
        functools.partial(merge_kernel, picks=[[(g, 2 * g + 1) for g in early], [(g, 2 * g + 1) for g in late]]),
        (block(len(early)), block(len(late))),
        inputs=2,
    )(far, swapped)
    flip = [(i, i ^ 2) for i in range(devices)]
    first = lax.ppermute(first, "site", flip)
    second = lax.ppermute(second, "site", flip)
    near = call(
        functools.partial(piece_kernel, cores=0, turns=(0,), **shared), block(groups), (), inputs=8, **cost
    )(*operands)
    near = call(
        functools.partial(merge_kernel, picks=[[(g, 2 * g) for g in range(groups)]]), (block(groups),), inputs=2
    )(near, swapped)[0]
    total = None
    arrived = []
    for steps, got in ((early, first), (late, second)):
        sums = call(
            functools.partial(merge_kernel, picks=[[(g, k)] for k, g in enumerate(steps)]),
            tuple(block(1) for _ in steps),
            inputs=2,
        )(near, got)
        for step, value in zip(steps, sums):
            if step == 0:
                total = value
            else:
                arrived.append(lax.ppermute(value, "site", [(i, (i + 4 * step) % devices) for i in range(devices)]))
    for value in arrived:
        total = total + value
    return total[0]


def solution(mesh):
    placed = (
        P("grp", None, "site", None, None),
        P("grp", None, None, None, "site", None),
        P(),
        P(),
    )
    return jax.shard_map(
        on_device,
        mesh=mesh,
        in_specs=placed,
        out_specs=P("site", "grp", None, None),
        check_vma=False,
    )
```

```python
import functools
import math

import jax
import jax.numpy as jnp
import numpy as np
from jax import lax
from jax.experimental import pallas as pl
from jax.experimental.pallas import tpu as pltpu
from jax.sharding import PartitionSpec as P

TLX = 12
TLY = 12
LZ = 2
KAPPA = 0.08

LAYER = LZ * TLY
SITES = TLX * LAYER
XROWS = 3 * LAYER
MAIN = TLX * XROWS
BOTH = 2 * XROWS
PADDED = (TLX + 2) * BOTH
WINDOW = 3 * BOTH
SPLIT = 4 * BOTH
EDGE = 4 * XROWS
HEAD = MAIN // 128 * 128
TAIL = MAIN - HEAD + EDGE
LANES = 128
CX, CY, CZ = 0, 18, 36
CYF, CYB, CZS, CZD = 54, 72, 90, 108
VMEM_LIMIT = 12 * 2**20


def call(kernel, outs, scratch=(), flops=0, moved=0, inputs=1, scalars=0, off_chip=0, **kwargs):
    on_chip = pl.BlockSpec(memory_space=pltpu.VMEM)
    first = [pl.BlockSpec(memory_space=pltpu.SMEM)] * scalars + [pl.BlockSpec(memory_space=pltpu.HBM)] * off_chip
    return pl.pallas_call(
        kernel,
        out_shape=outs,
        in_specs=first + [on_chip] * inputs,
        out_specs=jax.tree.map(lambda _: on_chip, outs),
        scratch_shapes=list(scratch),
        compiler_params=pltpu.CompilerParams(vmem_limit_bytes=VMEM_LIMIT),
        cost_estimate=pl.CostEstimate(flops=flops, bytes_accessed=moved, transcendentals=0),
        **kwargs,
    )


def f32(*shape):
    return jax.ShapeDtypeStruct(shape, jnp.float32)


def bf16(*shape):
    return jax.ShapeDtypeStruct(shape, jnp.bfloat16)


def spread(table, column, lanes=LANES):
    return jnp.broadcast_to(table[:, column : column + 1], (table.shape[0], lanes))


def matvec(table, first, field, adjoint=False, acc=None, minus=False):
    out = [[None] * 3, [None] * 3] if acc is None else [list(acc[0]), list(acc[1])]
    lanes = field[0][0].shape[-1]

    def put(part, row, value, negative):
        if negative != minus:
            out[part][row] = -value if out[part][row] is None else out[part][row] - value
        else:
            out[part][row] = value if out[part][row] is None else out[part][row] + value

    for row in range(3):
        for col in range(3):
            at = first + (3 * col + row if adjoint else 3 * row + col)
            real = spread(table, at, lanes)
            imag = spread(table, at + 9, lanes)
            put(0, row, real * field[0][col], False)
            put(0, row, imag * field[1][col], not adjoint)
            put(1, row, real * field[1][col], False)
            put(1, row, imag * field[0][col], adjoint)
    return out


def layer_rows(ref, part, half, first, size=LAYER):
    at = part * XROWS + first
    return ref[half, at : at + size, :]


def grid2(load):
    return [[load(part, colour) for colour in range(3)] for part in range(2)]


def y_rows(part, colour, z, y):
    return pl.ds(BOTH + part * XROWS + colour * LAYER + z * TLY + y, TLX, stride=BOTH)


def send_layers(f_ref, wc_ref, xlo_ref, xhi_ref, ylo_ref, yhi_ref):
    last = TLX * BOTH
    for half in range(f_ref.shape[0]):
        xlo_ref[half] = f_ref[half, BOTH : 2 * BOTH, :]
        for part in range(2):
            for colour in range(3):
                for z in range(LZ):
                    to = part * XROWS + colour * LAYER + z * TLX
                    ylo_ref[half, to : to + TLX, :] = f_ref[half, y_rows(part, colour, z, 0), :]
        table = wc_ref[TLX * LAYER : (TLX + 1) * LAYER, :]
        hop = matvec(table, CX, grid2(lambda p, c: layer_rows(f_ref, p, half, last + c * LAYER)), adjoint=True)
        for part in range(2):
            for colour in range(3):
                to = part * XROWS + colour * LAYER
                xhi_ref[half, to : to + LAYER, :] = hop[part][colour]
        for z in range(LZ):
            table = wc_ref[pl.ds(LAYER + z * TLY + TLY - 1, TLX, stride=LAYER), :]
            hop = matvec(table, CY, grid2(lambda p, c: f_ref[half, y_rows(p, c, z, TLY - 1), :]), adjoint=True)
            for part in range(2):
                for colour in range(3):
                    to = part * XROWS + colour * LAYER + z * TLX
                    yhi_ref[half, to : to + TLX, :] = hop[part][colour]


def clear_ends(ref):
    for half in range(ref.shape[0]):
        ref[half, 0:BOTH, :] = jnp.zeros((BOTH, LANES), jnp.float32)
        ref[half, PADDED - BOTH : PADDED, :] = jnp.zeros((BOTH, LANES), jnp.float32)


def pack_kernel(v_ref, l_ref, fr_ref, wc_ref, xlo_ref, xhi_ref, ylo_ref, yhi_ref, la, lb, ta, tb):
    la[...] = jnp.zeros_like(la)
    lb[...] = jnp.zeros_like(lb)
    plane = SITES // LZ
    la[0:54, 0:SITES] = l_ref[...]
    la[CYF : CYF + 18, 0:SITES] = l_ref[CY : CY + 18, :]
    la[CYB : CYB + 18, 0:SITES] = l_ref[CY : CY + 18, :]
    la[CZS : CZS + 18, 0:SITES] = l_ref[CZ : CZ + 18, :]
    la[CZD : CZD + 18, 0:SITES] = l_ref[CZ : CZ + 18, :]
    for part in range(2):
        for row in range(3):
            for col in range(3):
                k = 9 * part + 3 * row + col
                kt = CZ + 9 * part + 3 * col + row
                value = l_ref[kt : kt + 1, :]
                sign = 1.0 if part == 0 else -1.0
                lb[CZS + k : CZS + k + 1, 0:SITES] = sign * value
                lb[CZD + k : CZD + k + 1, 0:SITES] = -sign * value
    ta[...] = jnp.transpose(la[...])
    tb[...] = jnp.transpose(lb[...])
    raw = ta[0:SITES, :]
    other = jnp.concatenate([tb[plane:SITES, :], tb[0:plane, :]], axis=0)
    y = lax.broadcasted_iota(jnp.int32, (SITES, LANES), 0) % TLY
    column = lax.broadcasted_iota(jnp.int32, (SITES, LANES), 1)
    back = pltpu.roll(raw, 1, 0)
    is_yf = (column >= CYF) & (column < CYB)
    is_yb = (column >= CYB) & (column < CZS)
    table = jnp.where(is_yb, back, raw)
    gone = (is_yf & (y == TLY - 1)) | (is_yb & (y == 0))
    ta[0:SITES, :] = jnp.where(gone, 0.0, table) + other
    wc_ref[0:LAYER, :] = jnp.zeros((LAYER, LANES), jnp.float32)
    clear_ends(fr_ref)
    for x in range(TLX):
        for z in range(LZ):
            src = z * plane + x * TLY
            dst = (x + 1) * LAYER + z * TLY
            wc_ref[dst : dst + TLY, :] = ta[src : src + TLY, :]
            for half in range(fr_ref.shape[0]):
                for part in range(2):
                    for colour in range(3):
                        dst = (x + 1) * BOTH + part * XROWS + colour * LAYER + z * TLY
                        fr_ref[half, dst : dst + TLY, :] = v_ref[
                            3 * part + colour, src : src + TLY, half * LANES : (half + 1) * LANES
                        ]
    send_layers(fr_ref, wc_ref, xlo_ref, xhi_ref, ylo_ref, yhi_ref)


def split(value):
    high = value.astype(jnp.bfloat16)
    return high, (value - high.astype(jnp.float32)).astype(jnp.bfloat16)


def sources(kinds):
    column = np.full((6, len(kinds) * BOTH), -1, np.int32)
    sign = np.zeros((6, len(kinds) * BOTH), np.float32)
    for k, kind in enumerate(kinds):
        if kind is None:
            continue
        first, adjoint, factor, below = kind
        for ri in range(2):
            for row in range(3):
                for rj in range(2):
                    for col in range(3):
                        at = first + (3 * col + row if adjoint else 3 * row + col)
                        weight = 1.0
                        if ri != rj:
                            at += 9
                            weight = -1.0 if (ri == 0) != adjoint else 1.0
                        lanes = slice(k * BOTH + rj * XROWS + col * LAYER, k * BOTH + rj * XROWS + (col + 1) * LAYER)
                        column[3 * ri + row, lanes] = at + (2 * LANES if below else 0)
                        sign[3 * ri + row, lanes] = factor * weight
    return column, sign


def expand(terms, column_ref, sign_ref, block, first, width):
    deep = terms.shape[1] // (2 * LANES)
    row = lax.broadcasted_iota(jnp.int32, (LANES, width), 0)
    column = jnp.broadcast_to(column_ref[block : block + 1, first : first + width], (LANES, width))
    sign = jnp.broadcast_to(sign_ref[block : block + 1, first : first + width], (LANES, width))
    ones = []
    for k in range(deep):
        ones += [jnp.where(row + 2 * k * LANES == column, sign, 0.0).astype(jnp.bfloat16)] * 2
    return dot(terms, jnp.concatenate(ones, axis=0))


def operator_kernel(wc_ref, column_ref, sign_ref, more_ref, moresign_ref, high_ref, low_ref, *, middle, kinds, extra):
    high, low = split(wc_ref[...])
    own, below = slice(LAYER, (TLX + 1) * LAYER), slice(0, TLX * LAYER)
    deep = jnp.concatenate([high[own], low[own], high[below], low[below]], axis=1)
    single = jnp.concatenate([high[own], low[own]], axis=1)
    width = -(-len(kinds) * BOTH // LANES) * LANES
    wide = 2 * LANES

    def mask(first, size, shifts):
        p = lax.broadcasted_iota(jnp.int32, (LAYER, size), 0)
        lane = lax.broadcasted_iota(jnp.int32, (LAYER, size), 1) + first
        q = lane % LAYER
        block = lane // BOTH
        found = None
        for k, shift in enumerate(shifts):
            if shift is not None:
                here = (block == k) & (q == (p + shift if shift != TLY else (p + TLY) % LAYER))
                found = here if found is None else found | here
        return found

    keep = mask(0, width, kinds)
    keeps = [mask(middle, wide, [shift if k == place else None for k in range(len(kinds))]) for place, shift in extra]
    for block in range(6):
        value = expand(deep, column_ref, sign_ref, block, 0, width).reshape(TLX, LAYER, width)
        value = jnp.where(keep[None], value, 0.0)
        center = value[:, :, middle : middle + wide]
        for k in range(len(extra)):
            other = expand(single, more_ref, moresign_ref, block, k * wide, wide).reshape(TLX, LAYER, wide)
            center = center + jnp.where(keeps[k][None], other, 0.0)
        pieces = [value[:, :, :middle], center]
        if middle + wide < width:
            pieces.append(value[:, :, middle + wide :])
        at = 0
        for piece in pieces:
            size = min(piece.shape[2], len(kinds) * BOTH - at)
            if size > 0:
                high, low = split(piece)
                for x in range(TLX):
                    rows = slice(x * BOTH + block * LAYER, x * BOTH + (block + 1) * LAYER)
                    high_ref[rows, at : at + size] = high[x, :, :size]
                    low_ref[rows, at : at + size] = low[x, :, :size]
            at += piece.shape[2]


def split_field(f_ref, high_ref, low_ref, scale=None):
    for half in range(f_ref.shape[0]):
        lanes = slice(half * LANES, (half + 1) * LANES)
        for row in range(0, PADDED, BOTH):
            value = f_ref[half, row : row + BOTH, :]
            high, low = split(value if scale is None else scale * value)
            high_ref[row : row + BOTH, lanes] = high
            low_ref[row : row + BOTH, lanes] = low


def smear_kernel(f_ref, oh_ref, ol_ref, out_ref, fh, fl):
    clear_ends(out_ref)
    split_field(f_ref, fh, fl)
    for x in range(TLX):
        rows = slice(x * BOTH, (x + 1) * BOTH)
        high, low = oh_ref[rows, :], ol_ref[rows, :]
        window = slice(x * BOTH, x * BOTH + WINDOW)
        hops = dot(high, fh[window, :]) + dot(high, fl[window, :]) + dot(low, fh[window, :])
        at = slice((x + 1) * BOTH, (x + 2) * BOTH)
        for half in range(f_ref.shape[0]):
            lanes = slice(half * LANES, (half + 1) * LANES)
            out_ref[half, at, :] = (1.0 - 6.0 * KAPPA) * f_ref[half, at, :] + KAPPA * hops[:, lanes]


def cross(once_ref, wc_ref, rxlo, rxhi, rylo, ryhi, save=None):
    last = TLX * BOTH
    for half in range(once_ref.shape[0]):
        table = wc_ref[TLX * LAYER : (TLX + 1) * LAYER, :]
        hop_x = matvec(table, CX, grid2(lambda p, c: layer_rows(rxhi, p, half, c * LAYER)))
        hop_y = []
        for z in range(LZ):
            table = wc_ref[pl.ds(LAYER + z * TLY + TLY - 1, TLX, stride=LAYER), :]
            hop_y.append(matvec(table, CY, grid2(lambda p, c: layer_rows(ryhi, p, half, c * LAYER + z * TLX, TLX))))
        for part in range(2):
            for colour in range(3):
                at = colour * LAYER
                low = layer_rows(rxlo, part, half, at)
                to = part * XROWS + at
                once_ref[half, BOTH + to : BOTH + to + LAYER, :] += KAPPA * low
                once_ref[half, last + to : last + to + LAYER, :] += KAPPA * hop_x[part][colour]
                if save is not None:
                    save[part, half, at : at + LAYER, :] = low
                    save[part, half, XROWS + at : XROWS + at + LAYER, :] = hop_x[part][colour]
                for z in range(LZ):
                    low = layer_rows(rylo, part, half, at + z * TLX, TLX)
                    rows = y_rows(part, colour, z, 0)
                    once_ref[half, rows, :] = once_ref[half, rows, :] + KAPPA * low
                    rows = y_rows(part, colour, z, TLY - 1)
                    once_ref[half, rows, :] = once_ref[half, rows, :] + KAPPA * hop_y[z][part][colour]
                    if save is not None:
                        to = 2 * XROWS + at + z * TLX
                        save[part, half, to : to + TLX, :] = low
                        save[part, half, to + XROWS : to + XROWS + TLX, :] = hop_y[z][part][colour]


def edge_kernel(part_ref, wc_ref, rxlo, rxhi, rylo, ryhi, once_ref, save, xlo_ref, xhi_ref, ylo_ref, yhi_ref):
    once_ref[...] = part_ref[...]
    cross(once_ref, wc_ref, rxlo, rxhi, rylo, ryhi, save)
    send_layers(once_ref, wc_ref, xlo_ref, xhi_ref, ylo_ref, yhi_ref)


def phased(real, imag, half, lane, at, size, cos_ref, sin_ref, ah_ref, al_ref):
    real, imag = jnp.transpose(real), jnp.transpose(imag)
    halves = ah_ref.shape[0] // cos_ref.shape[0] // LANES
    for m in range(cos_ref.shape[0]):
        cosine = jnp.broadcast_to(cos_ref[m : m + 1, lane : lane + LANES], (LANES, LANES))
        sine = jnp.broadcast_to(sin_ref[m : m + 1, lane : lane + LANES], (LANES, LANES))
        row = (m * halves + half) * LANES
        high, low = split(cosine * real - sine * imag)
        ah_ref[row : row + LANES, at : at + LANES] = high
        al_ref[row : row + LANES, at : at + LANES] = low
        high, low = split(sine * real + cosine * imag)
        ah_ref[row : row + LANES, size + at : size + at + LANES] = high
        al_ref[row : row + LANES, size + at : size + at + LANES] = low


def own_rows(fr_ref, rows, half, first, stop):
    for part in range(2):
        for x in range(first // XROWS, -(-stop // XROWS)):
            low, high = max(first, x * XROWS), min(stop, (x + 1) * XROWS)
            at = (x + 1) * BOTH + part * XROWS + low - x * XROWS
            rows[part, low - first : high - first, :] = fr_ref[half, at : at + high - low, :]


def head_kernel(fr_ref, cos_ref, sin_ref, ah_ref, al_ref, rows):
    for half in range(fr_ref.shape[0]):
        own_rows(fr_ref, rows, half, 0, HEAD)
        for at in range(0, HEAD, LANES):
            real, imag = (rows[p, at : at + LANES, :] for p in range(2))
            phased(real, imag, half, at, at, HEAD, cos_ref, sin_ref, ah_ref, al_ref)


def tail_kernel(fr_ref, save, cos_ref, sin_ref, ah_ref, al_ref, rows):
    for half in range(fr_ref.shape[0]):
        own_rows(fr_ref, rows, half, HEAD, MAIN)
        for part in range(2):
            rows[part, MAIN - HEAD : TAIL, :] = save[part, half]
        for at in range(0, TAIL, LANES):
            real, imag = (rows[p, at : at + LANES, :] for p in range(2))
            phased(real, imag, half, HEAD + at, at, TAIL, cos_ref, sin_ref, ah_ref, al_ref)


def displace_kernel(part_ref, wc_ref, oh_ref, ol_ref, rxlo, rxhi, rylo, ryhi, dir_ref, sh_ref, sl_ref, th_ref, tl_ref, twice, shift, fh, fl, *, scale):
    twice[...] = part_ref[...]
    cross(twice, wc_ref, rxlo, rxhi, rylo, ryhi)
    halves = range(twice.shape[0])
    width = len(halves) * LANES

    def along(which, lanes, rows):
        return jnp.broadcast_to(dir_ref[0:1, lanes], (rows, lanes.stop - lanes.start)) == which

    for half in halves:
        lanes = slice(half * LANES, (half + 1) * LANES)
        for row in range(0, PADDED, BOTH):
            value = scale * twice[half, row : row + BOTH, :]
            for which in range(3):
                high, low = split(jnp.where(along(which, lanes, BOTH), value, 0.0))
                fh[which, row : row + BOTH, lanes] = high
                fl[which, row : row + BOTH, lanes] = low
    for x in range(TLX):
        rows = slice(x * BOTH, (x + 1) * BOTH)
        low, mid, top = (slice((x + k) * BOTH, (x + k + 1) * BOTH) for k in range(3))

        def columns(ref):
            return jnp.concatenate([ref[0, low, :], ref[0, top, :], ref[1, mid, :], ref[2, mid, :]], axis=0)

        fields, rest = columns(fh), columns(fl)
        weights = oh_ref[rows, :]
        value = dot(weights, fields) + dot(weights, rest) + dot(ol_ref[rows, :], fields)
        for part in range(2):
            shift[part, x * XROWS : (x + 1) * XROWS, :] = value[part * XROWS : (part + 1) * XROWS]
    last = TLX * BOTH
    for half in halves:
        lanes = slice(half * LANES, (half + 1) * LANES)
        mask_x = jnp.where(along(0, lanes, XROWS), scale, 0.0)
        mask_y = jnp.where(along(1, lanes, TLX), scale, 0.0)
        for part in range(2):
            at = part * XROWS
            shift[part, MAIN : MAIN + XROWS, lanes] = mask_x * twice[half, BOTH + at : BOTH + at + XROWS, :]
            shift[part, MAIN + XROWS : MAIN + 2 * XROWS, lanes] = -mask_x * twice[half, last + at : last + at + XROWS, :]
            for colour in range(3):
                for z in range(LZ):
                    to = MAIN + 2 * XROWS + colour * LAYER + z * TLX
                    shift[part, to : to + TLX, lanes] = mask_y * twice[half, y_rows(part, colour, z, 0), :]
                    to += XROWS
                    shift[part, to : to + TLX, lanes] = -mask_y * twice[half, y_rows(part, colour, z, TLY - 1), :]
    for high_ref, low_ref, first, size in ((sh_ref, sl_ref, 0, HEAD), (th_ref, tl_ref, HEAD, TAIL)):
        real, imag = slice(0, width), slice(width, 2 * width)
        for row in range(0, size, 128):
            top = slice(row, row + 128)
            bottom = slice(size + row, size + row + 128)
            high, low = split(shift[0, first + row : first + row + 128, :])
            high_ref[top, real] = high
            low_ref[top, real] = low
            high_ref[bottom, imag] = -high
            low_ref[bottom, imag] = -low
            high, low = split(shift[1, first + row : first + row + 128, :])
            high_ref[bottom, real] = high
            low_ref[bottom, real] = low
            high_ref[top, imag] = high
            low_ref[top, imag] = low


def dot(a, b):
    return jnp.dot(a, b, preferred_element_type=jnp.float32)


def meson_kernel(ah, al, bh, bl, sh, sl, th, tl, out_ref):
    total = dot(ah[...], sh[...]) + dot(ah[...], sl[...]) + dot(al[...], sh[...])
    out_ref[...] = total + dot(bh[...], th[...]) + dot(bh[...], tl[...]) + dot(bl[...], th[...])


def product(blocks, moments, refs):
    ah, al, bh, bl, sh, sl, th, tl = refs
    nev = ah.shape[0] // moments
    size = blocks[1]

    def rows(ref):
        picked = [ref[pl.ds(pl.multiple_of(m * nev + b, size), size), :] for m in range(moments) for b in blocks[0]]
        return jnp.concatenate(picked, axis=0)

    ahv, alv, bhv, blv = rows(ah), rows(al), rows(bh), rows(bl)
    total = dot(ahv, sh[...]) + dot(ahv, sl[...]) + dot(alv, sh[...])
    return total + dot(bhv, th[...]) + dot(bhv, tl[...]) + dot(blv, th[...])


def put(out_ref, value, count, moments, added=None):
    size, width = out_ref.shape[1], value.shape[-1]
    for m in range(moments):
        for k in range(count):
            block = value[(m * count + k) * size : (m * count + k + 1) * size]
            lanes = slice(m * width, (m + 1) * width)
            if added is not None:
                block = block + added(k, lanes)
            out_ref[k, :, lanes] = block


def owners(groups, size, cores, turns):
    position = lax.axis_index("site")
    core, y, z = position % 2, position // 2 % 2, position // 4
    core = (core + cores) % 2
    return [((z + g) % groups * 4 + (y + turn) % 2 * 2 + core) * size for g in range(groups) for turn in turns]


def piece_kernel(*refs, moments, groups, cores, turns):
    out_ref = refs[-1]
    size = out_ref.shape[1]
    blocks = owners(groups, size, cores, turns)
    put(out_ref, product((blocks, size), moments, refs[:-1]), len(blocks), moments)


def merge_kernel(mine, theirs, *outs, picks):
    for out_ref, pairs in zip(outs, picks):
        for k, (a, b) in enumerate(pairs):
            out_ref[k] = mine[a] + theirs[b]


def phases(momenta, position, devices, tiles):
    site = np.arange(SITES)
    x, zy = site // LAYER, site % LAYER
    own = [np.repeat(a.reshape(TLX, 1, LAYER), 3, 1).reshape(-1) for a in (x, zy % TLY, zy // TLY)]
    edge = np.arange(LAYER)
    full = np.full(LAYER, 0)
    edges = (
        (full + TLX - 1, edge % TLY, edge // TLY),
        (full, edge % TLY, edge // TLY),
        (edge % TLX, full + TLY - 1, edge // TLX),
        (edge % TLX, full, edge // TLX),
    )
    steps = (-tiles, tiles, -1, 1)
    xs, ys, zs, move = own[0], own[1], own[2], np.zeros(MAIN, np.int64)
    for step, (ex, ey, ez) in zip(steps, edges):
        xs = np.concatenate([xs] + [ex] * 3)
        ys = np.concatenate([ys] + [ey] * 3)
        zs = np.concatenate([zs] + [ez] * 3)
        move = np.concatenate([move, np.full(XROWS, step)])
    tile = (position + jnp.asarray(move, jnp.int32) + devices) % devices
    lx, ly = TLX * tiles, TLY * tiles
    sx = (tile // tiles) * TLX + jnp.asarray(xs, jnp.int32)
    sy = (tile % tiles) * TLY + jnp.asarray(ys, jnp.int32)
    sz = jnp.asarray(zs, jnp.int32)
    frac = (momenta[:, 0:1] * sx % lx).astype(jnp.float32) / lx
    frac = frac + (momenta[:, 1:2] * sy % ly).astype(jnp.float32) / ly
    frac = frac + (momenta[:, 2:3] * sz % LZ).astype(jnp.float32) / LZ
    theta = 2.0 * math.pi * frac
    return jnp.cos(theta), jnp.sin(theta)


def send(block, devices, distance):
    return lax.ppermute(block, "site", [(i, (i + distance) % devices) for i in range(devices)])


def halo(sends, devices, tiles):
    xlo, xhi, ylo, yhi = sends
    return (
        send(xhi, devices, tiles),
        send(xlo, devices, -tiles),
        send(yhi, devices, 1),
        send(ylo, devices, -1),
    )


def stages(devices):
    found, stride = [], 1
    while stride < devices:
        left = devices // stride
        size = 2 if stride < 4 else 4 if left % 4 == 0 else 2
        found.append((stride, size))
        stride *= size
    return found


def scatter_sum(block, position, devices):
    shape = block.shape[1:]
    for stride, size in stages(devices):
        left = block.shape[0] // size
        block = block.reshape((left, size) + shape)
        mine = (position // stride) % size
        total = lax.dynamic_index_in_dim(block, mine, 1, keepdims=False)
        for step in range(1, size):
            other = (mine + step) % size
            out = lax.dynamic_index_in_dim(block, other, 1, keepdims=False)
            route = []
            for i in range(devices):
                digit = (i // stride) % size
                route.append((i, i + ((digit + step) % size - digit) * stride))
            total = total + lax.ppermute(out, "site", route)
        block = total
    return block[0]


def on_device(vectors, links, momenta, directions):
    devices = lax.axis_size("site")
    tiles = math.isqrt(devices)
    position = lax.axis_index("site")
    nev = vectors.shape[-1]
    moments = momenta.shape[0]
    field = vectors.reshape(6, SITES, nev)
    table = links.reshape(54, SITES)
    halves = nev // LANES
    layer = f32(halves, BOTH, LANES)
    padded = f32(halves, PADDED, LANES)
    fr, wc, *sends = call(
        pack_kernel,
        (padded, f32((TLX + 1) * LAYER, LANES), layer, layer, layer, layer),
        [pltpu.VMEM((128, 384), jnp.float32)] * 2 + [pltpu.VMEM((384, 128), jnp.float32)] * 2,
        inputs=2,
    )(field, table)
    received = halo(sends, devices, tiles)
    flops = 2 * 180 * 2 * SITES * nev
    smear = operator(
        wc,
        kinds=((CX, True, 1.0, True), (CYF, False, 1.0, False), (CX, False, 1.0, False)),
        shifts=(0, 1, 0),
        extra=((1, CYB, True, 1.0, -1), (1, CZS, False, 1.0, TLY)),
        middle=LANES,
    )
    pair = [pltpu.VMEM((PADDED, nev), jnp.bfloat16)] * 2
    once = call(smear_kernel, padded, pair, flops, 3 << 20, 3)(fr, *smear)
    cosine, sine = phases(momenta, position, devices, tiles)
    head = bf16(moments * nev, 2 * HEAD)
    tail = bf16(moments * nev, 2 * TAIL)
    rows = pltpu.VMEM((2, HEAD, LANES), jnp.float32)
    ah, al = call(head_kernel, (head, head), [rows], flops, 8 << 20, 3)(fr, cosine, sine)
    displace = operator(
        wc,
        kinds=((CX, True, -1.0, True), (CX, False, 1.0, False), (CYF, False, 1.0, False), (CZD, False, 1.0, False)),
        shifts=(0, 0, 1, TLY),
        extra=((2, CYB, True, -1.0, -1),),
        middle=2 * LANES,
    )
    edges = f32(2, halves, EDGE, LANES)
    once, save, *sends = call(edge_kernel, (padded, edges, layer, layer, layer, layer), inputs=6)(once, wc, *received)
    received = halo(sends, devices, tiles)
    twice = call(smear_kernel, padded, pair, flops, 3 << 20, 3)(once, *smear)
    rows = pltpu.VMEM((2, TAIL, LANES), jnp.float32)
    bh, bl = call(tail_kernel, (tail, tail), [rows], flops, 4 << 20, 4)(fr, save, cosine, sine)
    scale = 1.0 / math.sqrt(3.0 * TLX * tiles * TLY * tiles * LZ)
    operands = call(
        functools.partial(displace_kernel, scale=scale),
        (bf16(2 * HEAD, 2 * nev), bf16(2 * HEAD, 2 * nev), bf16(2 * TAIL, 2 * nev), bf16(2 * TAIL, 2 * nev)),
        [
            pltpu.VMEM((halves, PADDED, LANES), jnp.float32),
            pltpu.VMEM((2, HEAD + TAIL, nev), jnp.float32),
        ]
        + [pltpu.VMEM((3, PADDED, nev), jnp.bfloat16)] * 2,
        inputs=9,
    )(twice, wc, *displace, *received, directions[None, :])
    operands = (ah, al, bh, bl) + tuple(operands)
    size, columns = nev // devices, moments * 2 * nev
    if size % 16 == 0 and devices % 8 == 0:
        total = pieces(operands, position, devices, moments, size, columns)
    else:
        total = whole_product(operands, position, devices, moments, nev)
    return total.reshape(size, moments, 2, nev)


def operator(wc, kinds, shifts, extra, middle):
    lanes = len(kinds) * BOTH
    width = -(-lanes // LANES) * LANES
    column, sign = sources(kinds)
    column = np.pad(column, ((0, 0), (0, width - lanes)), constant_values=-1)
    sign = np.pad(sign, ((0, 0), (0, width - lanes)))
    more, moresign = [], []
    for place, first, adjoint, factor, _ in extra:
        c, w = sources([(first, adjoint, factor, False) if k == place else None for k in range(len(kinds))])
        c = np.pad(c, ((0, 0), (0, width - lanes)), constant_values=-1)
        w = np.pad(w, ((0, 0), (0, width - lanes)))
        more.append(c[:, middle : middle + 2 * LANES])
        moresign.append(w[:, middle : middle + 2 * LANES])
    kernel = functools.partial(
        operator_kernel, middle=middle, kinds=shifts, extra=[(place, shift) for place, _, _, _, shift in extra]
    )
    out = bf16(TLX * BOTH, lanes)
    tables = (column, sign, np.concatenate(more, 1), np.concatenate(moresign, 1))
    return call(kernel, (out, out), (), 1 << 30, 4 << 20, 5)(wc, *map(jnp.asarray, tables))


def whole_product(operands, position, devices, moments, nev):
    whole = lambda a: pl.BlockSpec(a.shape, lambda m: (0, 0))
    partial = pl.pallas_call(
        meson_kernel,
        out_shape=f32(nev, moments * 2 * nev),
        grid=(moments,),
        in_specs=[pl.BlockSpec((nev, a.shape[1]), lambda m: (m, 0)) for a in operands[:4]]
        + [whole(a) for a in operands[4:]],
        out_specs=pl.BlockSpec((nev, 2 * nev), lambda m: (0, m)),
        compiler_params=pltpu.CompilerParams(vmem_limit_bytes=40 * 2**20),
    )(*operands)
    return scatter_sum(partial.reshape(devices, nev // devices, moments * 2 * nev), position, devices)


def pieces(operands, position, devices, moments, size, columns):
    groups = devices // 4
    shared = dict(moments=moments, groups=groups)
    cost = dict(flops=2 * 3 * size * groups * moments * 4 * (HEAD + TAIL) * 256, moved=1 << 20)
    block = lambda count: f32(count, size, columns)
    out = call(
        functools.partial(piece_kernel, cores=1, turns=(0, 1), **shared), block(2 * groups), (), inputs=8, **cost
    )(*operands)
    swapped = lax.ppermute(out, "site", [(i, i ^ 1) for i in range(devices)])
    far = call(
        functools.partial(piece_kernel, cores=0, turns=(1,), **shared), block(groups), (), inputs=8, **cost
    )(*operands)
    early = list(range(1, groups // 2 + 1))
    late = list(range(groups // 2 + 1, groups)) + [0]
    first, second = call(
        functools.partial(merge_kernel, picks=[[(g, 2 * g + 1) for g in early], [(g, 2 * g + 1) for g in late]]),
        (block(len(early)), block(len(late))),
        inputs=2,
    )(far, swapped)
    flip = [(i, i ^ 2) for i in range(devices)]
    first = lax.ppermute(first, "site", flip)
    second = lax.ppermute(second, "site", flip)
    near = call(
        functools.partial(piece_kernel, cores=0, turns=(0,), **shared), block(groups), (), inputs=8, **cost
    )(*operands)
    near = call(
        functools.partial(merge_kernel, picks=[[(g, 2 * g) for g in range(groups)]]), (block(groups),), inputs=2
    )(near, swapped)[0]
    total = None
    arrived = []
    for steps, got in ((early, first), (late, second)):
        sums = call(
            functools.partial(merge_kernel, picks=[[(g, k)] for k, g in enumerate(steps)]),
            tuple(block(1) for _ in steps),
            inputs=2,
        )(near, got)
        for step, value in zip(steps, sums):
            if step == 0:
                total = value
            else:
                arrived.append(lax.ppermute(value, "site", [(i, (i + 4 * step) % devices) for i in range(devices)]))
    for value in arrived:
        total = total + value
    return total[0]


def solution(mesh):
    placed = (
        P("grp", None, "site", None, None),
        P("grp", None, None, None, "site", None),
        P(),
        P(),
    )
    return jax.shard_map(
        on_device,
        mesh=mesh,
        in_specs=placed,
        out_specs=P("site", "grp", None, None),
        check_vma=False,
    )
```

```python
import functools
import math

import jax
import jax.numpy as jnp
import numpy as np
from jax import lax
from jax.experimental import pallas as pl
from jax.experimental.pallas import tpu as pltpu
from jax.sharding import PartitionSpec as P


TLX = 12
TLY = 12
LZ = 2
KAPPA = 0.08

LAYER = LZ * TLY
SITES = TLX * LAYER
XROWS = 3 * LAYER
MAIN = TLX * XROWS
BOTH = 2 * XROWS
PADDED = (TLX + 2) * BOTH
WINDOW = 3 * BOTH
EDGE = 4 * XROWS
HEAD = MAIN // 128 * 128
TAIL = MAIN - HEAD + EDGE
LANES = 128
CX, CY, CZ = 0, 18, 36
CYF, CYB, CZS, CZD = 54, 72, 90, 108
VMEM_LIMIT = 12 * 2**20


def call(kernel, outs, scratch=(), flops=0, moved=0, inputs=1, scalars=0, off_chip=0, **kwargs):
    on_chip = pl.BlockSpec(memory_space=pltpu.VMEM)
    first = [pl.BlockSpec(memory_space=pltpu.SMEM)] * scalars + [pl.BlockSpec(memory_space=pltpu.HBM)] * off_chip
    return pl.pallas_call(
        kernel,
        out_shape=outs,
        in_specs=first + [on_chip] * inputs,
        out_specs=jax.tree.map(lambda _: on_chip, outs),
        scratch_shapes=list(scratch),
        compiler_params=pltpu.CompilerParams(vmem_limit_bytes=VMEM_LIMIT),
        cost_estimate=pl.CostEstimate(flops=flops, bytes_accessed=moved, transcendentals=0),
        **kwargs,
    )


def f32(*shape):
    return jax.ShapeDtypeStruct(shape, jnp.float32)


def bf16(*shape):
    return jax.ShapeDtypeStruct(shape, jnp.bfloat16)


def spread(table, column, lanes=LANES):
    return jnp.broadcast_to(table[:, column : column + 1], (table.shape[0], lanes))


def matvec(table, first, field, adjoint=False, acc=None, minus=False):
    out = [[None] * 3, [None] * 3] if acc is None else [list(acc[0]), list(acc[1])]
    lanes = field[0][0].shape[-1]

    def put(part, row, value, negative):
        if negative != minus:
            out[part][row] = -value if out[part][row] is None else out[part][row] - value
        else:
            out[part][row] = value if out[part][row] is None else out[part][row] + value

    for row in range(3):
        for col in range(3):
            at = first + (3 * col + row if adjoint else 3 * row + col)
            real = spread(table, at, lanes)
            imag = spread(table, at + 9, lanes)
            put(0, row, real * field[0][col], False)
            put(0, row, imag * field[1][col], not adjoint)
            put(1, row, real * field[1][col], False)
            put(1, row, imag * field[0][col], adjoint)
    return out


def layer_rows(ref, part, half, first, size=LAYER):
    at = part * XROWS + first
    return ref[half, at : at + size, :]


def grid2(load):
    return [[load(part, colour) for colour in range(3)] for part in range(2)]


def y_rows(part, colour, z, y):
    return pl.ds(BOTH + part * XROWS + colour * LAYER + z * TLY + y, TLX, stride=BOTH)


def parity(tiles):
    position = lax.axis_index("site")
    return position // tiles % 2 == 0, position % 2 == 0


def send_layers(f_ref, wc_ref, ax_ref, bx_ref, ay_ref, by_ref, tiles):
    last = TLX * BOTH
    even_x, even_y = parity(tiles)
    for half in range(f_ref.shape[0]):
        table = wc_ref[TLX * LAYER : (TLX + 1) * LAYER, :]
        hop = matvec(table, CX, grid2(lambda p, c: layer_rows(f_ref, p, half, last + c * LAYER)), adjoint=True)
        for part in range(2):
            for colour in range(3):
                to = part * XROWS + colour * LAYER
                low, high = f_ref[half, BOTH + to : BOTH + to + LAYER, :], hop[part][colour]
                ax_ref[half, to : to + LAYER, :] = jnp.where(even_x, high, low)
                bx_ref[half, to : to + LAYER, :] = jnp.where(even_x, low, high)
        for z in range(LZ):
            table = wc_ref[pl.ds(LAYER + z * TLY + TLY - 1, TLX, stride=LAYER), :]
            hop = matvec(table, CY, grid2(lambda p, c: f_ref[half, y_rows(p, c, z, TLY - 1), :]), adjoint=True)
            for part in range(2):
                for colour in range(3):
                    to = part * XROWS + colour * LAYER + z * TLX
                    low, high = f_ref[half, y_rows(part, colour, z, 0), :], hop[part][colour]
                    ay_ref[half, to : to + TLX, :] = jnp.where(even_y, high, low)
                    by_ref[half, to : to + TLX, :] = jnp.where(even_y, low, high)


def clear_ends(ref):
    for half in range(ref.shape[0]):
        ref[half, 0:BOTH, :] = jnp.zeros((BOTH, LANES), jnp.float32)
        ref[half, PADDED - BOTH : PADDED, :] = jnp.zeros((BOTH, LANES), jnp.float32)


def pack_kernel(v_ref, l_ref, fr_ref, wc_ref, ax_ref, bx_ref, ay_ref, by_ref, la, lb, ta, tb, *, tiles):
    la[...] = jnp.zeros_like(la)
    lb[...] = jnp.zeros_like(lb)
    plane = SITES // LZ
    la[0:54, 0:SITES] = l_ref[...]
    la[CYF : CYF + 18, 0:SITES] = l_ref[CY : CY + 18, :]
    la[CYB : CYB + 18, 0:SITES] = l_ref[CY : CY + 18, :]
    la[CZS : CZS + 18, 0:SITES] = l_ref[CZ : CZ + 18, :]
    la[CZD : CZD + 18, 0:SITES] = l_ref[CZ : CZ + 18, :]
    for part in range(2):
        for row in range(3):
            for col in range(3):
                k = 9 * part + 3 * row + col
                kt = CZ + 9 * part + 3 * col + row
                value = l_ref[kt : kt + 1, :]
                sign = 1.0 if part == 0 else -1.0
                lb[CZS + k : CZS + k + 1, 0:SITES] = sign * value
                lb[CZD + k : CZD + k + 1, 0:SITES] = -sign * value
    ta[...] = jnp.transpose(la[...])
    tb[...] = jnp.transpose(lb[...])
    raw = ta[0:SITES, :]
    other = jnp.concatenate([tb[plane:SITES, :], tb[0:plane, :]], axis=0)
    y = lax.broadcasted_iota(jnp.int32, (SITES, LANES), 0) % TLY
    column = lax.broadcasted_iota(jnp.int32, (SITES, LANES), 1)
    back = pltpu.roll(raw, 1, 0)
    is_yf = (column >= CYF) & (column < CYB)
    is_yb = (column >= CYB) & (column < CZS)
    table = jnp.where(is_yb, back, raw)
    gone = (is_yf & (y == TLY - 1)) | (is_yb & (y == 0))
    ta[0:SITES, :] = jnp.where(gone, 0.0, table) + other
    wc_ref[0:LAYER, :] = jnp.zeros((LAYER, LANES), jnp.float32)
    clear_ends(fr_ref)
    for x in range(TLX):
        for z in range(LZ):
            src = z * plane + x * TLY
            dst = (x + 1) * LAYER + z * TLY
            wc_ref[dst : dst + TLY, :] = ta[src : src + TLY, :]
            for half in range(fr_ref.shape[0]):
                for part in range(2):
                    for colour in range(3):
                        dst = (x + 1) * BOTH + part * XROWS + colour * LAYER + z * TLY
                        fr_ref[half, dst : dst + TLY, :] = v_ref[
                            3 * part + colour, src : src + TLY, half * LANES : (half + 1) * LANES
                        ]
    send_layers(fr_ref, wc_ref, ax_ref, bx_ref, ay_ref, by_ref, tiles)


def split(value):
    high = value.astype(jnp.bfloat16)
    return high, (value - high.astype(jnp.float32)).astype(jnp.bfloat16)


def sources(kinds):
    column = np.full((6, len(kinds) * BOTH), -1, np.int32)
    sign = np.zeros((6, len(kinds) * BOTH), np.float32)
    for k, kind in enumerate(kinds):
        if kind is None:
            continue
        first, adjoint, factor, below = kind
        for ri in range(2):
            for row in range(3):
                for rj in range(2):
                    for col in range(3):
                        at = first + (3 * col + row if adjoint else 3 * row + col)
                        weight = 1.0
                        if ri != rj:
                            at += 9
                            weight = -1.0 if (ri == 0) != adjoint else 1.0
                        lanes = slice(k * BOTH + rj * XROWS + col * LAYER, k * BOTH + rj * XROWS + (col + 1) * LAYER)
                        column[3 * ri + row, lanes] = at + (2 * LANES if below else 0)
                        sign[3 * ri + row, lanes] = factor * weight
    return column, sign


def expand(terms, column_ref, sign_ref, block, first, width):
    deep = terms.shape[1] // (2 * LANES)
    row = lax.broadcasted_iota(jnp.int32, (LANES, width), 0)
    column = jnp.broadcast_to(column_ref[block : block + 1, first : first + width], (LANES, width))
    sign = jnp.broadcast_to(sign_ref[block : block + 1, first : first + width], (LANES, width))
    ones = []
    for k in range(deep):
        ones += [jnp.where(row + 2 * k * LANES == column, sign, 0.0).astype(jnp.bfloat16)] * 2
    return dot(terms, jnp.concatenate(ones, axis=0))


def operator_kernel(wc_ref, column_ref, sign_ref, more_ref, moresign_ref, high_ref, low_ref, *, middle, kinds, extra):
    high, low = split(wc_ref[...])
    own, below = slice(LAYER, (TLX + 1) * LAYER), slice(0, TLX * LAYER)
    deep = jnp.concatenate([high[own], low[own], high[below], low[below]], axis=1)
    single = jnp.concatenate([high[own], low[own]], axis=1)
    width = -(-len(kinds) * BOTH // LANES) * LANES
    wide = 2 * LANES

    def mask(first, size, shifts):
        p = lax.broadcasted_iota(jnp.int32, (LAYER, size), 0)
        lane = lax.broadcasted_iota(jnp.int32, (LAYER, size), 1) + first
        q = lane % LAYER
        block = lane // BOTH
        found = None
        for k, shift in enumerate(shifts):
            if shift is not None:
                here = (block == k) & (q == (p + shift if shift != TLY else (p + TLY) % LAYER))
                found = here if found is None else found | here
        return found

    keep = mask(0, width, kinds)
    keeps = [mask(middle, wide, [shift if k == place else None for k in range(len(kinds))]) for place, shift in extra]
    for block in range(6):
        value = expand(deep, column_ref, sign_ref, block, 0, width).reshape(TLX, LAYER, width)
        value = jnp.where(keep[None], value, 0.0)
        center = value[:, :, middle : middle + wide]
        for k in range(len(extra)):
            other = expand(single, more_ref, moresign_ref, block, k * wide, wide).reshape(TLX, LAYER, wide)
            center = center + jnp.where(keeps[k][None], other, 0.0)
        pieces = [value[:, :, :middle], center]
        if middle + wide < width:
            pieces.append(value[:, :, middle + wide :])
        at = 0
        for piece in pieces:
            size = min(piece.shape[2], len(kinds) * BOTH - at)
            if size > 0:
                high, low = split(piece)
                for x in range(TLX):
                    rows = slice(x * BOTH + block * LAYER, x * BOTH + (block + 1) * LAYER)
                    high_ref[rows, at : at + size] = high[x, :, :size]
                    low_ref[rows, at : at + size] = low[x, :, :size]
            at += piece.shape[2]


def split_field(f_ref, high_ref, low_ref, scale=None):
    for half in range(f_ref.shape[0]):
        lanes = slice(half * LANES, (half + 1) * LANES)
        for row in range(0, PADDED, BOTH):
            value = f_ref[half, row : row + BOTH, :]
            high, low = split(value if scale is None else scale * value)
            high_ref[row : row + BOTH, lanes] = high
            low_ref[row : row + BOTH, lanes] = low


def smear_kernel(f_ref, oh_ref, ol_ref, out_ref, fh, fl):
    clear_ends(out_ref)
    split_field(f_ref, fh, fl)
    for x in range(TLX):
        rows = slice(x * BOTH, (x + 1) * BOTH)
        high, low = oh_ref[rows, :], ol_ref[rows, :]
        window = slice(x * BOTH, x * BOTH + WINDOW)
        hops = dot(high, fh[window, :]) + dot(high, fl[window, :]) + dot(low, fh[window, :])
        at = slice((x + 1) * BOTH, (x + 2) * BOTH)
        for half in range(f_ref.shape[0]):
            lanes = slice(half * LANES, (half + 1) * LANES)
            out_ref[half, at, :] = (1.0 - 6.0 * KAPPA) * f_ref[half, at, :] + KAPPA * hops[:, lanes]


def cross(once_ref, wc_ref, received, tiles, save=None):
    last = TLX * BOTH
    even_x, even_y = parity(tiles)
    ax, bx, ay, by = received

    def arrived(above, half, part, first, size, along_y):
        one, two, even = (ay, by, even_y) if along_y else (ax, bx, even_x)
        values = (layer_rows(ref, part, half, first, size) for ref in ((one, two) if above else (two, one)))
        return jnp.where(even, *values)

    for half in range(once_ref.shape[0]):
        table = wc_ref[TLX * LAYER : (TLX + 1) * LAYER, :]
        hop_x = matvec(table, CX, grid2(lambda p, c: arrived(True, half, p, c * LAYER, LAYER, False)))
        hop_y = []
        for z in range(LZ):
            table = wc_ref[pl.ds(LAYER + z * TLY + TLY - 1, TLX, stride=LAYER), :]
            hop_y.append(
                matvec(table, CY, grid2(lambda p, c: arrived(True, half, p, c * LAYER + z * TLX, TLX, True)))
            )
        for part in range(2):
            for colour in range(3):
                at = colour * LAYER
                low = arrived(False, half, part, at, LAYER, False)
                to = part * XROWS + at
                once_ref[half, BOTH + to : BOTH + to + LAYER, :] += KAPPA * low
                once_ref[half, last + to : last + to + LAYER, :] += KAPPA * hop_x[part][colour]
                if save is not None:
                    save[part, half, at : at + LAYER, :] = low
                    save[part, half, XROWS + at : XROWS + at + LAYER, :] = hop_x[part][colour]
                for z in range(LZ):
                    low = arrived(False, half, part, at + z * TLX, TLX, True)
                    rows = y_rows(part, colour, z, 0)
                    once_ref[half, rows, :] = once_ref[half, rows, :] + KAPPA * low
                    rows = y_rows(part, colour, z, TLY - 1)
                    once_ref[half, rows, :] = once_ref[half, rows, :] + KAPPA * hop_y[z][part][colour]
                    if save is not None:
                        to = 2 * XROWS + at + z * TLX
                        save[part, half, to : to + TLX, :] = low
                        save[part, half, to + XROWS : to + XROWS + TLX, :] = hop_y[z][part][colour]


def edge_kernel(part_ref, wc_ref, rax, rbx, ray, rby, *refs, tiles):
    once_ref, save, ax_ref, bx_ref, ay_ref, by_ref = refs[-6:]
    once_ref[...] = part_ref[...]
    cross(once_ref, wc_ref, (rax, rbx, ray, rby), tiles, save)
    send_layers(once_ref, wc_ref, ax_ref, bx_ref, ay_ref, by_ref, tiles)


def phased(real, imag, half, lane, at, size, cos_ref, sin_ref, ah_ref, al_ref):
    real, imag = jnp.transpose(real), jnp.transpose(imag)
    halves = ah_ref.shape[0] // cos_ref.shape[0] // LANES
    for m in range(cos_ref.shape[0]):
        cosine = jnp.broadcast_to(cos_ref[m : m + 1, lane : lane + LANES], (LANES, LANES))
        sine = jnp.broadcast_to(sin_ref[m : m + 1, lane : lane + LANES], (LANES, LANES))
        row = (m * halves + half) * LANES
        high, low = split(cosine * real - sine * imag)
        ah_ref[row : row + LANES, at : at + LANES] = high
        al_ref[row : row + LANES, at : at + LANES] = low
        high, low = split(sine * real + cosine * imag)
        ah_ref[row : row + LANES, size + at : size + at + LANES] = high
        al_ref[row : row + LANES, size + at : size + at + LANES] = low


def own_rows(fr_ref, rows, half, first, stop):
    for part in range(2):
        for x in range(first // XROWS, -(-stop // XROWS)):
            low, high = max(first, x * XROWS), min(stop, (x + 1) * XROWS)
            at = (x + 1) * BOTH + part * XROWS + low - x * XROWS
            rows[part, low - first : high - first, :] = fr_ref[half, at : at + high - low, :]


def head_kernel(fr_ref, cos_ref, sin_ref, ah_ref, al_ref, rows):
    for half in range(fr_ref.shape[0]):
        own_rows(fr_ref, rows, half, 0, HEAD)
        for at in range(0, HEAD, LANES):
            real, imag = (rows[p, at : at + LANES, :] for p in range(2))
            phased(real, imag, half, at, at, HEAD, cos_ref, sin_ref, ah_ref, al_ref)


def tail_kernel(fr_ref, save, cos_ref, sin_ref, ah_ref, al_ref, rows):
    for half in range(fr_ref.shape[0]):
        own_rows(fr_ref, rows, half, HEAD, MAIN)
        for part in range(2):
            rows[part, MAIN - HEAD : TAIL, :] = save[part, half]
        for at in range(0, TAIL, LANES):
            real, imag = (rows[p, at : at + LANES, :] for p in range(2))
            phased(real, imag, half, HEAD + at, at, TAIL, cos_ref, sin_ref, ah_ref, al_ref)


def displace_kernel(
    part_ref, wc_ref, oh_ref, ol_ref, rax, rbx, ray, rby, dir_ref, *refs, scale, tiles
):
    sh_ref, sl_ref, th_ref, tl_ref, twice, shift, fh, fl = refs[-8:]
    twice[...] = part_ref[...]
    cross(twice, wc_ref, (rax, rbx, ray, rby), tiles)
    halves = range(twice.shape[0])
    width = len(halves) * LANES

    def along(which, lanes, rows):
        return jnp.broadcast_to(dir_ref[0:1, lanes], (rows, lanes.stop - lanes.start)) == which

    for half in halves:
        lanes = slice(half * LANES, (half + 1) * LANES)
        masks = [jnp.where(along(which, lanes, BOTH), 1.0, 0.0).astype(jnp.bfloat16) for which in range(3)]
        for row in range(0, PADDED, BOTH):
            high, low = split(scale * twice[half, row : row + BOTH, :])
            for which in range(3):
                fh[which, row : row + BOTH, lanes] = high * masks[which]
                fl[which, row : row + BOTH, lanes] = low * masks[which]
    for x in range(TLX):
        rows = slice(x * BOTH, (x + 1) * BOTH)
        low, mid, top = (slice((x + k) * BOTH, (x + k + 1) * BOTH) for k in range(3))

        def columns(ref):
            return jnp.concatenate([ref[0, low, :], ref[0, top, :], ref[1, mid, :], ref[2, mid, :]], axis=0)

        fields, rest = columns(fh), columns(fl)
        weights = oh_ref[rows, :]
        value = dot(weights, fields) + dot(weights, rest) + dot(ol_ref[rows, :], fields)
        for part in range(2):
            shift[part, x * XROWS : (x + 1) * XROWS, :] = value[part * XROWS : (part + 1) * XROWS]
    last = TLX * BOTH
    for half in halves:
        lanes = slice(half * LANES, (half + 1) * LANES)
        mask_x = jnp.where(along(0, lanes, XROWS), scale, 0.0)
        mask_y = jnp.where(along(1, lanes, TLX), scale, 0.0)
        for part in range(2):
            at = part * XROWS
            shift[part, MAIN : MAIN + XROWS, lanes] = mask_x * twice[half, BOTH + at : BOTH + at + XROWS, :]
            shift[part, MAIN + XROWS : MAIN + 2 * XROWS, lanes] = -mask_x * twice[half, last + at : last + at + XROWS, :]
            for colour in range(3):
                for z in range(LZ):
                    to = MAIN + 2 * XROWS + colour * LAYER + z * TLX
                    shift[part, to : to + TLX, lanes] = mask_y * twice[half, y_rows(part, colour, z, 0), :]
                    to += XROWS
                    shift[part, to : to + TLX, lanes] = -mask_y * twice[half, y_rows(part, colour, z, TLY - 1), :]
    for high_ref, low_ref, first, size in ((sh_ref, sl_ref, 0, HEAD), (th_ref, tl_ref, HEAD, TAIL)):
        real, imag = slice(0, width), slice(width, 2 * width)
        for row in range(0, size, 128):
            top = slice(row, row + 128)
            bottom = slice(size + row, size + row + 128)
            high, low = split(shift[0, first + row : first + row + 128, :])
            high_ref[top, real] = high
            low_ref[top, real] = low
            high_ref[bottom, imag] = -high
            low_ref[bottom, imag] = -low
            high, low = split(shift[1, first + row : first + row + 128, :])
            high_ref[bottom, real] = high
            low_ref[bottom, real] = low
            high_ref[top, imag] = high
            low_ref[top, imag] = low


def dot(a, b):
    return jnp.dot(a, b, preferred_element_type=jnp.float32)


def meson_kernel(ah, al, bh, bl, sh, sl, th, tl, out_ref):
    total = dot(ah[...], sh[...]) + dot(ah[...], sl[...]) + dot(al[...], sh[...])
    out_ref[...] = total + dot(bh[...], th[...]) + dot(bh[...], tl[...]) + dot(bl[...], th[...])


def product(blocks, moments, refs):
    ah, al, bh, bl, sh, sl, th, tl = refs
    nev = ah.shape[0] // moments
    size = blocks[1]

    def rows(ref):
        picked = [ref[pl.ds(pl.multiple_of(m * nev + b, size), size), :] for m in range(moments) for b in blocks[0]]
        return jnp.concatenate(picked, axis=0)

    ahv, alv, bhv, blv = rows(ah), rows(al), rows(bh), rows(bl)
    total = dot(ahv, sh[...]) + dot(ahv, sl[...]) + dot(alv, sh[...])
    return total + dot(bhv, th[...]) + dot(bhv, tl[...]) + dot(blv, th[...])


def put(out_ref, value, count, moments, added=None):
    size, width = out_ref.shape[1], value.shape[-1]
    for m in range(moments):
        for k in range(count):
            block = value[(m * count + k) * size : (m * count + k + 1) * size]
            lanes = slice(m * width, (m + 1) * width)
            if added is not None:
                block = block + added(k, lanes)
            out_ref[k, :, lanes] = block


def owners(groups, size, cores, turn, steps):
    position = lax.axis_index("site")
    core, y, z = position % 2, position // 2 % 2, position // 4
    return [((z + g) % groups * 4 + (y + turn) % 2 * 2 + (core + cores) % 2) * size for g in steps]


def piece_kernel(*refs, moments, groups, cores, turn, steps):
    out_ref = refs[-1]
    size = out_ref.shape[1]
    blocks = owners(groups, size, cores, turn, steps)
    put(out_ref, product((blocks, size), moments, refs[:8]), len(blocks), moments)


def merge_kernel(*refs, sources, picks):
    for out_ref, blocks in zip(refs[sources:], picks):
        for k, places in enumerate(blocks):
            total = refs[0][places[0]]
            for ref, at in zip(refs[1:sources], places[1:]):
                total = total + ref[at]
            out_ref[k] = total


def phases(momenta, position, devices, tiles):
    site = np.arange(SITES)
    x, zy = site // LAYER, site % LAYER
    own = [np.repeat(a.reshape(TLX, 1, LAYER), 3, 1).reshape(-1) for a in (x, zy % TLY, zy // TLY)]
    edge = np.arange(LAYER)
    full = np.full(LAYER, 0)
    edges = (
        (full + TLX - 1, edge % TLY, edge // TLY),
        (full, edge % TLY, edge // TLY),
        (edge % TLX, full + TLY - 1, edge // TLX),
        (edge % TLX, full, edge // TLX),
    )
    steps = (-tiles, tiles, -1, 1)
    xs, ys, zs, move = own[0], own[1], own[2], np.zeros(MAIN, np.int64)
    for step, (ex, ey, ez) in zip(steps, edges):
        xs = np.concatenate([xs] + [ex] * 3)
        ys = np.concatenate([ys] + [ey] * 3)
        zs = np.concatenate([zs] + [ez] * 3)
        move = np.concatenate([move, np.full(XROWS, step)])
    tile = (position + jnp.asarray(move, jnp.int32) + devices) % devices
    lx, ly = TLX * tiles, TLY * tiles
    sx = (tile // tiles) * TLX + jnp.asarray(xs, jnp.int32)
    sy = (tile % tiles) * TLY + jnp.asarray(ys, jnp.int32)
    sz = jnp.asarray(zs, jnp.int32)
    frac = (momenta[:, 0:1] * sx % lx).astype(jnp.float32) / lx
    frac = frac + (momenta[:, 1:2] * sy % ly).astype(jnp.float32) / ly
    frac = frac + (momenta[:, 2:3] * sz % LZ).astype(jnp.float32) / LZ
    theta = 2.0 * math.pi * frac
    return jnp.cos(theta), jnp.sin(theta)


def halo(sends, devices, tiles):
    found = []
    for block, stride, turn in zip(sends, (tiles, tiles, 1, 1), (1, -1, 1, -1)):
        route = [(i, (i + (turn if i // stride % 2 == 0 else -turn) * stride) % devices) for i in range(devices)]
        found.append(lax.ppermute(block, "site", route))
    return found


def stages(devices):
    found, stride = [], 1
    while stride < devices:
        left = devices // stride
        size = 2 if stride < 4 else 4 if left % 4 == 0 else 2
        found.append((stride, size))
        stride *= size
    return found


def scatter_sum(block, position, devices):
    shape = block.shape[1:]
    for stride, size in stages(devices):
        left = block.shape[0] // size
        block = block.reshape((left, size) + shape)
        mine = (position // stride) % size
        total = lax.dynamic_index_in_dim(block, mine, 1, keepdims=False)
        for step in range(1, size):
            other = (mine + step) % size
            out = lax.dynamic_index_in_dim(block, other, 1, keepdims=False)
            route = []
            for i in range(devices):
                digit = (i // stride) % size
                route.append((i, i + ((digit + step) % size - digit) * stride))
            total = total + lax.ppermute(out, "site", route)
        block = total
    return block[0]


def on_device(vectors, links, momenta, directions):
    devices = lax.axis_size("site")
    tiles = math.isqrt(devices)
    position = lax.axis_index("site")
    nev = vectors.shape[-1]
    moments = momenta.shape[0]
    field = vectors.reshape(6, SITES, nev)
    table = links.reshape(54, SITES)
    halves = nev // LANES
    layer = f32(halves, BOTH, LANES)
    padded = f32(halves, PADDED, LANES)
    fr, wc, *sends = call(
        functools.partial(pack_kernel, tiles=tiles),
        (padded, f32((TLX + 1) * LAYER, LANES), layer, layer, layer, layer),
        [pltpu.VMEM((128, 384), jnp.float32)] * 2 + [pltpu.VMEM((384, 128), jnp.float32)] * 2,
        inputs=2,
    )(field, table)
    received = halo(sends, devices, tiles)
    flops = 2 * 180 * 2 * SITES * nev
    smear = operator(
        wc,
        kinds=((CX, True, 1.0, True), (CYF, False, 1.0, False), (CX, False, 1.0, False)),
        shifts=(0, 1, 0),
        extra=((1, CYB, True, 1.0, -1), (1, CZS, False, 1.0, TLY)),
        middle=LANES,
    )
    pair = [pltpu.VMEM((PADDED, nev), jnp.bfloat16)] * 2
    once = call(smear_kernel, padded, pair, flops, 3 << 20, 3)(fr, *smear)
    cosine, sine = phases(momenta, position, devices, tiles)
    head = bf16(moments * nev, 2 * HEAD)
    tail = bf16(moments * nev, 2 * TAIL)
    rows = pltpu.VMEM((2, HEAD, LANES), jnp.float32)
    ah, al = call(head_kernel, (head, head), [rows], flops, 8 << 20, 3)(fr, cosine, sine)
    displace = operator(
        wc,
        kinds=((CX, True, -1.0, True), (CX, False, 1.0, False), (CYF, False, 1.0, False), (CZD, False, 1.0, False)),
        shifts=(0, 0, 1, TLY),
        extra=((2, CYB, True, -1.0, -1),),
        middle=2 * LANES,
    )
    edges = f32(2, halves, EDGE, LANES)
    once, save, *sends = call(
        functools.partial(edge_kernel, tiles=tiles), (padded, edges, layer, layer, layer, layer), inputs=7
    )(once, wc, *received, ah)
    received = halo(sends, devices, tiles)
    twice = call(smear_kernel, padded, pair, flops, 3 << 20, 3)(once, *smear)
    rows = pltpu.VMEM((2, TAIL, LANES), jnp.float32)
    bh, bl = call(tail_kernel, (tail, tail), [rows], flops, 4 << 20, 4)(fr, save, cosine, sine)
    scale = 1.0 / math.sqrt(3.0 * TLX * tiles * TLY * tiles * LZ)
    operands = call(
        functools.partial(displace_kernel, scale=scale, tiles=tiles),
        (bf16(2 * HEAD, 2 * nev), bf16(2 * HEAD, 2 * nev), bf16(2 * TAIL, 2 * nev), bf16(2 * TAIL, 2 * nev)),
        [
            pltpu.VMEM((halves, PADDED, LANES), jnp.float32),
            pltpu.VMEM((2, HEAD + TAIL, nev), jnp.float32),
        ]
        + [pltpu.VMEM((3, PADDED, nev), jnp.bfloat16)] * 2,
        inputs=9,
    )(twice, wc, *displace, *received, directions[None, :])
    operands = (ah, al, bh, bl) + tuple(operands)
    size, columns = nev // devices, moments * 2 * nev
    if size % 16 == 0 and devices % 8 == 0:
        total = pieces(operands, devices, moments, size, columns)
    else:
        total = whole_product(operands, position, devices, moments, nev)
    return total.reshape(size, moments, 2, nev)


def operator(wc, kinds, shifts, extra, middle):
    lanes = len(kinds) * BOTH
    width = -(-lanes // LANES) * LANES
    column, sign = sources(kinds)
    column = np.pad(column, ((0, 0), (0, width - lanes)), constant_values=-1)
    sign = np.pad(sign, ((0, 0), (0, width - lanes)))
    more, moresign = [], []
    for place, first, adjoint, factor, _ in extra:
        c, w = sources([(first, adjoint, factor, False) if k == place else None for k in range(len(kinds))])
        c = np.pad(c, ((0, 0), (0, width - lanes)), constant_values=-1)
        w = np.pad(w, ((0, 0), (0, width - lanes)))
        more.append(c[:, middle : middle + 2 * LANES])
        moresign.append(w[:, middle : middle + 2 * LANES])
    kernel = functools.partial(
        operator_kernel, middle=middle, kinds=shifts, extra=[(place, shift) for place, _, _, _, shift in extra]
    )
    out = bf16(TLX * BOTH, lanes)
    tables = (column, sign, np.concatenate(more, 1), np.concatenate(moresign, 1))
    return call(kernel, (out, out), (), 1 << 30, 4 << 20, 5)(wc, *map(jnp.asarray, tables))


def whole_product(operands, position, devices, moments, nev):
    whole = lambda a: pl.BlockSpec(a.shape, lambda m: (0, 0))
    partial = pl.pallas_call(
        meson_kernel,
        out_shape=f32(nev, moments * 2 * nev),
        grid=(moments,),
        in_specs=[pl.BlockSpec((nev, a.shape[1]), lambda m: (m, 0)) for a in operands[:4]]
        + [whole(a) for a in operands[4:]],
        out_specs=pl.BlockSpec((nev, 2 * nev), lambda m: (0, m)),
        compiler_params=pltpu.CompilerParams(vmem_limit_bytes=40 * 2**20),
    )(*operands)
    return scatter_sum(partial.reshape(devices, nev // devices, moments * 2 * nev), position, devices)


def pieces(operands, devices, moments, size, columns):
    groups = devices // 4
    block = lambda count: f32(count, size, columns)
    swap = [(i, i ^ 1) for i in range(devices)]
    flip = [(i, i ^ 2) for i in range(devices)]

    def piece(cores, turn, steps, *after):
        kernel = functools.partial(
            piece_kernel, moments=moments, groups=groups, cores=cores, turn=turn, steps=tuple(steps)
        )
        flops = 2 * 3 * size * len(steps) * moments * 4 * (HEAD + TAIL) * 256
        return call(kernel, block(len(steps)), (), flops, 1 << 20, 8 + len(after))(*operands, *after)

    def permute(value, route):
        return lax.ppermute(value, "site", route)

    def merge(arrays, picks):
        kernel = functools.partial(merge_kernel, sources=len(arrays), picks=picks)
        outs = tuple(block(len(p)) for p in picks)
        return call(kernel, outs, inputs=len(arrays))(*arrays)

    order = sorted(range(1, groups), key=lambda g: -min(g, groups - g)) + [0]
    early, late = order[: groups // 2], order[groups // 2 :]
    apart = [[[(k, k)] for k in range(len(early))], [[(k, k) for k in range(len(late))]]]
    a1 = piece(1, 1, early)
    got_a = permute(a1, swap)
    a2 = piece(0, 1, early, a1)
    b1 = piece(1, 1, late, a2)
    got_b = permute(b1, swap)
    out_a = merge((a2, got_a), apart[0])
    crossed = [[permute(out, flip) for out in out_a]]
    b2 = piece(0, 1, late, b1, out_a[0])
    out_b = merge((b2, got_b), apart[1])
    crossed.append([permute(out_b[0], flip)])
    c1 = piece(1, 0, early, out_b[0])
    got_c = permute(c1, swap)
    c2 = piece(0, 0, early, c1)
    d1 = piece(1, 0, late, c2)
    got_d = permute(d1, swap)
    d2 = piece(0, 0, late, d1)
    kept = [(c2, got_c), (d2, got_d)]
    total, arrived = None, []
    for steps, got, (mine, swapped) in zip((early, late), crossed, kept):
        for first, array in enumerate(got):
            count = array.shape[0]
            picks = [[(first + k, first + k, k)] for k in range(count)]
            for k, value in enumerate(merge((mine, swapped, array), picks)):
                step = steps[first + k]
                if step == 0:
                    total = value
                else:
                    route = [(i, (i + 4 * step) % devices) for i in range(devices)]
                    arrived.append(lax.ppermute(value, "site", route))
    for value in arrived:
        total = total + value
    return total[0]


def solution(mesh):
    placed = (
        P("grp", None, "site", None, None),
        P("grp", None, None, None, "site", None),
        P(),
        P(),
    )
    return jax.shard_map(
        on_device,
        mesh=mesh,
        in_specs=placed,
        out_specs=P("site", "grp", None, None),
        check_vma=False,
    )
```

```python
import functools
import math

import jax
import jax.numpy as jnp
import numpy as np
from jax import lax
from jax.experimental import pallas as pl
from jax.experimental.pallas import tpu as pltpu
from jax.sharding import PartitionSpec as P


TLX = 12
TLY = 12
LZ = 2
KAPPA = 0.08

LAYER = LZ * TLY
SITES = TLX * LAYER
XROWS = 3 * LAYER
MAIN = TLX * XROWS
BOTH = 2 * XROWS
PADDED = (TLX + 2) * BOTH
WINDOW = 3 * BOTH
EDGE = 4 * XROWS
HEAD = MAIN // 128 * 128
TAIL = MAIN - HEAD + EDGE
LANES = 128
CX, CY, CZ = 0, 18, 36
CYF, CYB, CZS, CZD = 54, 72, 90, 108
VMEM_LIMIT = 12 * 2**20


def call(kernel, outs, scratch=(), flops=0, moved=0, inputs=1, scalars=0, off_chip=0, **kwargs):
    on_chip = pl.BlockSpec(memory_space=pltpu.VMEM)
    first = [pl.BlockSpec(memory_space=pltpu.SMEM)] * scalars + [pl.BlockSpec(memory_space=pltpu.HBM)] * off_chip
    return pl.pallas_call(
        kernel,
        out_shape=outs,
        in_specs=first + [on_chip] * inputs,
        out_specs=jax.tree.map(lambda _: on_chip, outs),
        scratch_shapes=list(scratch),
        compiler_params=pltpu.CompilerParams(vmem_limit_bytes=VMEM_LIMIT),
        cost_estimate=pl.CostEstimate(flops=flops, bytes_accessed=moved, transcendentals=0),
        **kwargs,
    )


def f32(*shape):
    return jax.ShapeDtypeStruct(shape, jnp.float32)


def bf16(*shape):
    return jax.ShapeDtypeStruct(shape, jnp.bfloat16)


def spread(table, column, lanes=LANES):
    return jnp.broadcast_to(table[:, column : column + 1], (table.shape[0], lanes))


def matvec(table, first, field, adjoint=False, acc=None, minus=False):
    out = [[None] * 3, [None] * 3] if acc is None else [list(acc[0]), list(acc[1])]
    lanes = field[0][0].shape[-1]

    def put(part, row, value, negative):
        if negative != minus:
            out[part][row] = -value if out[part][row] is None else out[part][row] - value
        else:
            out[part][row] = value if out[part][row] is None else out[part][row] + value

    for row in range(3):
        for col in range(3):
            at = first + (3 * col + row if adjoint else 3 * row + col)
            real = spread(table, at, lanes)
            imag = spread(table, at + 9, lanes)
            put(0, row, real * field[0][col], False)
            put(0, row, imag * field[1][col], not adjoint)
            put(1, row, real * field[1][col], False)
            put(1, row, imag * field[0][col], adjoint)
    return out


def layer_rows(ref, part, half, first, size=LAYER):
    at = part * XROWS + first
    return ref[half, at : at + size, :]


def grid2(load):
    return [[load(part, colour) for colour in range(3)] for part in range(2)]


def y_rows(part, colour, z, y):
    return pl.ds(BOTH + part * XROWS + colour * LAYER + z * TLY + y, TLX, stride=BOTH)


def parity(tiles):
    position = lax.axis_index("site")
    return position // tiles % 2 == 0, position % 2 == 0


def send_layers(f_ref, wc_ref, ax_ref, bx_ref, ay_ref, by_ref, tiles):
    last = TLX * BOTH
    even_x, even_y = parity(tiles)
    for half in range(f_ref.shape[0]):
        table = wc_ref[TLX * LAYER : (TLX + 1) * LAYER, :]
        hop = matvec(table, CX, grid2(lambda p, c: layer_rows(f_ref, p, half, last + c * LAYER)), adjoint=True)
        for part in range(2):
            for colour in range(3):
                to = part * XROWS + colour * LAYER
                low, high = f_ref[half, BOTH + to : BOTH + to + LAYER, :], hop[part][colour]
                ax_ref[half, to : to + LAYER, :] = jnp.where(even_x, high, low)
                bx_ref[half, to : to + LAYER, :] = jnp.where(even_x, low, high)
        for z in range(LZ):
            table = wc_ref[pl.ds(LAYER + z * TLY + TLY - 1, TLX, stride=LAYER), :]
            hop = matvec(table, CY, grid2(lambda p, c: f_ref[half, y_rows(p, c, z, TLY - 1), :]), adjoint=True)
            for part in range(2):
                for colour in range(3):
                    to = part * XROWS + colour * LAYER + z * TLX
                    low, high = f_ref[half, y_rows(part, colour, z, 0), :], hop[part][colour]
                    ay_ref[half, to : to + TLX, :] = jnp.where(even_y, high, low)
                    by_ref[half, to : to + TLX, :] = jnp.where(even_y, low, high)


def clear_ends(ref):
    for half in range(ref.shape[0]):
        ref[half, 0:BOTH, :] = jnp.zeros((BOTH, LANES), jnp.float32)
        ref[half, PADDED - BOTH : PADDED, :] = jnp.zeros((BOTH, LANES), jnp.float32)


def pack_kernel(v_ref, l_ref, fr_ref, wc_ref, ax_ref, bx_ref, ay_ref, by_ref, la, lb, ta, tb, *, tiles):
    la[...] = jnp.zeros_like(la)
    lb[...] = jnp.zeros_like(lb)
    plane = SITES // LZ
    la[0:54, 0:SITES] = l_ref[...]
    la[CYF : CYF + 18, 0:SITES] = l_ref[CY : CY + 18, :]
    la[CYB : CYB + 18, 0:SITES] = l_ref[CY : CY + 18, :]
    la[CZS : CZS + 18, 0:SITES] = l_ref[CZ : CZ + 18, :]
    la[CZD : CZD + 18, 0:SITES] = l_ref[CZ : CZ + 18, :]
    for part in range(2):
        for row in range(3):
            for col in range(3):
                k = 9 * part + 3 * row + col
                kt = CZ + 9 * part + 3 * col + row
                value = l_ref[kt : kt + 1, :]
                sign = 1.0 if part == 0 else -1.0
                lb[CZS + k : CZS + k + 1, 0:SITES] = sign * value
                lb[CZD + k : CZD + k + 1, 0:SITES] = -sign * value
    ta[...] = jnp.transpose(la[...])
    tb[...] = jnp.transpose(lb[...])
    raw = ta[0:SITES, :]
    other = jnp.concatenate([tb[plane:SITES, :], tb[0:plane, :]], axis=0)
    y = lax.broadcasted_iota(jnp.int32, (SITES, LANES), 0) % TLY
    column = lax.broadcasted_iota(jnp.int32, (SITES, LANES), 1)
    back = pltpu.roll(raw, 1, 0)
    is_yf = (column >= CYF) & (column < CYB)
    is_yb = (column >= CYB) & (column < CZS)
    table = jnp.where(is_yb, back, raw)
    gone = (is_yf & (y == TLY - 1)) | (is_yb & (y == 0))
    ta[0:SITES, :] = jnp.where(gone, 0.0, table) + other
    wc_ref[0:LAYER, :] = jnp.zeros((LAYER, LANES), jnp.float32)
    clear_ends(fr_ref)
    for x in range(TLX):
        for z in range(LZ):
            src = z * plane + x * TLY
            dst = (x + 1) * LAYER + z * TLY
            wc_ref[dst : dst + TLY, :] = ta[src : src + TLY, :]
            for half in range(fr_ref.shape[0]):
                for part in range(2):
                    for colour in range(3):
                        dst = (x + 1) * BOTH + part * XROWS + colour * LAYER + z * TLY
                        fr_ref[half, dst : dst + TLY, :] = v_ref[
                            3 * part + colour, src : src + TLY, half * LANES : (half + 1) * LANES
                        ]
    send_layers(fr_ref, wc_ref, ax_ref, bx_ref, ay_ref, by_ref, tiles)


def split(value):
    high = value.astype(jnp.bfloat16)
    return high, (value - high.astype(jnp.float32)).astype(jnp.bfloat16)


def sources(kinds):
    column = np.full((6, len(kinds) * BOTH), -1, np.int32)
    sign = np.zeros((6, len(kinds) * BOTH), np.float32)
    for k, kind in enumerate(kinds):
        if kind is None:
            continue
        first, adjoint, factor, below = kind
        for ri in range(2):
            for row in range(3):
                for rj in range(2):
                    for col in range(3):
                        at = first + (3 * col + row if adjoint else 3 * row + col)
                        weight = 1.0
                        if ri != rj:
                            at += 9
                            weight = -1.0 if (ri == 0) != adjoint else 1.0
                        lanes = slice(k * BOTH + rj * XROWS + col * LAYER, k * BOTH + rj * XROWS + (col + 1) * LAYER)
                        column[3 * ri + row, lanes] = at + (2 * LANES if below else 0)
                        sign[3 * ri + row, lanes] = factor * weight
    return column, sign


def expand(terms, column_ref, sign_ref, block, first, width):
    deep = terms.shape[1] // (2 * LANES)
    row = lax.broadcasted_iota(jnp.int32, (LANES, width), 0)
    column = jnp.broadcast_to(column_ref[block : block + 1, first : first + width], (LANES, width))
    sign = jnp.broadcast_to(sign_ref[block : block + 1, first : first + width], (LANES, width))
    ones = []
    for k in range(deep):
        ones += [jnp.where(row + 2 * k * LANES == column, sign, 0.0).astype(jnp.bfloat16)] * 2
    return dot(terms, jnp.concatenate(ones, axis=0))


def operator_kernel(wc_ref, column_ref, sign_ref, more_ref, moresign_ref, high_ref, low_ref, *, middle, kinds, extra):
    high, low = split(wc_ref[...])
    own, below = slice(LAYER, (TLX + 1) * LAYER), slice(0, TLX * LAYER)
    deep = jnp.concatenate([high[own], low[own], high[below], low[below]], axis=1)
    single = jnp.concatenate([high[own], low[own]], axis=1)
    width = -(-len(kinds) * BOTH // LANES) * LANES
    wide = 2 * LANES

    def mask(first, size, shifts):
        p = lax.broadcasted_iota(jnp.int32, (LAYER, size), 0)
        lane = lax.broadcasted_iota(jnp.int32, (LAYER, size), 1) + first
        q = lane % LAYER
        block = lane // BOTH
        found = None
        for k, shift in enumerate(shifts):
            if shift is not None:
                here = (block == k) & (q == (p + shift if shift != TLY else (p + TLY) % LAYER))
                found = here if found is None else found | here
        return found

    keep = mask(0, width, kinds)
    keeps = [mask(middle, wide, [shift if k == place else None for k in range(len(kinds))]) for place, shift in extra]
    for block in range(6):
        value = expand(deep, column_ref, sign_ref, block, 0, width).reshape(TLX, LAYER, width)
        value = jnp.where(keep[None], value, 0.0)
        center = value[:, :, middle : middle + wide]
        for k in range(len(extra)):
            other = expand(single, more_ref, moresign_ref, block, k * wide, wide).reshape(TLX, LAYER, wide)
            center = center + jnp.where(keeps[k][None], other, 0.0)
        pieces = [value[:, :, :middle], center]
        if middle + wide < width:
            pieces.append(value[:, :, middle + wide :])
        at = 0
        for piece in pieces:
            size = min(piece.shape[2], len(kinds) * BOTH - at)
            if size > 0:
                high, low = split(piece)
                for x in range(TLX):
                    rows = slice(x * BOTH + block * LAYER, x * BOTH + (block + 1) * LAYER)
                    high_ref[rows, at : at + size] = high[x, :, :size]
                    low_ref[rows, at : at + size] = low[x, :, :size]
            at += piece.shape[2]


def split_field(f_ref, high_ref, low_ref, scale=None):
    for half in range(f_ref.shape[0]):
        lanes = slice(half * LANES, (half + 1) * LANES)
        for row in range(0, PADDED, BOTH):
            value = f_ref[half, row : row + BOTH, :]
            high, low = split(value if scale is None else scale * value)
            high_ref[row : row + BOTH, lanes] = high
            low_ref[row : row + BOTH, lanes] = low


def smear_kernel(f_ref, oh_ref, ol_ref, out_ref, fh, fl):
    clear_ends(out_ref)
    split_field(f_ref, fh, fl)
    for x in range(TLX):
        rows = slice(x * BOTH, (x + 1) * BOTH)
        high, low = oh_ref[rows, :], ol_ref[rows, :]
        window = slice(x * BOTH, x * BOTH + WINDOW)
        hops = dot(high, fh[window, :]) + dot(high, fl[window, :]) + dot(low, fh[window, :])
        at = slice((x + 1) * BOTH, (x + 2) * BOTH)
        for half in range(f_ref.shape[0]):
            lanes = slice(half * LANES, (half + 1) * LANES)
            out_ref[half, at, :] = (1.0 - 6.0 * KAPPA) * f_ref[half, at, :] + KAPPA * hops[:, lanes]


def cross(once_ref, wc_ref, received, tiles, save=None):
    last = TLX * BOTH
    even_x, even_y = parity(tiles)
    ax, bx, ay, by = received

    def arrived(above, half, part, first, size, along_y):
        one, two, even = (ay, by, even_y) if along_y else (ax, bx, even_x)
        values = (layer_rows(ref, part, half, first, size) for ref in ((one, two) if above else (two, one)))
        return jnp.where(even, *values)

    for half in range(once_ref.shape[0]):
        table = wc_ref[TLX * LAYER : (TLX + 1) * LAYER, :]
        hop_x = matvec(table, CX, grid2(lambda p, c: arrived(True, half, p, c * LAYER, LAYER, False)))
        hop_y = []
        for z in range(LZ):
            table = wc_ref[pl.ds(LAYER + z * TLY + TLY - 1, TLX, stride=LAYER), :]
            hop_y.append(
                matvec(table, CY, grid2(lambda p, c: arrived(True, half, p, c * LAYER + z * TLX, TLX, True)))
            )
        for part in range(2):
            for colour in range(3):
                at = colour * LAYER
                low = arrived(False, half, part, at, LAYER, False)
                to = part * XROWS + at
                once_ref[half, BOTH + to : BOTH + to + LAYER, :] += KAPPA * low
                once_ref[half, last + to : last + to + LAYER, :] += KAPPA * hop_x[part][colour]
                if save is not None:
                    save[part, half, at : at + LAYER, :] = low
                    save[part, half, XROWS + at : XROWS + at + LAYER, :] = hop_x[part][colour]
                for z in range(LZ):
                    low = arrived(False, half, part, at + z * TLX, TLX, True)
                    rows = y_rows(part, colour, z, 0)
                    once_ref[half, rows, :] = once_ref[half, rows, :] + KAPPA * low
                    rows = y_rows(part, colour, z, TLY - 1)
                    once_ref[half, rows, :] = once_ref[half, rows, :] + KAPPA * hop_y[z][part][colour]
                    if save is not None:
                        to = 2 * XROWS + at + z * TLX
                        save[part, half, to : to + TLX, :] = low
                        save[part, half, to + XROWS : to + XROWS + TLX, :] = hop_y[z][part][colour]


def edge_kernel(part_ref, wc_ref, rax, rbx, ray, rby, *refs, tiles):
    once_ref, save, ax_ref, bx_ref, ay_ref, by_ref = refs[-6:]
    once_ref[...] = part_ref[...]
    cross(once_ref, wc_ref, (rax, rbx, ray, rby), tiles, save)
    send_layers(once_ref, wc_ref, ax_ref, bx_ref, ay_ref, by_ref, tiles)


def phased(real, imag, half, lane, at, size, cos_ref, sin_ref, ah_ref, al_ref):
    real, imag = jnp.transpose(real), jnp.transpose(imag)
    halves = ah_ref.shape[0] // cos_ref.shape[0] // LANES
    for m in range(cos_ref.shape[0]):
        cosine = jnp.broadcast_to(cos_ref[m : m + 1, lane : lane + LANES], (LANES, LANES))
        sine = jnp.broadcast_to(sin_ref[m : m + 1, lane : lane + LANES], (LANES, LANES))
        row = (m * halves + half) * LANES
        high, low = split(cosine * real - sine * imag)
        ah_ref[row : row + LANES, at : at + LANES] = high
        al_ref[row : row + LANES, at : at + LANES] = low
        high, low = split(sine * real + cosine * imag)
        ah_ref[row : row + LANES, size + at : size + at + LANES] = high
        al_ref[row : row + LANES, size + at : size + at + LANES] = low


def own_rows(fr_ref, rows, half, first, stop):
    for part in range(2):
        for x in range(first // XROWS, -(-stop // XROWS)):
            low, high = max(first, x * XROWS), min(stop, (x + 1) * XROWS)
            at = (x + 1) * BOTH + part * XROWS + low - x * XROWS
            rows[part, low - first : high - first, :] = fr_ref[half, at : at + high - low, :]


def head_kernel(fr_ref, cos_ref, sin_ref, ah_ref, al_ref, rows):
    for half in range(fr_ref.shape[0]):
        own_rows(fr_ref, rows, half, 0, HEAD)
        for at in range(0, HEAD, LANES):
            real, imag = (rows[p, at : at + LANES, :] for p in range(2))
            phased(real, imag, half, at, at, HEAD, cos_ref, sin_ref, ah_ref, al_ref)


def tail_kernel(fr_ref, save, cos_ref, sin_ref, ah_ref, al_ref, rows):
    for half in range(fr_ref.shape[0]):
        own_rows(fr_ref, rows, half, HEAD, MAIN)
        for part in range(2):
            rows[part, MAIN - HEAD : TAIL, :] = save[part, half]
        for at in range(0, TAIL, LANES):
            real, imag = (rows[p, at : at + LANES, :] for p in range(2))
            phased(real, imag, half, HEAD + at, at, TAIL, cos_ref, sin_ref, ah_ref, al_ref)


def displace_kernel(
    part_ref, wc_ref, oh_ref, ol_ref, rax, rbx, ray, rby, dir_ref, *refs, scale, tiles
):
    sh_ref, sl_ref, th_ref, tl_ref, twice, shift, fh, fl = refs[-8:]
    twice[...] = part_ref[...]
    cross(twice, wc_ref, (rax, rbx, ray, rby), tiles)
    halves = range(twice.shape[0])
    width = len(halves) * LANES

    def along(which, lanes, rows):
        return jnp.broadcast_to(dir_ref[0:1, lanes], (rows, lanes.stop - lanes.start)) == which

    for half in halves:
        lanes = slice(half * LANES, (half + 1) * LANES)
        masks = [jnp.where(along(which, lanes, BOTH), 1.0, 0.0).astype(jnp.bfloat16) for which in range(3)]
        for row in range(0, PADDED, BOTH):
            high, low = split(scale * twice[half, row : row + BOTH, :])
            for which in range(3):
                fh[which, row : row + BOTH, lanes] = high * masks[which]
                fl[which, row : row + BOTH, lanes] = low * masks[which]
    for x in range(TLX):
        rows = slice(x * BOTH, (x + 1) * BOTH)
        low, mid, top = (slice((x + k) * BOTH, (x + k + 1) * BOTH) for k in range(3))

        def columns(ref):
            return jnp.concatenate([ref[0, low, :], ref[0, top, :], ref[1, mid, :], ref[2, mid, :]], axis=0)

        fields, rest = columns(fh), columns(fl)
        weights = oh_ref[rows, :]
        value = dot(weights, fields) + dot(weights, rest) + dot(ol_ref[rows, :], fields)
        for part in range(2):
            shift[part, x * XROWS : (x + 1) * XROWS, :] = value[part * XROWS : (part + 1) * XROWS]
    last = TLX * BOTH
    for half in halves:
        lanes = slice(half * LANES, (half + 1) * LANES)
        mask_x = jnp.where(along(0, lanes, XROWS), scale, 0.0)
        mask_y = jnp.where(along(1, lanes, TLX), scale, 0.0)
        for part in range(2):
            at = part * XROWS
            shift[part, MAIN : MAIN + XROWS, lanes] = mask_x * twice[half, BOTH + at : BOTH + at + XROWS, :]
            shift[part, MAIN + XROWS : MAIN + 2 * XROWS, lanes] = -mask_x * twice[half, last + at : last + at + XROWS, :]
            for colour in range(3):
                for z in range(LZ):
                    to = MAIN + 2 * XROWS + colour * LAYER + z * TLX
                    shift[part, to : to + TLX, lanes] = mask_y * twice[half, y_rows(part, colour, z, 0), :]
                    to += XROWS
                    shift[part, to : to + TLX, lanes] = -mask_y * twice[half, y_rows(part, colour, z, TLY - 1), :]
    for high_ref, low_ref, first, size in ((sh_ref, sl_ref, 0, HEAD), (th_ref, tl_ref, HEAD, TAIL)):
        real, imag = slice(0, width), slice(width, 2 * width)
        for row in range(0, size, 128):
            top = slice(row, row + 128)
            bottom = slice(size + row, size + row + 128)
            high, low = split(shift[0, first + row : first + row + 128, :])
            high_ref[top, real] = high
            low_ref[top, real] = low
            high_ref[bottom, imag] = -high
            low_ref[bottom, imag] = -low
            high, low = split(shift[1, first + row : first + row + 128, :])
            high_ref[bottom, real] = high
            low_ref[bottom, real] = low
            high_ref[top, imag] = high
            low_ref[top, imag] = low


def dot(a, b):
    return jnp.dot(a, b, preferred_element_type=jnp.float32)


def meson_kernel(ah, al, bh, bl, sh, sl, th, tl, out_ref):
    total = dot(ah[...], sh[...]) + dot(ah[...], sl[...]) + dot(al[...], sh[...])
    out_ref[...] = total + dot(bh[...], th[...]) + dot(bh[...], tl[...]) + dot(bl[...], th[...])


def product(blocks, moments, refs):
    ah, al, bh, bl, sh, sl, th, tl = refs
    nev = ah.shape[0] // moments
    size = blocks[1]

    def rows(ref):
        picked = [ref[pl.ds(pl.multiple_of(m * nev + b, size), size), :] for m in range(moments) for b in blocks[0]]
        return jnp.concatenate(picked, axis=0)

    ahv, alv, bhv, blv = rows(ah), rows(al), rows(bh), rows(bl)
    total = dot(ahv, sh[...]) + dot(ahv, sl[...]) + dot(alv, sh[...])
    return total + dot(bhv, th[...]) + dot(bhv, tl[...]) + dot(blv, th[...])


def put(out_ref, value, count, moments, added=None):
    size, width = out_ref.shape[1], value.shape[-1]
    for m in range(moments):
        for k in range(count):
            block = value[(m * count + k) * size : (m * count + k + 1) * size]
            lanes = slice(m * width, (m + 1) * width)
            if added is not None:
                block = block + added(k, lanes)
            out_ref[k, :, lanes] = block


def owners(groups, size, cores, turn, steps):
    position = lax.axis_index("site")
    core, y, z = position % 2, position // 2 % 2, position // 4
    return [((z + g) % groups * 4 + (y + turn) % 2 * 2 + (core + cores) % 2) * size for g in steps]


def piece_kernel(*refs, moments, groups, cores, turn, steps):
    out_ref = refs[-1]
    size = out_ref.shape[1]
    blocks = owners(groups, size, cores, turn, steps)
    put(out_ref, product((blocks, size), moments, refs[:8]), len(blocks), moments)


def merge_kernel(*refs, sources, picks):
    for out_ref, blocks in zip(refs[sources:], picks):
        for k, places in enumerate(blocks):
            total = refs[0][places[0]]
            for ref, at in zip(refs[1:sources], places[1:]):
                total = total + ref[at]
            out_ref[k] = total


def final_kernel(*refs):
    out_ref = refs[-1]
    width = out_ref.shape[3]
    for m in range(out_ref.shape[1]):
        for part in range(2):
            lanes = slice((2 * m + part) * width, (2 * m + part + 1) * width)
            total = refs[0][0, :, lanes]
            for ref in refs[1:-1]:
                total = total + ref[0, :, lanes]
            out_ref[:, m, part, :] = total


def phases(momenta, position, devices, tiles):
    site = np.arange(SITES)
    x, zy = site // LAYER, site % LAYER
    own = [np.repeat(a.reshape(TLX, 1, LAYER), 3, 1).reshape(-1) for a in (x, zy % TLY, zy // TLY)]
    edge = np.arange(LAYER)
    full = np.full(LAYER, 0)
    edges = (
        (full + TLX - 1, edge % TLY, edge // TLY),
        (full, edge % TLY, edge // TLY),
        (edge % TLX, full + TLY - 1, edge // TLX),
        (edge % TLX, full, edge // TLX),
    )
    steps = (-tiles, tiles, -1, 1)
    xs, ys, zs, move = own[0], own[1], own[2], np.zeros(MAIN, np.int64)
    for step, (ex, ey, ez) in zip(steps, edges):
        xs = np.concatenate([xs] + [ex] * 3)
        ys = np.concatenate([ys] + [ey] * 3)
        zs = np.concatenate([zs] + [ez] * 3)
        move = np.concatenate([move, np.full(XROWS, step)])
    tile = (position + jnp.asarray(move, jnp.int32) + devices) % devices
    lx, ly = TLX * tiles, TLY * tiles
    sx = (tile // tiles) * TLX + jnp.asarray(xs, jnp.int32)
    sy = (tile % tiles) * TLY + jnp.asarray(ys, jnp.int32)
    sz = jnp.asarray(zs, jnp.int32)
    frac = (momenta[:, 0:1] * sx % lx).astype(jnp.float32) / lx
    frac = frac + (momenta[:, 1:2] * sy % ly).astype(jnp.float32) / ly
    frac = frac + (momenta[:, 2:3] * sz % LZ).astype(jnp.float32) / LZ
    theta = 2.0 * math.pi * frac
    return jnp.cos(theta), jnp.sin(theta)


def halo(sends, devices, tiles):
    found = []
    for block, stride, turn in zip(sends, (tiles, tiles, 1, 1), (1, -1, 1, -1)):
        route = [(i, (i + (turn if i // stride % 2 == 0 else -turn) * stride) % devices) for i in range(devices)]
        found.append(lax.ppermute(block, "site", route))
    return found


def stages(devices):
    found, stride = [], 1
    while stride < devices:
        left = devices // stride
        size = 2 if stride < 4 else 4 if left % 4 == 0 else 2
        found.append((stride, size))
        stride *= size
    return found


def scatter_sum(block, position, devices):
    shape = block.shape[1:]
    for stride, size in stages(devices):
        left = block.shape[0] // size
        block = block.reshape((left, size) + shape)
        mine = (position // stride) % size
        total = lax.dynamic_index_in_dim(block, mine, 1, keepdims=False)
        for step in range(1, size):
            other = (mine + step) % size
            out = lax.dynamic_index_in_dim(block, other, 1, keepdims=False)
            route = []
            for i in range(devices):
                digit = (i // stride) % size
                route.append((i, i + ((digit + step) % size - digit) * stride))
            total = total + lax.ppermute(out, "site", route)
        block = total
    return block[0]


def on_device(vectors, links, momenta, directions):
    devices = lax.axis_size("site")
    tiles = math.isqrt(devices)
    position = lax.axis_index("site")
    nev = vectors.shape[-1]
    moments = momenta.shape[0]
    field = vectors.reshape(6, SITES, nev)
    table = links.reshape(54, SITES)
    halves = nev // LANES
    layer = f32(halves, BOTH, LANES)
    padded = f32(halves, PADDED, LANES)
    fr, wc, *sends = call(
        functools.partial(pack_kernel, tiles=tiles),
        (padded, f32((TLX + 1) * LAYER, LANES), layer, layer, layer, layer),
        [pltpu.VMEM((128, 384), jnp.float32)] * 2 + [pltpu.VMEM((384, 128), jnp.float32)] * 2,
        inputs=2,
    )(field, table)
    received = halo(sends, devices, tiles)
    flops = 2 * 180 * 2 * SITES * nev
    smear = operator(
        wc,
        kinds=((CX, True, 1.0, True), (CYF, False, 1.0, False), (CX, False, 1.0, False)),
        shifts=(0, 1, 0),
        extra=((1, CYB, True, 1.0, -1), (1, CZS, False, 1.0, TLY)),
        middle=LANES,
    )
    pair = [pltpu.VMEM((PADDED, nev), jnp.bfloat16)] * 2
    once = call(smear_kernel, padded, pair, flops, 3 << 20, 3)(fr, *smear)
    cosine, sine = phases(momenta, position, devices, tiles)
    head = bf16(moments * nev, 2 * HEAD)
    tail = bf16(moments * nev, 2 * TAIL)
    rows = pltpu.VMEM((2, HEAD, LANES), jnp.float32)
    ah, al = call(head_kernel, (head, head), [rows], flops, 8 << 20, 3)(fr, cosine, sine)
    displace = operator(
        wc,
        kinds=((CX, True, -1.0, True), (CX, False, 1.0, False), (CYF, False, 1.0, False), (CZD, False, 1.0, False)),
        shifts=(0, 0, 1, TLY),
        extra=((2, CYB, True, -1.0, -1),),
        middle=2 * LANES,
    )
    edges = f32(2, halves, EDGE, LANES)
    once, save, *sends = call(
        functools.partial(edge_kernel, tiles=tiles), (padded, edges, layer, layer, layer, layer), inputs=7
    )(once, wc, *received, ah)
    received = halo(sends, devices, tiles)
    twice = call(smear_kernel, padded, pair, flops, 3 << 20, 3)(once, *smear)
    rows = pltpu.VMEM((2, TAIL, LANES), jnp.float32)
    bh, bl = call(tail_kernel, (tail, tail), [rows], flops, 4 << 20, 4)(fr, save, cosine, sine)
    scale = 1.0 / math.sqrt(3.0 * TLX * tiles * TLY * tiles * LZ)
    operands = call(
        functools.partial(displace_kernel, scale=scale, tiles=tiles),
        (bf16(2 * HEAD, 2 * nev), bf16(2 * HEAD, 2 * nev), bf16(2 * TAIL, 2 * nev), bf16(2 * TAIL, 2 * nev)),
        [
            pltpu.VMEM((halves, PADDED, LANES), jnp.float32),
            pltpu.VMEM((2, HEAD + TAIL, nev), jnp.float32),
        ]
        + [pltpu.VMEM((3, PADDED, nev), jnp.bfloat16)] * 2,
        inputs=9,
    )(twice, wc, *displace, *received, directions[None, :])
    operands = (ah, al, bh, bl) + tuple(operands)
    size, columns = nev // devices, moments * 2 * nev
    if size % 16 == 0 and devices % 8 == 0:
        total = pieces(operands, devices, moments, size, columns)
    else:
        total = whole_product(operands, position, devices, moments, nev)
    return total.reshape(size, moments, 2, nev)


def operator(wc, kinds, shifts, extra, middle):
    lanes = len(kinds) * BOTH
    width = -(-lanes // LANES) * LANES
    column, sign = sources(kinds)
    column = np.pad(column, ((0, 0), (0, width - lanes)), constant_values=-1)
    sign = np.pad(sign, ((0, 0), (0, width - lanes)))
    more, moresign = [], []
    for place, first, adjoint, factor, _ in extra:
        c, w = sources([(first, adjoint, factor, False) if k == place else None for k in range(len(kinds))])
        c = np.pad(c, ((0, 0), (0, width - lanes)), constant_values=-1)
        w = np.pad(w, ((0, 0), (0, width - lanes)))
        more.append(c[:, middle : middle + 2 * LANES])
        moresign.append(w[:, middle : middle + 2 * LANES])
    kernel = functools.partial(
        operator_kernel, middle=middle, kinds=shifts, extra=[(place, shift) for place, _, _, _, shift in extra]
    )
    out = bf16(TLX * BOTH, lanes)
    tables = (column, sign, np.concatenate(more, 1), np.concatenate(moresign, 1))
    return call(kernel, (out, out), (), 1 << 30, 4 << 20, 5)(wc, *map(jnp.asarray, tables))


def whole_product(operands, position, devices, moments, nev):
    whole = lambda a: pl.BlockSpec(a.shape, lambda m: (0, 0))
    partial = pl.pallas_call(
        meson_kernel,
        out_shape=f32(nev, moments * 2 * nev),
        grid=(moments,),
        in_specs=[pl.BlockSpec((nev, a.shape[1]), lambda m: (m, 0)) for a in operands[:4]]
        + [whole(a) for a in operands[4:]],
        out_specs=pl.BlockSpec((nev, 2 * nev), lambda m: (0, m)),
        compiler_params=pltpu.CompilerParams(vmem_limit_bytes=40 * 2**20),
    )(*operands)
    return scatter_sum(partial.reshape(devices, nev // devices, moments * 2 * nev), position, devices)


def pieces(operands, devices, moments, size, columns):
    groups = devices // 4
    block = lambda count: f32(count, size, columns)
    swap = [(i, i ^ 1) for i in range(devices)]
    flip = [(i, i ^ 2) for i in range(devices)]

    def piece(cores, turn, steps, *after):
        kernel = functools.partial(
            piece_kernel, moments=moments, groups=groups, cores=cores, turn=turn, steps=tuple(steps)
        )
        flops = 2 * 3 * size * len(steps) * moments * 4 * (HEAD + TAIL) * 256
        return call(kernel, block(len(steps)), (), flops, 1 << 20, 8 + len(after))(*operands, *after)

    def permute(value, route):
        return lax.ppermute(value, "site", route)

    def merge(arrays, picks):
        kernel = functools.partial(merge_kernel, sources=len(arrays), picks=picks)
        outs = tuple(block(len(p)) for p in picks)
        return call(kernel, outs, inputs=len(arrays))(*arrays)

    order = sorted(range(1, groups), key=lambda g: -min(g, groups - g)) + [0]
    early, late = order[: groups // 2], order[groups // 2 :]

    def along_z(value, step):
        return permute(value, [(i, (i + 4 * step) % devices) for i in range(devices)])

    def split_sum(mine, swapped):
        return merge((mine, swapped), [[(k, k)] for k in range(mine.shape[0])])

    a1 = piece(1, 1, early)
    got_a = permute(a1, swap)
    a2 = piece(0, 1, early, a1)
    out_a = split_sum(a2, got_a)
    crossed_a = [permute(out_a[0], flip)]
    c1 = piece(1, 0, early, out_a[0])
    got_c = permute(c1, swap)
    crossed_a += [permute(out_a[k], flip) for k in range(1, len(early))]
    c2 = piece(0, 0, early, c1)
    b1 = piece(1, 1, late, c2)
    got_b = permute(b1, swap)
    b2 = piece(0, 1, late, b1)
    sums = list(merge((c2, got_c, crossed_a[0]), [[(0, 0, 0)]]))
    arrived = [along_z(sums[0], early[0])]
    out_b = split_sum(b2, got_b)
    crossed_b = [permute(out, flip) for out in out_b]
    for k in range(1, len(early)):
        sums += merge((c2, got_c, crossed_a[k]), [[(k, k, 0)]])
        arrived.append(along_z(sums[-1], early[k]))
    d1 = piece(1, 0, late, out_b[0], sums[0])
    got_d = permute(d1, swap)
    d2 = piece(0, 0, late, d1)
    total = None
    for k, step in enumerate(late):
        sums += merge((d2, got_d, crossed_b[k]), [[(k, k, 0)]])
        if step == 0:
            total = sums[-1]
        else:
            arrived.append(along_z(sums[-1], step))
    parts = (total, *arrived)
    return call(final_kernel, f32(size, moments, 2, columns // (2 * moments)), inputs=len(parts))(*parts)


def solution(mesh):
    placed = (
        P("grp", None, "site", None, None),
        P("grp", None, None, None, "site", None),
        P(),
        P(),
    )
    return jax.shard_map(
        on_device,
        mesh=mesh,
        in_specs=placed,
        out_specs=P("site", "grp", None, None),
        check_vma=False,
    )
```

```python
import functools
import math

import jax
import jax.numpy as jnp
import numpy as np
from jax import lax
from jax.experimental import pallas as pl
from jax.experimental.pallas import tpu as pltpu
from jax.sharding import PartitionSpec as P


TLX = 12
TLY = 12
LZ = 2
KAPPA = 0.08

LAYER = LZ * TLY
SITES = TLX * LAYER
XROWS = 3 * LAYER
MAIN = TLX * XROWS
BOTH = 2 * XROWS
PADDED = (TLX + 2) * BOTH
WINDOW = 3 * BOTH
EDGE = 4 * XROWS
HEAD = MAIN // 128 * 128
TAIL = MAIN - HEAD + EDGE
LANES = 128
CX, CY, CZ = 0, 18, 36
CYF, CYB, CZS, CZD = 54, 72, 90, 108
VMEM_LIMIT = 12 * 2**20


def call(kernel, outs, scratch=(), flops=0, moved=0, inputs=1, scalars=0, off_chip=0, **kwargs):
    on_chip = pl.BlockSpec(memory_space=pltpu.VMEM)
    first = [pl.BlockSpec(memory_space=pltpu.SMEM)] * scalars + [pl.BlockSpec(memory_space=pltpu.HBM)] * off_chip
    return pl.pallas_call(
        kernel,
        out_shape=outs,
        in_specs=first + [on_chip] * inputs,
        out_specs=jax.tree.map(lambda _: on_chip, outs),
        scratch_shapes=list(scratch),
        compiler_params=pltpu.CompilerParams(vmem_limit_bytes=VMEM_LIMIT),
        cost_estimate=pl.CostEstimate(flops=flops, bytes_accessed=moved, transcendentals=0),
        **kwargs,
    )


def f32(*shape):
    return jax.ShapeDtypeStruct(shape, jnp.float32)


def bf16(*shape):
    return jax.ShapeDtypeStruct(shape, jnp.bfloat16)


def spread(table, column, lanes=LANES):
    return jnp.broadcast_to(table[:, column : column + 1], (table.shape[0], lanes))


def matvec(table, first, field, adjoint=False, acc=None, minus=False):
    out = [[None] * 3, [None] * 3] if acc is None else [list(acc[0]), list(acc[1])]
    lanes = field[0][0].shape[-1]

    def put(part, row, value, negative):
        if negative != minus:
            out[part][row] = -value if out[part][row] is None else out[part][row] - value
        else:
            out[part][row] = value if out[part][row] is None else out[part][row] + value

    for row in range(3):
        for col in range(3):
            at = first + (3 * col + row if adjoint else 3 * row + col)
            real = spread(table, at, lanes)
            imag = spread(table, at + 9, lanes)
            put(0, row, real * field[0][col], False)
            put(0, row, imag * field[1][col], not adjoint)
            put(1, row, real * field[1][col], False)
            put(1, row, imag * field[0][col], adjoint)
    return out


def layer_rows(ref, part, half, first, size=LAYER):
    at = part * XROWS + first
    return ref[half, at : at + size, :]


def grid2(load):
    return [[load(part, colour) for colour in range(3)] for part in range(2)]


def y_rows(part, colour, z, y):
    return pl.ds(BOTH + part * XROWS + colour * LAYER + z * TLY + y, TLX, stride=BOTH)


def parity(tiles):
    position = lax.axis_index("site")
    return position // tiles % 2 == 0, position % 2 == 0


def send_layers(f_ref, wc_ref, ax_ref, bx_ref, ay_ref, by_ref, tiles):
    last = TLX * BOTH
    even_x, even_y = parity(tiles)
    for half in range(f_ref.shape[0]):
        table = wc_ref[TLX * LAYER : (TLX + 1) * LAYER, :]
        hop = matvec(table, CX, grid2(lambda p, c: layer_rows(f_ref, p, half, last + c * LAYER)), adjoint=True)
        for part in range(2):
            for colour in range(3):
                to = part * XROWS + colour * LAYER
                low, high = f_ref[half, BOTH + to : BOTH + to + LAYER, :], hop[part][colour]
                ax_ref[half, to : to + LAYER, :] = jnp.where(even_x, high, low)
                bx_ref[half, to : to + LAYER, :] = jnp.where(even_x, low, high)
        for z in range(LZ):
            table = wc_ref[pl.ds(LAYER + z * TLY + TLY - 1, TLX, stride=LAYER), :]
            hop = matvec(table, CY, grid2(lambda p, c: f_ref[half, y_rows(p, c, z, TLY - 1), :]), adjoint=True)
            for part in range(2):
                for colour in range(3):
                    to = part * XROWS + colour * LAYER + z * TLX
                    low, high = f_ref[half, y_rows(part, colour, z, 0), :], hop[part][colour]
                    ay_ref[half, to : to + TLX, :] = jnp.where(even_y, high, low)
                    by_ref[half, to : to + TLX, :] = jnp.where(even_y, low, high)


def clear_ends(ref):
    for half in range(ref.shape[0]):
        ref[half, 0:BOTH, :] = jnp.zeros((BOTH, LANES), jnp.float32)
        ref[half, PADDED - BOTH : PADDED, :] = jnp.zeros((BOTH, LANES), jnp.float32)


def pack_kernel(v_ref, l_ref, fr_ref, wc_ref, ax_ref, bx_ref, ay_ref, by_ref, la, lb, ta, tb, *, tiles):
    la[...] = jnp.zeros_like(la)
    lb[...] = jnp.zeros_like(lb)
    plane = SITES // LZ
    la[0:54, 0:SITES] = l_ref[...]
    la[CYF : CYF + 18, 0:SITES] = l_ref[CY : CY + 18, :]
    la[CYB : CYB + 18, 0:SITES] = l_ref[CY : CY + 18, :]
    la[CZS : CZS + 18, 0:SITES] = l_ref[CZ : CZ + 18, :]
    la[CZD : CZD + 18, 0:SITES] = l_ref[CZ : CZ + 18, :]
    for part in range(2):
        for row in range(3):
            for col in range(3):
                k = 9 * part + 3 * row + col
                kt = CZ + 9 * part + 3 * col + row
                value = l_ref[kt : kt + 1, :]
                sign = 1.0 if part == 0 else -1.0
                lb[CZS + k : CZS + k + 1, 0:SITES] = sign * value
                lb[CZD + k : CZD + k + 1, 0:SITES] = -sign * value
    ta[...] = jnp.transpose(la[...])
    tb[...] = jnp.transpose(lb[...])
    raw = ta[0:SITES, :]
    other = jnp.concatenate([tb[plane:SITES, :], tb[0:plane, :]], axis=0)
    y = lax.broadcasted_iota(jnp.int32, (SITES, LANES), 0) % TLY
    column = lax.broadcasted_iota(jnp.int32, (SITES, LANES), 1)
    back = pltpu.roll(raw, 1, 0)
    is_yf = (column >= CYF) & (column < CYB)
    is_yb = (column >= CYB) & (column < CZS)
    table = jnp.where(is_yb, back, raw)
    gone = (is_yf & (y == TLY - 1)) | (is_yb & (y == 0))
    ta[0:SITES, :] = jnp.where(gone, 0.0, table) + other
    wc_ref[0:LAYER, :] = jnp.zeros((LAYER, LANES), jnp.float32)
    clear_ends(fr_ref)
    for x in range(TLX):
        for z in range(LZ):
            src = z * plane + x * TLY
            dst = (x + 1) * LAYER + z * TLY
            wc_ref[dst : dst + TLY, :] = ta[src : src + TLY, :]
            for half in range(fr_ref.shape[0]):
                for part in range(2):
                    for colour in range(3):
                        dst = (x + 1) * BOTH + part * XROWS + colour * LAYER + z * TLY
                        fr_ref[half, dst : dst + TLY, :] = v_ref[
                            3 * part + colour, src : src + TLY, half * LANES : (half + 1) * LANES
                        ]
    send_layers(fr_ref, wc_ref, ax_ref, bx_ref, ay_ref, by_ref, tiles)


def split(value):
    high = value.astype(jnp.bfloat16)
    return high, (value - high.astype(jnp.float32)).astype(jnp.bfloat16)


def sources(kinds):
    column = np.full((6, len(kinds) * BOTH), -1, np.int32)
    sign = np.zeros((6, len(kinds) * BOTH), np.float32)
    for k, kind in enumerate(kinds):
        if kind is None:
            continue
        first, adjoint, factor, below = kind
        for ri in range(2):
            for row in range(3):
                for rj in range(2):
                    for col in range(3):
                        at = first + (3 * col + row if adjoint else 3 * row + col)
                        weight = 1.0
                        if ri != rj:
                            at += 9
                            weight = -1.0 if (ri == 0) != adjoint else 1.0
                        lanes = slice(k * BOTH + rj * XROWS + col * LAYER, k * BOTH + rj * XROWS + (col + 1) * LAYER)
                        column[3 * ri + row, lanes] = at + (2 * LANES if below else 0)
                        sign[3 * ri + row, lanes] = factor * weight
    return column, sign


def expand(terms, column_ref, sign_ref, block, first, width):
    deep = terms.shape[1] // (2 * LANES)
    row = lax.broadcasted_iota(jnp.int32, (LANES, width), 0)
    column = jnp.broadcast_to(column_ref[block : block + 1, first : first + width], (LANES, width))
    sign = jnp.broadcast_to(sign_ref[block : block + 1, first : first + width], (LANES, width))
    ones = []
    for k in range(deep):
        ones += [jnp.where(row + 2 * k * LANES == column, sign, 0.0).astype(jnp.bfloat16)] * 2
    return dot(terms, jnp.concatenate(ones, axis=0))


def operator_kernel(wc_ref, column_ref, sign_ref, more_ref, moresign_ref, high_ref, low_ref, *, middle, kinds, extra):
    high, low = split(wc_ref[...])
    own, below = slice(LAYER, (TLX + 1) * LAYER), slice(0, TLX * LAYER)
    deep = jnp.concatenate([high[own], low[own], high[below], low[below]], axis=1)
    single = jnp.concatenate([high[own], low[own]], axis=1)
    width = -(-len(kinds) * BOTH // LANES) * LANES
    wide = 2 * LANES

    def mask(first, size, shifts):
        p = lax.broadcasted_iota(jnp.int32, (LAYER, size), 0)
        lane = lax.broadcasted_iota(jnp.int32, (LAYER, size), 1) + first
        q = lane % LAYER
        block = lane // BOTH
        found = None
        for k, shift in enumerate(shifts):
            if shift is not None:
                here = (block == k) & (q == (p + shift if shift != TLY else (p + TLY) % LAYER))
                found = here if found is None else found | here
        return found

    keep = mask(0, width, kinds)
    keeps = [mask(middle, wide, [shift if k == place else None for k in range(len(kinds))]) for place, shift in extra]
    for block in range(6):
        value = expand(deep, column_ref, sign_ref, block, 0, width).reshape(TLX, LAYER, width)
        value = jnp.where(keep[None], value, 0.0)
        center = value[:, :, middle : middle + wide]
        for k in range(len(extra)):
            other = expand(single, more_ref, moresign_ref, block, k * wide, wide).reshape(TLX, LAYER, wide)
            center = center + jnp.where(keeps[k][None], other, 0.0)
        pieces = [value[:, :, :middle], center]
        if middle + wide < width:
            pieces.append(value[:, :, middle + wide :])
        at = 0
        for piece in pieces:
            size = min(piece.shape[2], len(kinds) * BOTH - at)
            if size > 0:
                high, low = split(piece)
                for x in range(TLX):
                    rows = slice(x * BOTH + block * LAYER, x * BOTH + (block + 1) * LAYER)
                    high_ref[rows, at : at + size] = high[x, :, :size]
                    low_ref[rows, at : at + size] = low[x, :, :size]
            at += piece.shape[2]


def split_field(f_ref, high_ref, low_ref, scale=None):
    for half in range(f_ref.shape[0]):
        lanes = slice(half * LANES, (half + 1) * LANES)
        for row in range(0, PADDED, BOTH):
            value = f_ref[half, row : row + BOTH, :]
            high, low = split(value if scale is None else scale * value)
            high_ref[row : row + BOTH, lanes] = high
            low_ref[row : row + BOTH, lanes] = low


def smear_kernel(f_ref, oh_ref, ol_ref, out_ref, fh, fl):
    clear_ends(out_ref)
    split_field(f_ref, fh, fl)
    for x in range(TLX):
        rows = slice(x * BOTH, (x + 1) * BOTH)
        high, low = oh_ref[rows, :], ol_ref[rows, :]
        window = slice(x * BOTH, x * BOTH + WINDOW)
        hops = dot(high, fh[window, :]) + dot(high, fl[window, :]) + dot(low, fh[window, :])
        at = slice((x + 1) * BOTH, (x + 2) * BOTH)
        for half in range(f_ref.shape[0]):
            lanes = slice(half * LANES, (half + 1) * LANES)
            out_ref[half, at, :] = (1.0 - 6.0 * KAPPA) * f_ref[half, at, :] + KAPPA * hops[:, lanes]


def cross(once_ref, wc_ref, received, tiles, save=None):
    last = TLX * BOTH
    even_x, even_y = parity(tiles)
    ax, bx, ay, by = received

    def arrived(above, half, part, first, size, along_y):
        one, two, even = (ay, by, even_y) if along_y else (ax, bx, even_x)
        values = (layer_rows(ref, part, half, first, size) for ref in ((one, two) if above else (two, one)))
        return jnp.where(even, *values)

    for half in range(once_ref.shape[0]):
        table = wc_ref[TLX * LAYER : (TLX + 1) * LAYER, :]
        hop_x = matvec(table, CX, grid2(lambda p, c: arrived(True, half, p, c * LAYER, LAYER, False)))
        hop_y = []
        for z in range(LZ):
            table = wc_ref[pl.ds(LAYER + z * TLY + TLY - 1, TLX, stride=LAYER), :]
            hop_y.append(
                matvec(table, CY, grid2(lambda p, c: arrived(True, half, p, c * LAYER + z * TLX, TLX, True)))
            )
        for part in range(2):
            for colour in range(3):
                at = colour * LAYER
                low = arrived(False, half, part, at, LAYER, False)
                to = part * XROWS + at
                once_ref[half, BOTH + to : BOTH + to + LAYER, :] += KAPPA * low
                once_ref[half, last + to : last + to + LAYER, :] += KAPPA * hop_x[part][colour]
                if save is not None:
                    save[part, half, at : at + LAYER, :] = low
                    save[part, half, XROWS + at : XROWS + at + LAYER, :] = hop_x[part][colour]
                for z in range(LZ):
                    low = arrived(False, half, part, at + z * TLX, TLX, True)
                    rows = y_rows(part, colour, z, 0)
                    once_ref[half, rows, :] = once_ref[half, rows, :] + KAPPA * low
                    rows = y_rows(part, colour, z, TLY - 1)
                    once_ref[half, rows, :] = once_ref[half, rows, :] + KAPPA * hop_y[z][part][colour]
                    if save is not None:
                        to = 2 * XROWS + at + z * TLX
                        save[part, half, to : to + TLX, :] = low
                        save[part, half, to + XROWS : to + XROWS + TLX, :] = hop_y[z][part][colour]


def edge_kernel(part_ref, wc_ref, rax, rbx, ray, rby, *refs, tiles):
    once_ref, save, ax_ref, bx_ref, ay_ref, by_ref = refs[-6:]
    cross(once_ref, wc_ref, (rax, rbx, ray, rby), tiles, save)
    send_layers(once_ref, wc_ref, ax_ref, bx_ref, ay_ref, by_ref, tiles)


def phased(real, imag, half, lane, at, size, cos_ref, sin_ref, ah_ref, al_ref):
    real, imag = jnp.transpose(real), jnp.transpose(imag)
    halves = ah_ref.shape[0] // cos_ref.shape[0] // LANES
    for m in range(cos_ref.shape[0]):
        cosine = jnp.broadcast_to(cos_ref[m : m + 1, lane : lane + LANES], (LANES, LANES))
        sine = jnp.broadcast_to(sin_ref[m : m + 1, lane : lane + LANES], (LANES, LANES))
        row = (m * halves + half) * LANES
        high, low = split(cosine * real - sine * imag)
        ah_ref[row : row + LANES, at : at + LANES] = high
        al_ref[row : row + LANES, at : at + LANES] = low
        high, low = split(sine * real + cosine * imag)
        ah_ref[row : row + LANES, size + at : size + at + LANES] = high
        al_ref[row : row + LANES, size + at : size + at + LANES] = low


def own_rows(fr_ref, rows, half, first, stop):
    for part in range(2):
        for x in range(first // XROWS, -(-stop // XROWS)):
            low, high = max(first, x * XROWS), min(stop, (x + 1) * XROWS)
            at = (x + 1) * BOTH + part * XROWS + low - x * XROWS
            rows[part, low - first : high - first, :] = fr_ref[half, at : at + high - low, :]


def head_kernel(fr_ref, cos_ref, sin_ref, ah_ref, al_ref, rows):
    for half in range(fr_ref.shape[0]):
        own_rows(fr_ref, rows, half, 0, HEAD)
        for at in range(0, HEAD, LANES):
            real, imag = (rows[p, at : at + LANES, :] for p in range(2))
            phased(real, imag, half, at, at, HEAD, cos_ref, sin_ref, ah_ref, al_ref)


def tail_kernel(fr_ref, save, cos_ref, sin_ref, ah_ref, al_ref, rows):
    for half in range(fr_ref.shape[0]):
        own_rows(fr_ref, rows, half, HEAD, MAIN)
        for part in range(2):
            rows[part, MAIN - HEAD : TAIL, :] = save[part, half]
        for at in range(0, TAIL, LANES):
            real, imag = (rows[p, at : at + LANES, :] for p in range(2))
            phased(real, imag, half, HEAD + at, at, TAIL, cos_ref, sin_ref, ah_ref, al_ref)


def displace_kernel(
    part_ref, wc_ref, oh_ref, ol_ref, rax, rbx, ray, rby, dir_ref, *refs, scale, tiles
):
    sh_ref, sl_ref, th_ref, tl_ref, twice, shift, fh, fl = refs[-8:]
    twice[...] = part_ref[...]
    cross(twice, wc_ref, (rax, rbx, ray, rby), tiles)
    halves = range(twice.shape[0])
    width = len(halves) * LANES

    def along(which, lanes, rows):
        return jnp.broadcast_to(dir_ref[0:1, lanes], (rows, lanes.stop - lanes.start)) == which

    for half in halves:
        lanes = slice(half * LANES, (half + 1) * LANES)
        masks = [jnp.where(along(which, lanes, BOTH), 1.0, 0.0).astype(jnp.bfloat16) for which in range(3)]
        for row in range(0, PADDED, BOTH):
            high, low = split(scale * twice[half, row : row + BOTH, :])
            for which in range(3):
                fh[which, row : row + BOTH, lanes] = high * masks[which]
                fl[which, row : row + BOTH, lanes] = low * masks[which]
    for x in range(TLX):
        rows = slice(x * BOTH, (x + 1) * BOTH)
        low, mid, top = (slice((x + k) * BOTH, (x + k + 1) * BOTH) for k in range(3))

        def columns(ref):
            return jnp.concatenate([ref[0, low, :], ref[0, top, :], ref[1, mid, :], ref[2, mid, :]], axis=0)

        fields, rest = columns(fh), columns(fl)
        weights = oh_ref[rows, :]
        value = dot(weights, fields) + dot(weights, rest) + dot(ol_ref[rows, :], fields)
        for part in range(2):
            shift[part, x * XROWS : (x + 1) * XROWS, :] = value[part * XROWS : (part + 1) * XROWS]
    last = TLX * BOTH
    for half in halves:
        lanes = slice(half * LANES, (half + 1) * LANES)
        mask_x = jnp.where(along(0, lanes, XROWS), scale, 0.0)
        mask_y = jnp.where(along(1, lanes, TLX), scale, 0.0)
        for part in range(2):
            at = part * XROWS
            shift[part, MAIN : MAIN + XROWS, lanes] = mask_x * twice[half, BOTH + at : BOTH + at + XROWS, :]
            shift[part, MAIN + XROWS : MAIN + 2 * XROWS, lanes] = -mask_x * twice[half, last + at : last + at + XROWS, :]
            for colour in range(3):
                for z in range(LZ):
                    to = MAIN + 2 * XROWS + colour * LAYER + z * TLX
                    shift[part, to : to + TLX, lanes] = mask_y * twice[half, y_rows(part, colour, z, 0), :]
                    to += XROWS
                    shift[part, to : to + TLX, lanes] = -mask_y * twice[half, y_rows(part, colour, z, TLY - 1), :]
    for high_ref, low_ref, first, size in ((sh_ref, sl_ref, 0, HEAD), (th_ref, tl_ref, HEAD, TAIL)):
        real, imag = slice(0, width), slice(width, 2 * width)
        for row in range(0, size, 128):
            top = slice(row, row + 128)
            bottom = slice(size + row, size + row + 128)
            high, low = split(shift[0, first + row : first + row + 128, :])
            high_ref[top, real] = high
            low_ref[top, real] = low
            high_ref[bottom, imag] = -high
            low_ref[bottom, imag] = -low
            high, low = split(shift[1, first + row : first + row + 128, :])
            high_ref[bottom, real] = high
            low_ref[bottom, real] = low
            high_ref[top, imag] = high
            low_ref[top, imag] = low


def dot(a, b):
    return jnp.dot(a, b, preferred_element_type=jnp.float32)


def meson_kernel(ah, al, bh, bl, sh, sl, th, tl, out_ref):
    total = dot(ah[...], sh[...]) + dot(ah[...], sl[...]) + dot(al[...], sh[...])
    out_ref[...] = total + dot(bh[...], th[...]) + dot(bh[...], tl[...]) + dot(bl[...], th[...])


def product(blocks, moments, refs):
    ah, al, bh, bl, sh, sl, th, tl = refs
    nev = ah.shape[0] // moments
    size = blocks[1]

    def rows(ref):
        picked = [ref[pl.ds(pl.multiple_of(m * nev + b, size), size), :] for m in range(moments) for b in blocks[0]]
        return jnp.concatenate(picked, axis=0)

    ahv, alv, bhv, blv = rows(ah), rows(al), rows(bh), rows(bl)
    total = dot(ahv, sh[...]) + dot(ahv, sl[...]) + dot(alv, sh[...])
    return total + dot(bhv, th[...]) + dot(bhv, tl[...]) + dot(blv, th[...])


def put(out_ref, value, count, moments, added=None):
    size, width = out_ref.shape[1], value.shape[-1]
    for m in range(moments):
        for k in range(count):
            block = value[(m * count + k) * size : (m * count + k + 1) * size]
            lanes = slice(m * width, (m + 1) * width)
            if added is not None:
                block = block + added(k, lanes)
            out_ref[k, :, lanes] = block


def owners(groups, size, cores, turn, steps):
    position = lax.axis_index("site")
    core, y, z = position % 2, position // 2 % 2, position // 4
    return [((z + g) % groups * 4 + (y + turn) % 2 * 2 + (core + cores) % 2) * size for g in steps]


def piece_kernel(*refs, moments, groups, cores, turn, steps):
    out_ref = refs[-1]
    size = out_ref.shape[1]
    blocks = owners(groups, size, cores, turn, steps)
    put(out_ref, product((blocks, size), moments, refs[:8]), len(blocks), moments)


def merge_kernel(*refs, sources, picks):
    for out_ref, blocks in zip(refs[sources:], picks):
        for k, places in enumerate(blocks):
            total = refs[0][places[0]]
            for ref, at in zip(refs[1:sources], places[1:]):
                total = total + ref[at]
            out_ref[k] = total


def final_kernel(*refs):
    out_ref = refs[-1]
    width = out_ref.shape[3]
    for m in range(out_ref.shape[1]):
        for part in range(2):
            lanes = slice((2 * m + part) * width, (2 * m + part + 1) * width)
            total = refs[0][0, :, lanes]
            for ref in refs[1:-1]:
                total = total + ref[0, :, lanes]
            out_ref[:, m, part, :] = total


def phases(momenta, position, devices, tiles):
    site = np.arange(SITES)
    x, zy = site // LAYER, site % LAYER
    own = [np.repeat(a.reshape(TLX, 1, LAYER), 3, 1).reshape(-1) for a in (x, zy % TLY, zy // TLY)]
    edge = np.arange(LAYER)
    full = np.full(LAYER, 0)
    edges = (
        (full + TLX - 1, edge % TLY, edge // TLY),
        (full, edge % TLY, edge // TLY),
        (edge % TLX, full + TLY - 1, edge // TLX),
        (edge % TLX, full, edge // TLX),
    )
    steps = (-tiles, tiles, -1, 1)
    xs, ys, zs, move = own[0], own[1], own[2], np.zeros(MAIN, np.int64)
    for step, (ex, ey, ez) in zip(steps, edges):
        xs = np.concatenate([xs] + [ex] * 3)
        ys = np.concatenate([ys] + [ey] * 3)
        zs = np.concatenate([zs] + [ez] * 3)
        move = np.concatenate([move, np.full(XROWS, step)])
    tile = (position + jnp.asarray(move, jnp.int32) + devices) % devices
    lx, ly = TLX * tiles, TLY * tiles
    sx = (tile // tiles) * TLX + jnp.asarray(xs, jnp.int32)
    sy = (tile % tiles) * TLY + jnp.asarray(ys, jnp.int32)
    sz = jnp.asarray(zs, jnp.int32)
    frac = (momenta[:, 0:1] * sx % lx).astype(jnp.float32) / lx
    frac = frac + (momenta[:, 1:2] * sy % ly).astype(jnp.float32) / ly
    frac = frac + (momenta[:, 2:3] * sz % LZ).astype(jnp.float32) / LZ
    theta = 2.0 * math.pi * frac
    return jnp.cos(theta), jnp.sin(theta)


def halo(sends, devices, tiles):
    found = []
    for block, stride, turn in zip(sends, (tiles, tiles, 1, 1), (1, -1, 1, -1)):
        route = [(i, (i + (turn if i // stride % 2 == 0 else -turn) * stride) % devices) for i in range(devices)]
        found.append(lax.ppermute(block, "site", route))
    return found


def stages(devices):
    found, stride = [], 1
    while stride < devices:
        left = devices // stride
        size = 2 if stride < 4 else 4 if left % 4 == 0 else 2
        found.append((stride, size))
        stride *= size
    return found


def scatter_sum(block, position, devices):
    shape = block.shape[1:]
    for stride, size in stages(devices):
        left = block.shape[0] // size
        block = block.reshape((left, size) + shape)
        mine = (position // stride) % size
        total = lax.dynamic_index_in_dim(block, mine, 1, keepdims=False)
        for step in range(1, size):
            other = (mine + step) % size
            out = lax.dynamic_index_in_dim(block, other, 1, keepdims=False)
            route = []
            for i in range(devices):
                digit = (i // stride) % size
                route.append((i, i + ((digit + step) % size - digit) * stride))
            total = total + lax.ppermute(out, "site", route)
        block = total
    return block[0]


def on_device(vectors, links, momenta, directions):
    devices = lax.axis_size("site")
    tiles = math.isqrt(devices)
    position = lax.axis_index("site")
    nev = vectors.shape[-1]
    moments = momenta.shape[0]
    field = vectors.reshape(6, SITES, nev)
    table = links.reshape(54, SITES)
    halves = nev // LANES
    layer = f32(halves, BOTH, LANES)
    padded = f32(halves, PADDED, LANES)
    fr, wc, *sends = call(
        functools.partial(pack_kernel, tiles=tiles),
        (padded, f32((TLX + 1) * LAYER, LANES), layer, layer, layer, layer),
        [pltpu.VMEM((128, 384), jnp.float32)] * 2 + [pltpu.VMEM((384, 128), jnp.float32)] * 2,
        inputs=2,
    )(field, table)
    received = halo(sends, devices, tiles)
    flops = 2 * 180 * 2 * SITES * nev
    smear = operator(
        wc,
        kinds=((CX, True, 1.0, True), (CYF, False, 1.0, False), (CX, False, 1.0, False)),
        shifts=(0, 1, 0),
        extra=((1, CYB, True, 1.0, -1), (1, CZS, False, 1.0, TLY)),
        middle=LANES,
    )
    pair = [pltpu.VMEM((PADDED, nev), jnp.bfloat16)] * 2
    once = call(smear_kernel, padded, pair, flops, 3 << 20, 3)(fr, *smear)
    cosine, sine = phases(momenta, position, devices, tiles)
    head = bf16(moments * nev, 2 * HEAD)
    tail = bf16(moments * nev, 2 * TAIL)
    rows = pltpu.VMEM((2, HEAD, LANES), jnp.float32)
    ah, al = call(head_kernel, (head, head), [rows], flops, 8 << 20, 3)(fr, cosine, sine)
    displace = operator(
        wc,
        kinds=((CX, True, -1.0, True), (CX, False, 1.0, False), (CYF, False, 1.0, False), (CZD, False, 1.0, False)),
        shifts=(0, 0, 1, TLY),
        extra=((2, CYB, True, -1.0, -1),),
        middle=2 * LANES,
    )
    edges = f32(2, halves, EDGE, LANES)
    once, save, *sends = call(
        functools.partial(edge_kernel, tiles=tiles), (padded, edges, layer, layer, layer, layer), inputs=7,
        input_output_aliases={0: 0},
    )(once, wc, *received, ah)
    received = halo(sends, devices, tiles)
    twice = call(smear_kernel, padded, pair, flops, 3 << 20, 3)(once, *smear)
    rows = pltpu.VMEM((2, TAIL, LANES), jnp.float32)
    bh, bl = call(tail_kernel, (tail, tail), [rows], flops, 4 << 20, 4)(fr, save, cosine, sine)
    scale = 1.0 / math.sqrt(3.0 * TLX * tiles * TLY * tiles * LZ)
    operands = call(
        functools.partial(displace_kernel, scale=scale, tiles=tiles),
        (bf16(2 * HEAD, 2 * nev), bf16(2 * HEAD, 2 * nev), bf16(2 * TAIL, 2 * nev), bf16(2 * TAIL, 2 * nev)),
        [
            pltpu.VMEM((halves, PADDED, LANES), jnp.float32),
            pltpu.VMEM((2, HEAD + TAIL, nev), jnp.float32),
        ]
        + [pltpu.VMEM((3, PADDED, nev), jnp.bfloat16)] * 2,
        inputs=9,
    )(twice, wc, *displace, *received, directions[None, :])
    operands = (ah, al, bh, bl) + tuple(operands)
    size, columns = nev // devices, moments * 2 * nev
    if size % 16 == 0 and devices % 8 == 0:
        total = pieces(operands, devices, moments, size, columns)
    else:
        total = whole_product(operands, position, devices, moments, nev)
    return total.reshape(size, moments, 2, nev)


def operator(wc, kinds, shifts, extra, middle):
    lanes = len(kinds) * BOTH
    width = -(-lanes // LANES) * LANES
    column, sign = sources(kinds)
    column = np.pad(column, ((0, 0), (0, width - lanes)), constant_values=-1)
    sign = np.pad(sign, ((0, 0), (0, width - lanes)))
    more, moresign = [], []
    for place, first, adjoint, factor, _ in extra:
        c, w = sources([(first, adjoint, factor, False) if k == place else None for k in range(len(kinds))])
        c = np.pad(c, ((0, 0), (0, width - lanes)), constant_values=-1)
        w = np.pad(w, ((0, 0), (0, width - lanes)))
        more.append(c[:, middle : middle + 2 * LANES])
        moresign.append(w[:, middle : middle + 2 * LANES])
    kernel = functools.partial(
        operator_kernel, middle=middle, kinds=shifts, extra=[(place, shift) for place, _, _, _, shift in extra]
    )
    out = bf16(TLX * BOTH, lanes)
    tables = (column, sign, np.concatenate(more, 1), np.concatenate(moresign, 1))
    return call(kernel, (out, out), (), 1 << 30, 4 << 20, 5)(wc, *map(jnp.asarray, tables))


def whole_product(operands, position, devices, moments, nev):
    whole = lambda a: pl.BlockSpec(a.shape, lambda m: (0, 0))
    partial = pl.pallas_call(
        meson_kernel,
        out_shape=f32(nev, moments * 2 * nev),
        grid=(moments,),
        in_specs=[pl.BlockSpec((nev, a.shape[1]), lambda m: (m, 0)) for a in operands[:4]]
        + [whole(a) for a in operands[4:]],
        out_specs=pl.BlockSpec((nev, 2 * nev), lambda m: (0, m)),
        compiler_params=pltpu.CompilerParams(vmem_limit_bytes=40 * 2**20),
    )(*operands)
    return scatter_sum(partial.reshape(devices, nev // devices, moments * 2 * nev), position, devices)


def pieces(operands, devices, moments, size, columns):
    groups = devices // 4
    block = lambda count: f32(count, size, columns)
    swap = [(i, i ^ 1) for i in range(devices)]
    flip = [(i, i ^ 2) for i in range(devices)]

    def piece(cores, turn, steps, *after):
        kernel = functools.partial(
            piece_kernel, moments=moments, groups=groups, cores=cores, turn=turn, steps=tuple(steps)
        )
        flops = 2 * 3 * size * len(steps) * moments * 4 * (HEAD + TAIL) * 256
        return call(kernel, block(len(steps)), (), flops, 1 << 20, 8 + len(after))(*operands, *after)

    def permute(value, route):
        return lax.ppermute(value, "site", route)

    def merge(arrays, picks):
        kernel = functools.partial(merge_kernel, sources=len(arrays), picks=picks)
        outs = tuple(block(len(p)) for p in picks)
        return call(kernel, outs, inputs=len(arrays))(*arrays)

    order = [*range(1, groups), 0]
    early, late = order[: groups // 2], order[groups // 2 :]

    def along_z(value, step):
        return permute(value, [(i, (i + 4 * step) % devices) for i in range(devices)])

    def split_sum(mine, swapped):
        return merge((mine, swapped), [[(k, k)] for k in range(mine.shape[0])])

    a1 = piece(1, 1, early)
    got_a = permute(a1, swap)
    a2 = piece(0, 1, early, a1)
    out_a = split_sum(a2, got_a)
    crossed_a = [permute(out_a[0], flip)]
    c1 = piece(1, 0, early, out_a[0])
    got_c = permute(c1, swap)
    crossed_a += [permute(out_a[k], flip) for k in range(1, len(early))]
    c2 = piece(0, 0, early, c1)
    b1 = piece(1, 1, late, c2)
    got_b = permute(b1, swap)
    b2 = piece(0, 1, late, b1)
    sums = list(merge((c2, got_c, crossed_a[0]), [[(0, 0, 0)]]))
    arrived = [along_z(sums[0], early[0])]
    out_b = split_sum(b2, got_b)
    crossed_b = [permute(out, flip) for out in out_b]
    for k in range(1, len(early)):
        sums += merge((c2, got_c, crossed_a[k]), [[(k, k, 0)]])
        arrived.append(along_z(sums[-1], early[k]))
    d1 = piece(1, 0, late, out_b[0], sums[0])
    got_d = permute(d1, swap)
    d2 = piece(0, 0, late, d1)
    total = None
    for k, step in enumerate(late):
        sums += merge((d2, got_d, crossed_b[k]), [[(k, k, 0)]])
        if step == 0:
            total = sums[-1]
        else:
            arrived.append(along_z(sums[-1], step))
    parts = (total, *arrived)
    return call(final_kernel, f32(size, moments, 2, columns // (2 * moments)), inputs=len(parts))(*parts)


def solution(mesh):
    placed = (
        P("grp", None, "site", None, None),
        P("grp", None, None, None, "site", None),
        P(),
        P(),
    )
    return jax.shard_map(
        on_device,
        mesh=mesh,
        in_specs=placed,
        out_specs=P("site", "grp", None, None),
        check_vma=False,
    )
```
